32 devices in a mesh: section: 8 (over z, core), ctx: 4 (over y, x).
Axes of the slice: x: 2, y: 2, z: 4, core: 2. Of those that a mesh axis runs over, the one named last changes fastest.
Arguments:
- gate_q: bfloat16 [8, 512, 4096], P('section', 'ctx'), may hold values from -6 to 6
- gate_k: bfloat16 [8, 512, 4096], P('section', 'ctx'), may hold values from -6 to 6
- value_in: bfloat16 [8, 512, 4096], P('section', 'ctx'), may hold values from -6 to 6
- filter_raw: bfloat16 [8, 512, 4096], P('section', 'ctx'), may hold values from -0.5 to 0.5
- decay_rate: float32 [8, 4096], P('section'), may hold values from 0.25 to 16
- skip_gain: float32 [8, 4096], P('section'), may hold values from -4 to 4
- grad_out: bfloat16 [8, 512, 4096], P('section', 'ctx'), may hold values from -6 to 6
Outputs:
- grad_q: bfloat16 [8, 512, 4096], P('section', 'ctx')
- grad_k: bfloat16 [8, 512, 4096], P('section', 'ctx')
- grad_passed: bfloat16 [8, 512, 4096], P('section', 'ctx')
- filter_grad: bfloat16 [8, 512, 4096], P('section', 'ctx')
- rate_grad: float32 [8, 4096], P('section')
- skip_grad: float32 [8, 4096], P('section')
The draws below stay inside these ranges and needn't reach their ends.
All inputs are finite; a program needn't handle non-finite values.
Results may differ from the reference program's by a relative error of at most 0.013.
Values may be sent and summed in bfloat16 or wider, within the bound.
A program may use at most 128 MiB of HBM per device.

```python
import math
import jax
import jax.numpy as jnp
from jax import lax

CH = 4096
TOK_DEV = 128
NS = 8
BLOCKS = 4
FACTOR = 8
SEQ = 512
FFT = 1024


def shard_levels(own_key, shape, shards, least, high):
    loudness, own = 1.0, jax.random.fold_in(own_key, 6)
    for position, parts in shards:
        heights = jnp.exp(jax.random.uniform(jax.random.fold_in(own, position), (parts,), jnp.float32, least / len(shards), high / len(shards)))
        loudness = loudness * jnp.repeat(heights, shape[position] // parts).reshape([-1 if axis == position else 1 for axis in range(len(shape))])
    return loudness


def noise(key, dims, spread, most, pieces=(), held_as=jnp.bfloat16):
    gain = shard_levels(key, dims, pieces, -0.22, 0.18) if pieces else 1.0
    drawn = jax.random.normal(key, dims, jnp.float32) * spread * gain
    return jnp.minimum(jnp.maximum(drawn, -most), most).astype(held_as)


def setup_inputs(seed: int = 0) -> dict:
    splits = jax.random.split(jax.random.key(seed), 8)
    gate_q = noise(splits[0], (NS, SEQ, CH), 1.0, 6.0, ((0, 8), (1, 4)))
    gate_k = noise(splits[1], (NS, SEQ, CH), 1.0, 6.0, ((0, 8), (1, 4)))
    value_in = noise(splits[2], (NS, SEQ, CH), 1.0, 6.0, ((0, 8), (1, 4)))
    filter_raw = noise(splits[3], (NS, SEQ, CH), (SEQ // 4) ** -0.5, 0.5, ((0, 8), (1, 4)))
    decay_rate = jnp.clip(jnp.exp(math.log(16.0) - 4.158883 * jax.random.uniform(splits[4], (NS, CH), jnp.float32) ** shard_levels(splits[4], (NS, CH), ((0, 8),), -0.2, 0.2)), 0.25, 16.0)
    skip_gain = noise(splits[5], (NS, CH), 1.0, 4.0, ((0, 8),), jnp.float32)
    grad_out = noise(splits[6], (NS, SEQ, CH), 1.0, 6.0, ((0, 8), (1, 4)))
    return dict(gate_q=gate_q, gate_k=gate_k, value_in=value_in, filter_raw=filter_raw, decay_rate=decay_rate, skip_gain=skip_gain, grad_out=grad_out)


def round_trip(values):
    return lax.optimization_barrier(values.astype(jnp.bfloat16)).astype(jnp.float32)


def twist_angle():
    bins = jnp.arange(FACTOR, dtype=jnp.int32)[:, None]
    rows = jnp.arange(TOK_DEV, dtype=jnp.int32)[None, :]
    product = (bins * rows) % FFT
    angle = product.astype(jnp.float32) * (2.0 * math.pi / FFT)
    return jnp.cos(angle)[:, :, None], jnp.sin(angle)[:, :, None]


def forward_spectrum(signal):
    blocks = signal.astype(jnp.float32).reshape(BLOCKS, TOK_DEV, CH)
    padded = jnp.concatenate([blocks, jnp.zeros_like(blocks)], axis=0)
    partial_value = jnp.fft.fft(padded, axis=0)
    part_real = round_trip(jnp.real(partial_value))
    part_imag = round_trip(jnp.imag(partial_value))
    twist_cos, twist_sin = twist_angle()
    turned = lax.complex(part_real * twist_cos + part_imag * twist_sin,
                         part_imag * twist_cos - part_real * twist_sin)
    return jnp.fft.fft(turned, axis=1)


def inverse_spectrum(spectrum):
    back = jnp.fft.ifft(spectrum, axis=1) * TOK_DEV
    back_real = jnp.real(back)
    back_imag = jnp.imag(back)
    twist_cos, twist_sin = twist_angle()
    fold_real = round_trip(back_real * twist_cos - back_imag * twist_sin)
    fold_imag = round_trip(back_real * twist_sin + back_imag * twist_cos)
    summed = jnp.fft.ifft(lax.complex(fold_real, fold_imag), axis=0) * FACTOR
    values = jnp.real(summed)[:BLOCKS] / FFT
    return values.reshape(SEQ, CH).astype(jnp.bfloat16)


def one_section(inputs):
    gate_q, gate_k, value_in, filter_raw, decay_rate, skip_gain, grad_out = inputs
    positions = (jnp.arange(SEQ, dtype=jnp.int32).astype(jnp.float32) / SEQ)[:, None]
    envelope = jnp.exp(-decay_rate[None, :] * positions)
    modulated = filter_raw.astype(jnp.float32) * envelope
    filter_bf = modulated.astype(jnp.bfloat16)
    mixed_in = (gate_k.astype(jnp.float32) * value_in.astype(jnp.float32)).astype(jnp.bfloat16)
    pulled = (gate_q.astype(jnp.float32) * grad_out.astype(jnp.float32)).astype(jnp.bfloat16)
    spec_mixed = forward_spectrum(mixed_in)
    spec_filter = forward_spectrum(filter_bf)
    spec_pulled = forward_spectrum(pulled)
    conv_out = inverse_spectrum(spec_filter * spec_mixed).astype(jnp.float32)
    adjoint = inverse_spectrum(jnp.conj(spec_filter) * spec_pulled).astype(jnp.float32)
    filter_corr = inverse_spectrum(jnp.conj(spec_mixed) * spec_pulled).astype(jnp.float32)
    skip_row = skip_gain[None, :]
    mixed_f = mixed_in.astype(jnp.float32)
    pulled_f = pulled.astype(jnp.float32)
    grad_q = (grad_out.astype(jnp.float32) * (conv_out + skip_row * mixed_f)).astype(jnp.bfloat16)
    mixed_grad = adjoint + skip_row * pulled_f
    grad_k = (mixed_grad * value_in.astype(jnp.float32)).astype(jnp.bfloat16)
    passing = (mixed_grad * gate_k.astype(jnp.float32)).astype(jnp.bfloat16)
    filter_grad = (filter_corr * envelope).astype(jnp.bfloat16)
    rate_grad = -jnp.sum(positions * filter_corr * modulated, axis=0)
    skip_grad = jnp.sum(mixed_f * pulled_f, axis=0)
    return grad_q, grad_k, passing, filter_grad, rate_grad, skip_grad


def reference(gate_q, gate_k, value_in, filter_raw, decay_rate, skip_gain, grad_out):
    grad_q, grad_k, passing, filter_grad, rate_grad, skip_grad = lax.map(
        one_section, (gate_q, gate_k, value_in, filter_raw, decay_rate, skip_gain, grad_out))
    grad_passed = jnp.concatenate([passing[1:], jnp.zeros_like(passing[:1])], axis=0)
    return grad_q, grad_k, grad_passed, filter_grad, rate_grad, skip_grad
```

```python
import functools
import math

import jax
import jax.numpy as jnp
import numpy as np
from jax import lax
from jax.experimental import pallas as pl
from jax.experimental.pallas import tpu as pltpu
from jax.sharding import PartitionSpec as P

MESH = pl.DeviceIdType.MESH
F32 = jnp.float32
BF16 = jnp.bfloat16


def make_tables(n, rows):
    length = 2 * n * rows
    half = rows // 2
    j = np.arange(rows)[None, :]
    b = np.arange(rows)[:, None]

    def angle(a):
        return 2.0 * np.pi * ((j * (a + 2 * n * b)) % length) / length

    fwd = np.zeros((n, 2 * rows, 2 * rows))
    inv = np.zeros((n, 2 * rows, 2 * rows))
    for a in range(1, n):
        c, s = np.cos(angle(a)), np.sin(angle(a))
        fwd[a] = np.block([[c, s], [-s, c]])
        inv[a] = np.block([[c.T, -s.T], [s.T, c.T]]) * (2.0 / length)
    for slot, a in ((0, 0), (1, n)):
        c, s = np.cos(angle(a))[:half], np.sin(angle(a))[:half]
        weight = np.full((half, 1), 2.0 / length)
        re_rows = slice(slot * half, (slot + 1) * half)
        im_rows = slice(rows + slot * half, rows + (slot + 1) * half)
        cols = slice(slot * rows, (slot + 1) * rows)
        im = -s
        if slot == 0:
            im = im.copy()
            im[0] = np.cos(np.pi * np.arange(rows))
            weight[0] = 1.0 / length
        fwd[0, re_rows, cols] = c
        fwd[0, im_rows, cols] = im
        inv[0, cols, re_rows] = (c * weight).T
        inv[0, cols, im_rows] = (im * weight).T
    return fwd, inv


def scaled(coef, x):
    if abs(coef - 1.0) < 1e-12:
        return x
    if abs(coef + 1.0) < 1e-12:
        return -x
    return x * np.float32(coef)


def combine(terms, zero):
    total = None
    for coef, x in terms:
        if abs(coef) < 1e-12:
            continue
        if total is None:
            total = scaled(coef, x)
        elif coef < 0:
            total = total - scaled(-coef, x)
        else:
            total = total + scaled(coef, x)
    return zero if total is None else total


def kernel(
    n, nsec, chunk, steps,
    gq_hbm, gk_hbm, vi_hbm, fr_hbm, go_hbm, rate_hbm, skip_hbm, fwd_hbm, inv_hbm,
    oq_ref, ok_ref, op_ref, of_ref, orate_ref, oskip_ref,
    gq_ref, gk_ref, vi_ref, fr_ref, go_ref, rate_ref, skip_ref, fwd_ref, inv_ref,
    in_sem, row_sem,
    sbuf, rbuf, obuf, hbuf, pbuf, part, fold, sstat, gstat,
    s_send, s_recv, o_send, o_recv, p_send, p_recv, t_send, t_recv,
):
    rows = gq_ref.shape[0]
    width = chunk * steps
    seq = rows * n
    me = lax.axis_index("ctx")
    sec = lax.axis_index("section")
    before = lax.rem(sec + nsec - 1, nsec)
    after = lax.rem(sec + 1, nsec)

    def columns(owner, k):
        return pl.ds(pl.multiple_of(owner * width + k * chunk, chunk), chunk)

    tokens = (
        (gk_hbm, gk_ref), (vi_hbm, vi_ref), (gq_hbm, gq_ref), (go_hbm, go_ref), (fr_hbm, fr_ref)
    )
    whole = (
        (rate_hbm, rate_ref), (skip_hbm, skip_ref), (fwd_hbm, fwd_ref), (inv_hbm, inv_ref)
    )

    def load_first(g, d):
        hbm, ref = tokens[g]
        return pltpu.make_async_copy(
            hbm.at[:, columns(d, 0)], ref.at[:, columns(d, 0)], in_sem.at[g, 0, d]
        )

    def load_rest(g, d):
        hbm, ref = tokens[g]
        cols = pl.ds(pl.multiple_of(d * width + chunk, chunk), width - chunk)
        return pltpu.make_async_copy(hbm.at[:, cols], ref.at[:, cols], in_sem.at[g, 1, d])

    def load_whole(g):
        return pltpu.make_async_copy(whole[g][0], whole[g][1], row_sem.at[g])

    load_whole(0).start()
    for o in range(n):
        for g in range(5):
            load_first(g, lax.rem(me + 1 + o, n)).start()
    if steps > 1:
        for d in range(n):
            for g in range(5):
                load_rest(g, d).start()
    for g in range(1, 4):
        load_whole(g).start()

    barrier = pltpu.get_barrier_semaphore()
    for o in range(1, n):
        pl.semaphore_signal(
            barrier, inc=1, device_id={"ctx": lax.rem(me + o, n)}, device_id_type=MESH
        )
    for other in (before, after):
        pl.semaphore_signal(barrier, inc=1, device_id={"section": other}, device_id_type=MESH)
    pl.semaphore_wait(barrier, n + 1)
    load_whole(0).wait()

    def here(row0, count):
        row = lax.broadcasted_iota(jnp.int32, (count, 1), 0) + (row0 + me * rows)
        return row.astype(F32) * np.float32(1.0 / seq)

    def send_in(k, d):
        return pltpu.make_async_remote_copy(
            src_ref=sbuf.at[k, d], dst_ref=rbuf.at[k, me], send_sem=s_send.at[k, d],
            recv_sem=s_recv.at[k, me], device_id={"ctx": d}, device_id_type=MESH,
        )

    def got_in(k, m):
        return pltpu.make_async_remote_copy(
            src_ref=sbuf.at[k, m], dst_ref=rbuf.at[k, m], send_sem=s_send.at[k, m],
            recv_sem=s_recv.at[k, m], device_id={"ctx": m}, device_id_type=MESH,
        )

    def send_out(k, m):
        return pltpu.make_async_remote_copy(
            src_ref=obuf.at[k, m], dst_ref=hbuf.at[k, me], send_sem=o_send.at[k, m],
            recv_sem=o_recv.at[k, me], device_id={"ctx": m}, device_id_type=MESH,
        )

    def got_out(k, m):
        return pltpu.make_async_remote_copy(
            src_ref=obuf.at[k, m], dst_ref=hbuf.at[k, m], send_sem=o_send.at[k, m],
            recv_sem=o_recv.at[k, m], device_id={"ctx": m}, device_id_type=MESH,
        )

    def send_stat(d):
        return pltpu.make_async_remote_copy(
            src_ref=sstat, dst_ref=gstat.at[me], send_sem=t_send.at[d],
            recv_sem=t_recv.at[me], device_id={"ctx": d}, device_id_type=MESH,
        )

    def got_stat(m):
        return pltpu.make_async_remote_copy(
            src_ref=sstat, dst_ref=gstat.at[m], send_sem=t_send.at[m],
            recv_sem=t_recv.at[m], device_id={"ctx": m}, device_id_type=MESH,
        )

    def pass_copy(k, m):
        return pltpu.make_async_remote_copy(
            src_ref=pbuf.at[k, m], dst_ref=op_ref.at[:, columns(m, k)], send_sem=p_send.at[k, m],
            recv_sem=p_recv.at[k, m], device_id={"section": before}, device_id_type=MESH,
        )

    @pl.loop(0, steps * n)
    def _(i):
        k, o = i // n, lax.rem(i, n)
        d = lax.rem(me + 1 + o, n)
        cols = columns(d, k)

        @pl.when(k == 0)
        def _():
            for g in range(5):
                load_first(g, d).wait()

        if steps > 1:
            @pl.when(k == 1)
            def _():
                for g in range(5):
                    load_rest(g, d).wait()

        mixed = (gk_ref[:, cols].astype(F32) * vi_ref[:, cols].astype(F32)).astype(BF16)
        pulled = (gq_ref[:, cols].astype(F32) * go_ref[:, cols].astype(F32)).astype(BF16)
        envelope = jnp.exp(-rate_ref[:, cols] * here(0, rows))
        filt = (fr_ref[:, cols].astype(F32) * envelope).astype(BF16)
        sbuf[k, d, :, 0:chunk] = mixed
        sbuf[k, d, :, chunk:2 * chunk] = filt
        sbuf[k, d, :, 2 * chunk:3 * chunk] = pulled

        @pl.when(o < n - 1)
        def _():
            send_in(k, d).start()

        @pl.when(o == n - 1)
        def _():
            rbuf[k, me, :, 0:chunk] = mixed
            rbuf[k, me, :, chunk:2 * chunk] = filt
            rbuf[k, me, :, 2 * chunk:3 * chunk] = pulled

    @pl.when(sec == nsec - 1)
    def _():
        op_ref[...] = jnp.zeros_like(op_ref)

    for g in range(1, 4):
        load_whole(g).wait()

    tile = 16
    top = lax.broadcasted_iota(jnp.int32, (rows, 1), 0)

    @pl.loop(0, steps)
    def _(k):
        @pl.loop(0, n - 1)
        def _(o):
            got_in(k, lax.rem(me + 1 + o, n)).wait_recv()

        @pl.loop(0, rows // tile)
        def _(t):
            at = pl.ds(pl.multiple_of(t * tile, tile), tile)
            low = pl.ds(pl.multiple_of(rows + t * tile, tile), tile)
            for g in range(3):
                lanes = slice(g * chunk, (g + 1) * chunk)
                x = [rbuf[k, m, at, lanes].astype(F32) for m in range(n)]
                zero = jnp.zeros_like(x[0])
                even = combine([(1.0, x[m]) for m in range(0, n, 2)], zero)
                odd = combine([(1.0, x[m]) for m in range(1, n, 2)], zero)
                part[0, at, lanes] = (even + odd).astype(BF16)
                part[0, low, lanes] = (even - odd).astype(BF16)
                for a in range(1, n // 2 + 1):
                    cos = [math.cos(math.pi * m * a / n) for m in range(n)]
                    sin = [math.sin(math.pi * m * a / n) for m in range(n)]
                    ce = combine([(cos[m], x[m]) for m in range(0, n, 2)], zero)
                    co = combine([(cos[m], x[m]) for m in range(1, n, 2)], zero)
                    se = combine([(sin[m], x[m]) for m in range(0, n, 2)], zero)
                    so = combine([(sin[m], x[m]) for m in range(1, n, 2)], zero)
                    part[a, at, lanes] = (ce + co).astype(BF16)
                    part[a, low, lanes] = (-se - so).astype(BF16)
                    if n - a != a:
                        part[n - a, at, lanes] = (ce - co).astype(BF16)
                        part[n - a, low, lanes] = (se - so).astype(BF16)

        @pl.loop(0, n)
        def _(a):
            spec = jnp.dot(fwd_ref[a], part[a], preferred_element_type=F32)
            mr, fr, pr = (spec[:rows, g * chunk:(g + 1) * chunk] for g in range(3))
            mi, fi, pi = (spec[rows:, g * chunk:(g + 1) * chunk] for g in range(3))
            real_pair = jnp.logical_and(top == 0, a == 0)

            def product(ar, ai, br, bi, sign):
                cross = ai * bi
                re = ar * br + jnp.where(real_pair, 0.0, sign * cross)
                im = jnp.where(real_pair, cross, ar * bi - sign * ai * br)
                return re, im

            outs = (
                product(fr, fi, mr, mi, -1.0),
                product(fr, fi, pr, pi, 1.0),
                product(mr, mi, pr, pi, 1.0),
            )
            for g in range(3):
                lanes = slice(g * chunk, (g + 1) * chunk)
                part[a, 0:rows, lanes] = outs[g][0].astype(BF16)
                part[a, rows:2 * rows, lanes] = outs[g][1].astype(BF16)
            fold[a] = jnp.dot(inv_ref[a], part[a], preferred_element_type=F32)

        def unfold(t, carry):
            rate_sum, skip_sum = carry
            at = pl.ds(pl.multiple_of(t * tile, tile), tile)
            low = pl.ds(pl.multiple_of(rows + t * tile, tile), tile)
            for g in range(3):
                lanes = slice(g * chunk, (g + 1) * chunk)
                re = [fold[a, at, lanes] for a in range(n)]
                im = [fold[a, low, lanes] for a in range(n)]
                zero = jnp.zeros_like(re[0])
                for m in range(n):
                    terms = [(1.0, re[0]), ((-1.0) ** m, im[0])]
                    for a in range(1, n):
                        terms.append((math.cos(math.pi * m * a / n), re[a]))
                        terms.append((-math.sin(math.pi * m * a / n), im[a]))
                    value = combine(terms, zero).astype(BF16)
                    obuf[k, m, at, lanes] = value
                    if g == 2:
                        when = lax.broadcasted_iota(jnp.int32, (tile, 1), 0) + (t * tile + m * rows)
                        when = when.astype(F32) * np.float32(1.0 / seq)
                        mixed = rbuf[k, m, at, 0:chunk].astype(F32)
                        filt = rbuf[k, m, at, chunk:2 * chunk].astype(F32)
                        pulled = rbuf[k, m, at, 2 * chunk:3 * chunk].astype(F32)
                        rate_sum = rate_sum + when * value.astype(F32) * filt
                        skip_sum = skip_sum + mixed * pulled
            return rate_sum, skip_sum

        start = jnp.zeros((tile, chunk), F32)
        rate_sum, skip_sum = lax.fori_loop(0, rows // tile, unfold, (start, start))
        mine = pl.ds(pl.multiple_of(k * chunk, chunk), chunk)
        sstat[0:1, mine] = -jnp.sum(rate_sum, axis=0, keepdims=True)
        sstat[1:2, mine] = jnp.sum(skip_sum, axis=0, keepdims=True)

        @pl.loop(0, n - 1)
        def _(o):
            send_out(k, lax.rem(me + 1 + o, n)).start()

        hbuf[k, me] = obuf[k, me]

    for o in range(1, n):
        send_stat(lax.rem(me + o, n)).start()
    gstat[me] = sstat[...]

    @pl.loop(0, steps * n)
    def _(i):
        k, o = i // n, lax.rem(i, n)
        m = lax.rem(me + o, n)

        @pl.when(o > 0)
        def _():
            got_out(k, m).wait_recv()

        cols = columns(m, k)
        conv = hbuf[k, m, :, 0:chunk].astype(F32)
        adjoint = hbuf[k, m, :, chunk:2 * chunk].astype(F32)
        corr = hbuf[k, m, :, 2 * chunk:3 * chunk].astype(F32)
        mixed = sbuf[k, m, :, 0:chunk].astype(F32)
        pulled = sbuf[k, m, :, 2 * chunk:3 * chunk].astype(F32)
        skip = skip_ref[:, cols]
        oq_ref[:, cols] = (go_ref[:, cols].astype(F32) * (conv + skip * mixed)).astype(BF16)
        mixed_grad = adjoint + skip * pulled
        pbuf[k, m] = (mixed_grad * gk_ref[:, cols].astype(F32)).astype(BF16)

        @pl.when(sec > 0)
        def _():
            pass_copy(k, m).start()

        ok_ref[:, cols] = (mixed_grad * vi_ref[:, cols].astype(F32)).astype(BF16)
        envelope = jnp.exp(-rate_ref[:, cols] * here(0, rows))
        of_ref[:, cols] = (corr * envelope).astype(BF16)

    for o in range(1, n):
        got_stat(lax.rem(me + o, n)).wait_recv()
    for m in range(n):
        orate_ref[:, m * width:(m + 1) * width] = gstat[m, 0:1, :]
        oskip_ref[:, m * width:(m + 1) * width] = gstat[m, 1:2, :]

    for o in range(1, n):
        send_stat(lax.rem(me + o, n)).wait_send()

    @pl.loop(0, steps * (n - 1))
    def _(i):
        k, o = i // (n - 1), lax.rem(i, n - 1)
        d = lax.rem(me + 1 + o, n)
        send_in(k, d).wait_send()
        send_out(k, d).wait_send()

    @pl.loop(0, steps * n)
    def _(i):
        k, m = i // n, lax.rem(i, n)

        @pl.when(sec > 0)
        def _():
            pass_copy(k, m).wait_send()

        @pl.when(sec < nsec - 1)
        def _():
            pass_copy(k, m).wait_recv()


def finish(*refs):
    count = (len(refs) - 1) // 2
    sem = refs[-1]
    copies = [
        pltpu.make_async_copy(refs[g], refs[count + g], sem.at[g]) for g in range(count)
    ]
    for copy in copies:
        copy.start()
    for copy in copies:
        copy.wait()


def shards(n, nsec, gate_q, gate_k, value_in, filter_raw, decay_rate, skip_gain, grad_out):
    rows, channels = gate_q.shape[1:]
    width = channels // n
    chunk = 128
    steps = width // chunk
    fwd, inv = make_tables(n, rows)
    fwd, inv = jnp.asarray(fwd, BF16), jnp.asarray(inv, BF16)
    block = jax.ShapeDtypeStruct((rows, channels), BF16)
    row = jax.ShapeDtypeStruct((1, channels), F32)
    message = (steps, n, rows, 3 * chunk)
    dma = pltpu.SemaphoreType.DMA
    anywhere = pl.BlockSpec(memory_space=pl.ANY)
    inside = pl.BlockSpec(memory_space=pltpu.VMEM)
    shapes = (block, block, block, block, row, row)
    outs = pl.pallas_call(
        functools.partial(kernel, n, nsec, chunk, steps),
        out_shape=tuple(pltpu.VMEM(shape.shape, shape.dtype) for shape in shapes),
        in_specs=[anywhere] * 9,
        out_specs=(inside,) * 6,
        scratch_shapes=[
            *([pltpu.VMEM((rows, channels), BF16)] * 5),
            *([pltpu.VMEM((1, channels), F32)] * 2),
            *([pltpu.VMEM(fwd.shape, BF16)] * 2),
            dma((5, 2, n)), dma((4,)),
            pltpu.VMEM(message, BF16),
            pltpu.VMEM(message, BF16),
            pltpu.VMEM(message, BF16),
            pltpu.VMEM(message, BF16),
            pltpu.VMEM((steps, n, rows, chunk), BF16),
            pltpu.VMEM((n, 2 * rows, 3 * chunk), BF16),
            pltpu.VMEM((n, 2 * rows, 3 * chunk), F32),
            pltpu.VMEM((2, width), F32),
            pltpu.VMEM((n, 2, width), F32),
            dma((steps, n)), dma((steps, n)), dma((steps, n)), dma((steps, n)),
            dma((steps, n)), dma((steps, n)), dma((n,)), dma((n,)),
        ],
        compiler_params=pltpu.CompilerParams(
            collective_id=0, has_side_effects=True, vmem_limit_bytes=58 * 1024 * 1024
        ),
        name="hyena_backward",
    )(
        gate_q[0], gate_k[0], value_in[0], filter_raw[0], grad_out[0],
        decay_rate, skip_gain, fwd, inv,
    )
    oq, ok, op, of, orate, oskip = pl.pallas_call(
        finish,
        out_shape=shapes,
        in_specs=[inside] * 6,
        out_specs=(anywhere,) * 6,
        scratch_shapes=[dma((6,))],
        compiler_params=pltpu.CompilerParams(vmem_limit_bytes=4 * 1024 * 1024),
        name="hand_over",
    )(*(pltpu.with_memory_space_constraint(out, pltpu.VMEM) for out in outs))
    return oq[None], ok[None], op[None], of[None], orate, oskip


def solution(mesh):
    n, nsec = mesh.shape["ctx"], mesh.shape["section"]
    tokens = P("section", "ctx", None)
    return jax.shard_map(
        functools.partial(shards, n, nsec),
        mesh=mesh,
        in_specs=(tokens, tokens, tokens, tokens, P("section", None), P("section", None), tokens),
        out_specs=(tokens, tokens, tokens, tokens, P("section", None), P("section", None)),
        check_vma=False,
    )
```

```python
import functools
import math

import jax
import jax.numpy as jnp
import numpy as np
from jax import lax
from jax.experimental import pallas as pl
from jax.experimental.pallas import tpu as pltpu
from jax.sharding import PartitionSpec as P

MESH = pl.DeviceIdType.MESH
F32 = jnp.float32
BF16 = jnp.bfloat16


def make_tables(n, rows):
    length = 2 * n * rows
    half = rows // 2
    j = np.arange(rows)[None, :]
    b = np.arange(rows)[:, None]

    def angle(a):
        return 2.0 * np.pi * ((j * (a + 2 * n * b)) % length) / length

    fwd = np.zeros((n, 2 * rows, 2 * rows))
    inv = np.zeros((n, 2 * rows, 2 * rows))
    for a in range(1, n):
        c, s = np.cos(angle(a)), np.sin(angle(a))
        fwd[a] = np.block([[c, s], [-s, c]])
        inv[a] = np.block([[c.T, -s.T], [s.T, c.T]]) * (2.0 / length)
    for slot, a in ((0, 0), (1, n)):
        c, s = np.cos(angle(a))[:half], np.sin(angle(a))[:half]
        weight = np.full((half, 1), 2.0 / length)
        re_rows = slice(slot * half, (slot + 1) * half)
        im_rows = slice(rows + slot * half, rows + (slot + 1) * half)
        cols = slice(slot * rows, (slot + 1) * rows)
        im = -s
        if slot == 0:
            im = im.copy()
            im[0] = np.cos(np.pi * np.arange(rows))
            weight[0] = 1.0 / length
        fwd[0, re_rows, cols] = c
        fwd[0, im_rows, cols] = im
        inv[0, cols, re_rows] = (c * weight).T
        inv[0, cols, im_rows] = (im * weight).T
    return fwd, inv


def scaled(coef, x):
    if abs(coef - 1.0) < 1e-12:
        return x
    if abs(coef + 1.0) < 1e-12:
        return -x
    return x * np.float32(coef)


def combine(terms, zero):
    total = None
    for coef, x in terms:
        if abs(coef) < 1e-12:
            continue
        if total is None:
            total = scaled(coef, x)
        elif coef < 0:
            total = total - scaled(-coef, x)
        else:
            total = total + scaled(coef, x)
    return zero if total is None else total


def kernel(
    n, nsec, chunk, steps,
    gq_hbm, gk_hbm, vi_hbm, fr_hbm, go_hbm, rate_hbm, skip_hbm, fwd_hbm, inv_hbm,
    oq_ref, ok_ref, op_ref, of_ref, orate_ref, oskip_ref,
    gq_ref, gk_ref, vi_ref, fr_ref, go_ref, rate_ref, skip_ref, fwd_ref, inv_ref,
    in_sem, row_sem,
    sbuf, rbuf, obuf, hbuf, pbuf, part, fold, sstat, gstat,
    s_send, s_recv, o_send, o_recv, p_send, p_recv, t_send, t_recv,
):
    rows = gq_ref.shape[0]
    width = chunk * steps
    seq = rows * n
    me = lax.axis_index("ctx")
    sec = lax.axis_index("section")
    before = lax.rem(sec + nsec - 1, nsec)
    after = lax.rem(sec + 1, nsec)

    def columns(owner, k):
        return pl.ds(pl.multiple_of(owner * width + k * chunk, chunk), chunk)

    tokens = (
        (gk_hbm, gk_ref), (vi_hbm, vi_ref), (gq_hbm, gq_ref), (go_hbm, go_ref), (fr_hbm, fr_ref)
    )
    whole = (
        (rate_hbm, rate_ref), (skip_hbm, skip_ref), (fwd_hbm, fwd_ref), (inv_hbm, inv_ref)
    )

    def load_first(g, d):
        hbm, ref = tokens[g]
        return pltpu.make_async_copy(
            hbm.at[:, columns(d, 0)], ref.at[:, columns(d, 0)], in_sem.at[g, 0, d]
        )

    def load_rest(g, d):
        hbm, ref = tokens[g]
        cols = pl.ds(pl.multiple_of(d * width + chunk, chunk), width - chunk)
        return pltpu.make_async_copy(hbm.at[:, cols], ref.at[:, cols], in_sem.at[g, 1, d])

    def load_whole(g):
        return pltpu.make_async_copy(whole[g][0], whole[g][1], row_sem.at[g])

    load_whole(0).start()
    for o in range(n):
        for g in range(5):
            load_first(g, lax.rem(me + 1 + o, n)).start()
    if steps > 1:
        for d in range(n):
            for g in range(5):
                load_rest(g, d).start()
    for g in range(1, 4):
        load_whole(g).start()

    barrier = pltpu.get_barrier_semaphore()
    for o in range(1, n):
        pl.semaphore_signal(
            barrier, inc=1, device_id={"ctx": lax.rem(me + o, n)}, device_id_type=MESH
        )
    for other in (before, after):
        pl.semaphore_signal(barrier, inc=1, device_id={"section": other}, device_id_type=MESH)
    pl.semaphore_wait(barrier, n + 1)
    load_whole(0).wait()

    def here(row0, count):
        row = lax.broadcasted_iota(jnp.int32, (count, 1), 0) + (row0 + me * rows)
        return row.astype(F32) * np.float32(1.0 / seq)

    def send_in(k, d):
        return pltpu.make_async_remote_copy(
            src_ref=sbuf.at[k, d], dst_ref=rbuf.at[k, me], send_sem=s_send.at[k, d],
            recv_sem=s_recv.at[k, me], device_id={"ctx": d}, device_id_type=MESH,
        )

    def got_in(k, m):
        return pltpu.make_async_remote_copy(
            src_ref=sbuf.at[k, m], dst_ref=rbuf.at[k, m], send_sem=s_send.at[k, m],
            recv_sem=s_recv.at[k, m], device_id={"ctx": m}, device_id_type=MESH,
        )

    def send_out(k, m):
        return pltpu.make_async_remote_copy(
            src_ref=obuf.at[k, m], dst_ref=hbuf.at[k, me], send_sem=o_send.at[k, m],
            recv_sem=o_recv.at[k, me], device_id={"ctx": m}, device_id_type=MESH,
        )

    def got_out(k, m):
        return pltpu.make_async_remote_copy(
            src_ref=obuf.at[k, m], dst_ref=hbuf.at[k, m], send_sem=o_send.at[k, m],
            recv_sem=o_recv.at[k, m], device_id={"ctx": m}, device_id_type=MESH,
        )

    def send_stat(d):
        return pltpu.make_async_remote_copy(
            src_ref=sstat, dst_ref=gstat.at[me], send_sem=t_send.at[d],
            recv_sem=t_recv.at[me], device_id={"ctx": d}, device_id_type=MESH,
        )

    def got_stat(m):
        return pltpu.make_async_remote_copy(
            src_ref=sstat, dst_ref=gstat.at[m], send_sem=t_send.at[m],
            recv_sem=t_recv.at[m], device_id={"ctx": m}, device_id_type=MESH,
        )

    def pass_copy(k, m):
        return pltpu.make_async_remote_copy(
            src_ref=pbuf.at[k, m], dst_ref=op_ref.at[:, columns(m, k)], send_sem=p_send.at[k, m],
            recv_sem=p_recv.at[k, m], device_id={"section": before}, device_id_type=MESH,
        )

    @pl.loop(0, steps * n)
    def _(i):
        k, o = i // n, lax.rem(i, n)
        d = lax.rem(me + 1 + o, n)
        cols = columns(d, k)

        @pl.when(k == 0)
        def _():
            for g in range(5):
                load_first(g, d).wait()

        if steps > 1:
            @pl.when(k == 1)
            def _():
                for g in range(5):
                    load_rest(g, d).wait()

        mixed = (gk_ref[:, cols].astype(F32) * vi_ref[:, cols].astype(F32)).astype(BF16)
        pulled = (gq_ref[:, cols].astype(F32) * go_ref[:, cols].astype(F32)).astype(BF16)
        envelope = jnp.exp(-rate_ref[:, cols] * here(0, rows))
        filt = (fr_ref[:, cols].astype(F32) * envelope).astype(BF16)
        sbuf[k, d, :, 0:chunk] = mixed
        sbuf[k, d, :, chunk:2 * chunk] = filt
        sbuf[k, d, :, 2 * chunk:3 * chunk] = pulled

        @pl.when(o < n - 1)
        def _():
            send_in(k, d).start()

        @pl.when(o == n - 1)
        def _():
            rbuf[k, me, :, 0:chunk] = mixed
            rbuf[k, me, :, chunk:2 * chunk] = filt
            rbuf[k, me, :, 2 * chunk:3 * chunk] = pulled

    @pl.when(sec == nsec - 1)
    def _():
        op_ref[...] = jnp.zeros_like(op_ref)

    for g in range(1, 4):
        load_whole(g).wait()

    tile = 16
    top = lax.broadcasted_iota(jnp.int32, (rows, 1), 0)

    @pl.loop(0, steps)
    def _(k):
        @pl.loop(0, n - 1)
        def _(o):
            got_in(k, lax.rem(me + 1 + o, n)).wait_recv()

        @pl.loop(0, rows // tile)
        def _(t):
            at = pl.ds(pl.multiple_of(t * tile, tile), tile)
            low = pl.ds(pl.multiple_of(rows + t * tile, tile), tile)
            for g in range(3):
                lanes = slice(g * chunk, (g + 1) * chunk)
                x = [rbuf[k, m, at, lanes].astype(F32) for m in range(n)]
                zero = jnp.zeros_like(x[0])
                even = combine([(1.0, x[m]) for m in range(0, n, 2)], zero)
                odd = combine([(1.0, x[m]) for m in range(1, n, 2)], zero)
                part[0, at, lanes] = (even + odd).astype(BF16)
                part[0, low, lanes] = (even - odd).astype(BF16)
                for a in range(1, n // 2 + 1):
                    cos = [math.cos(math.pi * m * a / n) for m in range(n)]
                    sin = [math.sin(math.pi * m * a / n) for m in range(n)]
                    ce = combine([(cos[m], x[m]) for m in range(0, n, 2)], zero)
                    co = combine([(cos[m], x[m]) for m in range(1, n, 2)], zero)
                    se = combine([(sin[m], x[m]) for m in range(0, n, 2)], zero)
                    so = combine([(sin[m], x[m]) for m in range(1, n, 2)], zero)
                    part[a, at, lanes] = (ce + co).astype(BF16)
                    part[a, low, lanes] = (-se - so).astype(BF16)
                    if n - a != a:
                        part[n - a, at, lanes] = (ce - co).astype(BF16)
                        part[n - a, low, lanes] = (se - so).astype(BF16)

        @pl.loop(0, n)
        def _(a):
            spec = jnp.dot(fwd_ref[a], part[a], preferred_element_type=F32)
            mr, fr, pr = (spec[:rows, g * chunk:(g + 1) * chunk] for g in range(3))
            mi, fi, pi = (spec[rows:, g * chunk:(g + 1) * chunk] for g in range(3))
            real_pair = jnp.logical_and(top == 0, a == 0)

            def product(ar, ai, br, bi, sign):
                cross = ai * bi
                re = ar * br + jnp.where(real_pair, 0.0, sign * cross)
                im = jnp.where(real_pair, cross, ar * bi - sign * ai * br)
                return re, im

            outs = (
                product(fr, fi, mr, mi, -1.0),
                product(fr, fi, pr, pi, 1.0),
                product(mr, mi, pr, pi, 1.0),
            )
            for g in range(3):
                lanes = slice(g * chunk, (g + 1) * chunk)
                part[a, 0:rows, lanes] = outs[g][0].astype(BF16)
                part[a, rows:2 * rows, lanes] = outs[g][1].astype(BF16)
            fold[a] = jnp.dot(inv_ref[a], part[a], preferred_element_type=F32)

        def unfold(t, carry):
            rate_sum, skip_sum = carry
            at = pl.ds(pl.multiple_of(t * tile, tile), tile)
            low = pl.ds(pl.multiple_of(rows + t * tile, tile), tile)
            for g in range(3):
                lanes = slice(g * chunk, (g + 1) * chunk)
                re = [fold[a, at, lanes] for a in range(n)]
                im = [fold[a, low, lanes] for a in range(n)]
                zero = jnp.zeros_like(re[0])
                for m in range(n):
                    terms = [(1.0, re[0]), ((-1.0) ** m, im[0])]
                    for a in range(1, n):
                        terms.append((math.cos(math.pi * m * a / n), re[a]))
                        terms.append((-math.sin(math.pi * m * a / n), im[a]))
                    value = combine(terms, zero).astype(BF16)
                    obuf[k, m, at, lanes] = value
                    if g == 2:
                        when = lax.broadcasted_iota(jnp.int32, (tile, 1), 0) + (t * tile + m * rows)
                        when = when.astype(F32) * np.float32(1.0 / seq)
                        mixed = rbuf[k, m, at, 0:chunk].astype(F32)
                        filt = rbuf[k, m, at, chunk:2 * chunk].astype(F32)
                        pulled = rbuf[k, m, at, 2 * chunk:3 * chunk].astype(F32)
                        rate_sum = rate_sum + when * value.astype(F32) * filt
                        skip_sum = skip_sum + mixed * pulled
            return rate_sum, skip_sum

        start = jnp.zeros((tile, chunk), F32)
        rate_sum, skip_sum = lax.fori_loop(0, rows // tile, unfold, (start, start))
        mine = pl.ds(pl.multiple_of(k * chunk, chunk), chunk)
        sstat[0:1, mine] = -jnp.sum(rate_sum, axis=0, keepdims=True)
        sstat[1:2, mine] = jnp.sum(skip_sum, axis=0, keepdims=True)

        @pl.loop(0, n - 1)
        def _(o):
            send_out(k, lax.rem(me + 1 + o, n)).start()

        hbuf[k, me] = obuf[k, me]

    for o in range(1, n):
        send_stat(lax.rem(me + o, n)).start()
    gstat[me] = sstat[...]

    @pl.loop(0, steps * n)
    def _(i):
        k, o = i // n, lax.rem(i, n)
        m = lax.rem(me + o, n)

        @pl.when(o > 0)
        def _():
            got_out(k, m).wait_recv()

        cols = columns(m, k)
        conv = hbuf[k, m, :, 0:chunk].astype(F32)
        adjoint = hbuf[k, m, :, chunk:2 * chunk].astype(F32)
        corr = hbuf[k, m, :, 2 * chunk:3 * chunk].astype(F32)
        mixed = sbuf[k, m, :, 0:chunk].astype(F32)
        pulled = sbuf[k, m, :, 2 * chunk:3 * chunk].astype(F32)
        skip = skip_ref[:, cols]
        oq_ref[:, cols] = (go_ref[:, cols].astype(F32) * (conv + skip * mixed)).astype(BF16)
        mixed_grad = adjoint + skip * pulled
        pbuf[k, m] = (mixed_grad * gk_ref[:, cols].astype(F32)).astype(BF16)

        @pl.when(sec > 0)
        def _():
            pass_copy(k, m).start()

        ok_ref[:, cols] = (mixed_grad * vi_ref[:, cols].astype(F32)).astype(BF16)
        envelope = jnp.exp(-rate_ref[:, cols] * here(0, rows))
        of_ref[:, cols] = (corr * envelope).astype(BF16)

    for o in range(1, n):
        got_stat(lax.rem(me + o, n)).wait_recv()
    for m in range(n):
        orate_ref[:, m * width:(m + 1) * width] = gstat[m, 0:1, :]
        oskip_ref[:, m * width:(m + 1) * width] = gstat[m, 1:2, :]

    for o in range(1, n):
        send_stat(lax.rem(me + o, n)).wait_send()

    @pl.loop(0, steps * (n - 1))
    def _(i):
        k, o = i // (n - 1), lax.rem(i, n - 1)
        d = lax.rem(me + 1 + o, n)
        send_in(k, d).wait_send()
        send_out(k, d).wait_send()

    @pl.loop(0, steps * n)
    def _(i):
        k, m = i // n, lax.rem(i, n)

        @pl.when(sec > 0)
        def _():
            pass_copy(k, m).wait_send()

        @pl.when(sec < nsec - 1)
        def _():
            pass_copy(k, m).wait_recv()


def make_local_tables(rows):
    length = 2 * rows
    j = np.arange(rows)[None, :]
    b = np.arange(rows)[:, None]
    angle = 2.0 * np.pi * ((j * b) % length) / length
    re, im = np.cos(angle), -np.sin(angle)
    im[0] = np.cos(np.pi * np.arange(rows))
    weight = np.full((rows, 1), 2.0 / length)
    weight[0] = 1.0 / length
    return np.concatenate([re, im]), np.concatenate([re * weight, im * weight]).T


def split(chunks):
    zero, first = chunks * 6 // 32, chunks // 4
    third = (chunks - zero - first) // 2
    counts = (zero, first, chunks - zero - first - third, third)
    bases = tuple(sum(counts[:o]) for o in range(4))
    return counts, bases, chunks // 16, chunks * 3 // 32


def quad_kernel(
    nsec, chunk,
    gq_hbm, gk_hbm, vi_hbm, fr_hbm, go_hbm, rate_hbm, skip_hbm, fwd_hbm, inv_hbm, fwdl_hbm, invl_hbm,
    oq_ref, ok_ref, op_ref, of_ref, orate_ref, oskip_ref,
    gq_ref, gk_ref, vi_ref, fr_ref, go_ref, rate_ref, skip_ref, fwd_ref, inv_ref, fwdl_ref, invl_ref,
    in_sem, row_sem,
    sbuf, rbuf, obuf, hbuf, pbuf, lbuf, relin, relout, part, fold, sown, sloc, gown, gloc,
    i_send, i_recv, ri_send, ri_recv, o_send, o_recv, ro_send, ro_recv, p_send, p_recv,
    t_send, t_recv,
):
    n = 4
    rows, channels = gq_ref.shape
    chunks = channels // chunk
    counts, bases, rin, rout = split(chunks)
    most = max(counts)
    seq = rows * n
    me = lax.axis_index("ctx")
    sec = lax.axis_index("section")
    before = lax.rem(sec + nsec - 1, nsec)
    after = lax.rem(sec + 1, nsec)
    is1 = me * (3 - me) * (2 - me) // 2
    is2 = me * (3 - me) * (me - 1) // 2
    is3 = me * (me - 1) * (me - 2) // 6
    is0 = 1 - is1 - is2 - is3
    own = is0 * counts[0] + is1 * counts[1] + is2 * counts[2] + is3 * counts[3]
    base = is1 * bases[1] + is2 * bases[2] + is3 * bases[3]

    def lanes_of(c):
        return pl.ds(pl.multiple_of(c * chunk, chunk), chunk)

    tokens = (
        (gk_hbm, gk_ref), (vi_hbm, vi_ref), (gq_hbm, gq_ref), (go_hbm, go_ref), (fr_hbm, fr_ref)
    )
    whole = (
        (rate_hbm, rate_ref), (skip_hbm, skip_ref), (fwd_hbm, fwd_ref), (inv_hbm, inv_ref),
        (fwdl_hbm, fwdl_ref), (invl_hbm, invl_ref),
    )

    def load(g, o, rest):
        hbm, ref = tokens[g]
        lo = bases[o] + rest
        hi = bases[o] + counts[o] if rest else lo + 1
        cols = slice(lo * chunk, hi * chunk)
        return pltpu.make_async_copy(hbm.at[:, cols], ref.at[:, cols], in_sem.at[g, rest, o])

    def load_whole(g):
        return pltpu.make_async_copy(whole[g][0], whole[g][1], row_sem.at[g])

    load_whole(0).start()
    for rest in range(2):
        for o in range(n):
            for g in range(5):
                load(g, o, rest).start()
    for g in range(1, 6):
        load_whole(g).start()

    barrier = pltpu.get_barrier_semaphore()
    for o in range(1, n):
        pl.semaphore_signal(
            barrier, inc=1, device_id={"ctx": lax.rem(me + o, n)}, device_id_type=MESH
        )
    for other in (before, after):
        pl.semaphore_signal(barrier, inc=1, device_id={"section": other}, device_id_type=MESH)
    pl.semaphore_wait(barrier, n + 1)
    load_whole(0).wait()

    def to(d):
        return {"ctx": jnp.int32(d)}

    def remote(src, dst, send, recv, where):
        return pltpu.make_async_remote_copy(
            src_ref=src, dst_ref=dst, send_sem=send, recv_sem=recv,
            device_id=where, device_id_type=MESH,
        )

    def give_pair(o, k):
        c = bases[o] + k
        return remote(
            sbuf.at[c, 0:2], rbuf.at[k, 0, 0:2], i_send.at[c], i_recv.at[k, 0], to(o)
        )

    def give_all(o, k):
        c = bases[o] + k
        return remote(sbuf.at[c], rbuf.at[k, me], i_send.at[c], i_recv.at[k, me], to(o))

    def give_relay(k):
        c = bases[1] + k
        return remote(sbuf.at[c], relin.at[k], i_send.at[c], ri_recv.at[k], to(0))

    def forward_in(i):
        return remote(
            relin.at[i], rbuf.at[i, 2], ri_send.at[i], i_recv.at[i, 2], to(1)
        )

    def got_in(k, s):
        at = rbuf.at[k, 0, 0:2] if s == 0 else rbuf.at[k, s]
        src = sbuf.at[0, 0:2] if s == 0 else sbuf.at[0]
        return remote(src, at, i_send.at[0], i_recv.at[k, s], to(s))

    def back_pair(k):
        return remote(
            obuf.at[k, 0, 1:3], hbuf.at[base + k, 1:3], o_send.at[k, 0], o_recv.at[base + k], to(0)
        )

    def back_all(k, m):
        return remote(
            obuf.at[k, m], hbuf.at[base + k], o_send.at[k, m], o_recv.at[base + k], to(m)
        )

    def back_relay(k):
        return remote(obuf.at[k, 1], relout.at[k], o_send.at[k, 1], ro_recv.at[k], to(0))

    def forward_out(k):
        c = bases[2] + k
        return remote(relout.at[k], hbuf.at[c], ro_send.at[k], o_recv.at[c], to(1))

    def got_pair(c):
        return remote(
            obuf.at[0, 0, 1:3], hbuf.at[c, 1:3], o_send.at[0, 0], o_recv.at[c], to(1)
        )

    def got_all(c):
        return remote(obuf.at[0, 0], hbuf.at[c], o_send.at[0, 0], o_recv.at[c], to(1))

    def stat_own(o, d):
        cols = slice(bases[o] * chunk, (bases[o] + counts[o]) * chunk)
        return remote(
            sown.at[:, cols], gown.at[:, cols], t_send.at[0, d], t_recv.at[0, o], to(d)
        )

    def stat_local(d):
        return remote(sloc, gloc, t_send.at[1, d], t_recv.at[1, 0], to(d))

    def pass_copy(c):
        return remote(
            pbuf.at[c], op_ref.at[:, lanes_of(c)], p_send.at[c], p_recv.at[c],
            {"section": before},
        )

    when = lax.broadcasted_iota(jnp.int32, (rows, 1), 0) + me * rows
    when = when.astype(F32) * np.float32(1.0 / seq)

    @pl.loop(0, most)
    def _(step):
        for o in range(n):
            k = step * counts[o] // most

            @pl.when((step + 1) * counts[o] // most > k)
            def _(o=o, k=k):
                for rest in range(2):
                    @pl.when(k == rest)
                    def _():
                        for g in range(5):
                            load(g, o, rest).wait()

                c = bases[o] + k
                cols = lanes_of(c)
                mixed = (gk_ref[:, cols].astype(F32) * vi_ref[:, cols].astype(F32)).astype(BF16)
                pulled = (gq_ref[:, cols].astype(F32) * go_ref[:, cols].astype(F32)).astype(BF16)
                envelope = jnp.exp(-rate_ref[:, cols] * when)
                filt = (fr_ref[:, cols].astype(F32) * envelope).astype(BF16)
                sbuf[c, 0] = mixed
                sbuf[c, 1] = filt
                sbuf[c, 2] = pulled

                @pl.when(me == o)
                def _():
                    rbuf[k, o, 0] = mixed
                    rbuf[k, o, 1] = filt
                    if o:
                        rbuf[k, o, 2] = pulled

                if o:
                    @pl.when(me == 0)
                    def _():
                        give_pair(o, k).start()

                if o == 1:
                    @pl.when(jnp.logical_and(me == 2, k < rin))
                    def _():
                        give_relay(k).start()

                    @pl.when(jnp.logical_or(me == 3, jnp.logical_and(me == 2, k >= rin)))
                    def _():
                        give_all(o, k).start()
                else:
                    @pl.when(jnp.logical_and(me != 0, me != o))
                    def _():
                        give_all(o, k).start()

    @pl.when(sec == nsec - 1)
    def _():
        op_ref[...] = jnp.zeros_like(op_ref)

    for g in range(1, 6):
        load_whole(g).wait()

    tile = 16
    top = lax.broadcasted_iota(jnp.int32, (rows, 1), 0)

    def product(real_pair, ar, ai, br, bi, sign):
        cross = ai * bi
        re = ar * br + jnp.where(real_pair, 0.0, sign * cross)
        im = jnp.where(real_pair, cross, ar * bi - sign * ai * br)
        return re, im

    def products(spec, real_pair):
        mr, fr, pr = (spec[:rows, g * chunk:(g + 1) * chunk] for g in range(3))
        mi, fi, pi = (spec[rows:, g * chunk:(g + 1) * chunk] for g in range(3))
        return (
            product(real_pair, fr, fi, mr, mi, -1.0),
            product(real_pair, fr, fi, pr, pi, 1.0),
            product(real_pair, mr, mi, pr, pi, 1.0),
        )

    @pl.when(me == 0)
    def _():
        @pl.loop(0, chunks)
        def _(c):
            if rin:
                @pl.when(c < rin)
                def _():
                    give_relay(c).wait_recv()
                    forward_in(c).start()

            for g in range(3):
                part[0, 0:rows, g * chunk:(g + 1) * chunk] = sbuf[c, g]
            spec = jnp.dot(fwdl_ref[...], part[0, 0:rows, :], preferred_element_type=F32)
            outs = products(spec, top == 0)
            for g in range(3):
                lanes = slice(g * chunk, (g + 1) * chunk)
                part[1, 0:rows, lanes] = outs[g][0].astype(BF16)
                part[1, rows:2 * rows, lanes] = outs[g][1].astype(BF16)
            back = jnp.dot(invl_ref[...], part[1], preferred_element_type=F32).astype(BF16)
            corr = back[:, 2 * chunk:3 * chunk]
            hbuf[c, 0] = back[:, 0:chunk]
            lbuf[c, 0] = back[:, chunk:2 * chunk]
            lbuf[c, 1] = corr
            rate = when * corr.astype(F32) * sbuf[c, 1].astype(F32)
            skip = sbuf[c, 0].astype(F32) * sbuf[c, 2].astype(F32)
            cols = lanes_of(c)
            sloc[0:1, cols] = -jnp.sum(rate, axis=0, keepdims=True)
            sloc[1:2, cols] = jnp.sum(skip, axis=0, keepdims=True)

        for d in range(1, n):
            stat_local(d).start()
        gloc[...] = sloc[...]

    @pl.loop(0, own)
    def _(k):
        for s in range(n):
            @pl.when(me != s)
            def _():
                got_in(k, s).wait_recv()

        @pl.when(jnp.logical_and(me == 0, jnp.logical_and(k >= 1, k <= rout)))
        def _():
            back_relay(k - 1).wait_recv()
            forward_out(k - 1).start()

        @pl.loop(0, rows // tile)
        def _(t):
            at = pl.ds(pl.multiple_of(t * tile, tile), tile)
            low = pl.ds(pl.multiple_of(rows + t * tile, tile), tile)
            for g in range(3):
                lanes = slice(g * chunk, (g + 1) * chunk)
                held = range(1, n) if g == 2 else range(n)
                x = {m: rbuf[k, m, g, at, :].astype(F32) for m in held}
                even = [m for m in held if m % 2 == 0]
                odd = [m for m in held if m % 2 == 1]
                zero = jnp.zeros_like(x[1])
                e = combine([(1.0, x[m]) for m in even], zero)
                d = combine([(1.0, x[m]) for m in odd], zero)
                part[0, at, lanes] = (e + d).astype(BF16)
                part[0, low, lanes] = (e - d).astype(BF16)
                for a in range(1, n // 2 + 1):
                    cos = [math.cos(math.pi * m * a / n) for m in range(n)]
                    sin = [math.sin(math.pi * m * a / n) for m in range(n)]
                    ce = combine([(cos[m], x[m]) for m in even], zero)
                    co = combine([(cos[m], x[m]) for m in odd], zero)
                    se = combine([(sin[m], x[m]) for m in even], zero)
                    so = combine([(sin[m], x[m]) for m in odd], zero)
                    part[a, at, lanes] = (ce + co).astype(BF16)
                    part[a, low, lanes] = (-se - so).astype(BF16)
                    if n - a != a:
                        part[n - a, at, lanes] = (ce - co).astype(BF16)
                        part[n - a, low, lanes] = (se - so).astype(BF16)

        @pl.loop(0, n)
        def _(a):
            spec = jnp.dot(fwd_ref[a], part[a], preferred_element_type=F32)
            outs = products(spec, jnp.logical_and(top == 0, a == 0))
            for g in range(3):
                lanes = slice(g * chunk, (g + 1) * chunk)
                part[a, 0:rows, lanes] = outs[g][0].astype(BF16)
                part[a, rows:2 * rows, lanes] = outs[g][1].astype(BF16)
            fold[a] = jnp.dot(inv_ref[a], part[a], preferred_element_type=F32)

        def unfold(t, carry):
            rate_sum, skip_sum = carry
            at = pl.ds(pl.multiple_of(t * tile, tile), tile)
            low = pl.ds(pl.multiple_of(rows + t * tile, tile), tile)
            for g in range(3):
                lanes = slice(g * chunk, (g + 1) * chunk)
                re = [fold[a, at, lanes] for a in range(n)]
                im = [fold[a, low, lanes] for a in range(n)]
                zero = jnp.zeros_like(re[0])
                for m in range(1 if g == 0 else 0, n):
                    terms = [(1.0, re[0]), ((-1.0) ** m, im[0])]
                    for a in range(1, n):
                        terms.append((math.cos(math.pi * m * a / n), re[a]))
                        terms.append((-math.sin(math.pi * m * a / n), im[a]))
                    value = combine(terms, zero).astype(BF16)
                    obuf[k, m, g, at, :] = value
                    if g == 2:
                        pos = lax.broadcasted_iota(jnp.int32, (tile, 1), 0) + (t * tile + m * rows)
                        pos = pos.astype(F32) * np.float32(1.0 / seq)
                        filt = rbuf[k, m, 1, at, :].astype(F32)
                        rate_sum = rate_sum + pos * value.astype(F32) * filt
                        if m:
                            mixed = rbuf[k, m, 0, at, :].astype(F32)
                            pulled = rbuf[k, m, 2, at, :].astype(F32)
                            skip_sum = skip_sum + mixed * pulled
            return rate_sum, skip_sum

        start = jnp.zeros((tile, chunk), F32)
        rate_sum, skip_sum = lax.fori_loop(0, rows // tile, unfold, (start, start))
        mine = lanes_of(base + k)
        sown[0:1, mine] = -jnp.sum(rate_sum, axis=0, keepdims=True)
        sown[1:2, mine] = jnp.sum(skip_sum, axis=0, keepdims=True)

        @pl.when(me != 0)
        def _():
            back_pair(k).start()

        direct = jnp.logical_or(me != 2, k >= rout)

        @pl.when(jnp.logical_not(direct))
        def _():
            back_relay(k).start()

        @pl.when(jnp.logical_and(me != 1, direct))
        def _():
            back_all(k, 1).start()

        for m in range(2, n):
            @pl.when(me != m)
            def _():
                back_all(k, m).start()

        @pl.when(me == 0)
        def _():
            hbuf[base + k, 1:3] = obuf[k, 0, 1:3]

        @pl.when(me != 0)
        def _():
            hbuf[base + k] = obuf[k, me]

    for o in range(n):
        @pl.when(me == o)
        def _():
            cols = slice(bases[o] * chunk, (bases[o] + counts[o]) * chunk)
            for d in range(n):
                if d != o:
                    stat_own(o, d).start()
            gown[:, cols] = sown[:, cols]

    @pl.loop(0, most)
    def _(step):
        for o in range(n):
            k = step * counts[o] // most

            @pl.when((step + 1) * counts[o] // most > k)
            def _(o=o, k=k):
                c = bases[o] + k

                @pl.when(me == 0)
                def _():
                    if o:
                        got_pair(c).wait_recv()
                    for g in range(2):
                        both = hbuf[c, 1 + g].astype(F32) + lbuf[c, g].astype(F32)
                        hbuf[c, 1 + g] = both.astype(BF16)

                @pl.when(jnp.logical_and(me != 0, me != o))
                def _():
                    got_all(c).wait_recv()

                cols = lanes_of(c)
                conv = hbuf[c, 0].astype(F32)
                adjoint = hbuf[c, 1].astype(F32)
                corr = hbuf[c, 2].astype(F32)
                mixed = sbuf[c, 0].astype(F32)
                pulled = sbuf[c, 2].astype(F32)
                skip = skip_ref[:, cols]
                oq_ref[:, cols] = (
                    go_ref[:, cols].astype(F32) * (conv + skip * mixed)
                ).astype(BF16)
                mixed_grad = adjoint + skip * pulled
                pbuf[c] = (mixed_grad * gk_ref[:, cols].astype(F32)).astype(BF16)

                @pl.when(sec > 0)
                def _():
                    pass_copy(c).start()

                ok_ref[:, cols] = (mixed_grad * vi_ref[:, cols].astype(F32)).astype(BF16)
                envelope = jnp.exp(-rate_ref[:, cols] * when)
                of_ref[:, cols] = (corr * envelope).astype(BF16)

    @pl.when(me != 0)
    def _():
        stat_local(1).wait_recv()

    for o in range(n):
        @pl.when(me != o)
        def _():
            stat_own(o, 0).wait_recv()
    orate_ref[...] = gown[0:1, :] + gloc[0:1, :]
    oskip_ref[...] = gown[1:2, :] + gloc[1:2, :]

    for d in range(1, n):
        @pl.when(me == 0)
        def _():
            stat_local(d).wait_send()
    for o in range(n):
        @pl.when(me == o)
        def _():
            for d in range(n):
                if d != o:
                    stat_own(o, d).wait_send()

    @pl.loop(0, most)
    def _(k):
        for o in range(n):
            @pl.when(k < counts[o])
            def _():
                if o:
                    @pl.when(me == 0)
                    def _():
                        give_pair(o, k).wait_send()

                @pl.when(jnp.logical_and(me != 0, me != o))
                def _():
                    give_all(o, k).wait_send()

    @pl.loop(0, own)
    def _(k):
        @pl.when(me != 0)
        def _():
            back_pair(k).wait_send()

        for m in range(1, n):
            @pl.when(me != m)
            def _():
                back_all(k, m).wait_send()

    @pl.when(me == 0)
    def _():
        for i in range(rin):
            forward_in(i).wait_send()

        @pl.loop(0, rout)
        def _(k):
            forward_out(k).wait_send()

    @pl.loop(0, chunks)
    def _(c):
        @pl.when(sec > 0)
        def _():
            pass_copy(c).wait_send()

        @pl.when(sec < nsec - 1)
        def _():
            pass_copy(c).wait_recv()


def quad_call(nsec, shapes, chunk, args, decay_rate, skip_gain):
    rows, channels = shapes[0].shape
    chunks = channels // chunk
    counts, _, rin, rout = split(chunks)
    most = max(counts)
    tables = (*make_tables(4, rows), *make_local_tables(rows))
    tables = tuple(jnp.asarray(table, BF16) for table in tables)
    dma = pltpu.SemaphoreType.DMA
    block = pltpu.VMEM((rows, channels), BF16)
    row = pltpu.VMEM((1, channels), F32)
    stat = pltpu.VMEM((2, channels), F32)
    return pl.pallas_call(
        functools.partial(quad_kernel, nsec, chunk),
        out_shape=tuple(pltpu.VMEM(shape.shape, shape.dtype) for shape in shapes),
        in_specs=[pl.BlockSpec(memory_space=pl.ANY)] * 11,
        out_specs=(pl.BlockSpec(memory_space=pltpu.VMEM),) * 6,
        scratch_shapes=[
            *([block] * 5), row, row, *(pltpu.VMEM(table.shape, BF16) for table in tables),
            dma((5, 2, 4)), dma((6,)),
            pltpu.VMEM((chunks, 3, rows, chunk), BF16),
            pltpu.VMEM((most, 4, 3, rows, chunk), BF16),
            pltpu.VMEM((most, 4, 3, rows, chunk), BF16),
            pltpu.VMEM((chunks, 3, rows, chunk), BF16),
            pltpu.VMEM((chunks, rows, chunk), BF16),
            pltpu.VMEM((chunks, 2, rows, chunk), BF16),
            pltpu.VMEM((max(rin, 1), 3, rows, chunk), BF16),
            pltpu.VMEM((rout, 3, rows, chunk), BF16),
            pltpu.VMEM((4, 2 * rows, 3 * chunk), BF16),
            pltpu.VMEM((4, 2 * rows, 3 * chunk), F32),
            stat, stat, stat, stat,
            dma((chunks,)), dma((most, 4)), dma((max(rin, 1),)), dma((max(rin, 1),)),
            dma((most, 4)), dma((chunks,)), dma((rout,)), dma((rout,)),
            dma((chunks,)), dma((chunks,)), dma((2, 4)), dma((2, 4)),
        ],
        compiler_params=pltpu.CompilerParams(
            collective_id=0, has_side_effects=True, vmem_limit_bytes=58 * 1024 * 1024
        ),
        name="hyena_backward_quad",
    )(*args, decay_rate, skip_gain, *tables)


def finish(*refs):
    count = (len(refs) - 1) // 2
    sem = refs[-1]
    copies = [
        pltpu.make_async_copy(refs[g], refs[count + g], sem.at[g]) for g in range(count)
    ]
    for copy in copies:
        copy.start()
    for copy in copies:
        copy.wait()


def general_call(n, nsec, shapes, chunk, args, decay_rate, skip_gain):
    rows, channels = shapes[0].shape
    width = channels // n
    steps = width // chunk
    fwd, inv = make_tables(n, rows)
    fwd, inv = jnp.asarray(fwd, BF16), jnp.asarray(inv, BF16)
    message = (steps, n, rows, 3 * chunk)
    dma = pltpu.SemaphoreType.DMA
    anywhere = pl.BlockSpec(memory_space=pl.ANY)
    inside = pl.BlockSpec(memory_space=pltpu.VMEM)
    return pl.pallas_call(
        functools.partial(kernel, n, nsec, chunk, steps),
        out_shape=tuple(pltpu.VMEM(shape.shape, shape.dtype) for shape in shapes),
        in_specs=[anywhere] * 9,
        out_specs=(inside,) * 6,
        scratch_shapes=[
            *([pltpu.VMEM((rows, channels), BF16)] * 5),
            *([pltpu.VMEM((1, channels), F32)] * 2),
            *([pltpu.VMEM(fwd.shape, BF16)] * 2),
            dma((5, 2, n)), dma((4,)),
            pltpu.VMEM(message, BF16),
            pltpu.VMEM(message, BF16),
            pltpu.VMEM(message, BF16),
            pltpu.VMEM(message, BF16),
            pltpu.VMEM((steps, n, rows, chunk), BF16),
            pltpu.VMEM((n, 2 * rows, 3 * chunk), BF16),
            pltpu.VMEM((n, 2 * rows, 3 * chunk), F32),
            pltpu.VMEM((2, width), F32),
            pltpu.VMEM((n, 2, width), F32),
            dma((steps, n)), dma((steps, n)), dma((steps, n)), dma((steps, n)),
            dma((steps, n)), dma((steps, n)), dma((n,)), dma((n,)),
        ],
        compiler_params=pltpu.CompilerParams(
            collective_id=0, has_side_effects=True, vmem_limit_bytes=58 * 1024 * 1024
        ),
        name="hyena_backward",
    )(
        *args, decay_rate, skip_gain, fwd, inv,
    )


def shards(n, nsec, gate_q, gate_k, value_in, filter_raw, decay_rate, skip_gain, grad_out):
    rows, channels = gate_q.shape[1:]
    block = jax.ShapeDtypeStruct((rows, channels), BF16)
    row = jax.ShapeDtypeStruct((1, channels), F32)
    dma = pltpu.SemaphoreType.DMA
    anywhere = pl.BlockSpec(memory_space=pl.ANY)
    inside = pl.BlockSpec(memory_space=pltpu.VMEM)
    shapes = (block, block, block, block, row, row)
    args = (gate_q[0], gate_k[0], value_in[0], filter_raw[0], grad_out[0])
    call = quad_call if n == 4 and channels >= 16 * 128 else functools.partial(general_call, n)
    outs = call(nsec, shapes, 128, args, decay_rate, skip_gain)
    oq, ok, op, of, orate, oskip = pl.pallas_call(
        finish,
        out_shape=shapes,
        in_specs=[inside] * 6,
        out_specs=(anywhere,) * 6,
        scratch_shapes=[dma((6,))],
        compiler_params=pltpu.CompilerParams(vmem_limit_bytes=4 * 1024 * 1024),
        name="hand_over",
    )(*(pltpu.with_memory_space_constraint(out, pltpu.VMEM) for out in outs))
    return oq[None], ok[None], op[None], of[None], orate, oskip


def solution(mesh):
    n, nsec = mesh.shape["ctx"], mesh.shape["section"]
    tokens = P("section", "ctx", None)
    return jax.shard_map(
        functools.partial(shards, n, nsec),
        mesh=mesh,
        in_specs=(tokens, tokens, tokens, tokens, P("section", None), P("section", None), tokens),
        out_specs=(tokens, tokens, tokens, tokens, P("section", None), P("section", None)),
        check_vma=False,
    )
```

```python
import functools
import math

import jax
import jax.numpy as jnp
import numpy as np
from jax import lax
from jax.experimental import pallas as pl
from jax.experimental.pallas import tpu as pltpu
from jax.sharding import PartitionSpec as P

MESH = pl.DeviceIdType.MESH
F32 = jnp.float32
BF16 = jnp.bfloat16


def make_tables(n, rows):
    length = 2 * n * rows
    half = rows // 2
    j = np.arange(rows)[None, :]
    b = np.arange(rows)[:, None]

    def angle(a):
        return 2.0 * np.pi * ((j * (a + 2 * n * b)) % length) / length

    fwd = np.zeros((n, 2 * rows, 2 * rows))
    inv = np.zeros((n, 2 * rows, 2 * rows))
    for a in range(1, n):
        c, s = np.cos(angle(a)), np.sin(angle(a))
        fwd[a] = np.block([[c, s], [-s, c]])
        inv[a] = np.block([[c.T, -s.T], [s.T, c.T]]) * (2.0 / length)
    for slot, a in ((0, 0), (1, n)):
        c, s = np.cos(angle(a))[:half], np.sin(angle(a))[:half]
        weight = np.full((half, 1), 2.0 / length)
        re_rows = slice(slot * half, (slot + 1) * half)
        im_rows = slice(rows + slot * half, rows + (slot + 1) * half)
        cols = slice(slot * rows, (slot + 1) * rows)
        im = -s
        if slot == 0:
            im = im.copy()
            im[0] = np.cos(np.pi * np.arange(rows))
            weight[0] = 1.0 / length
        fwd[0, re_rows, cols] = c
        fwd[0, im_rows, cols] = im
        inv[0, cols, re_rows] = (c * weight).T
        inv[0, cols, im_rows] = (im * weight).T
    return fwd, inv


def scaled(coef, x):
    if abs(coef - 1.0) < 1e-12:
        return x
    if abs(coef + 1.0) < 1e-12:
        return -x
    return x * np.float32(coef)


def combine(terms, zero):
    total = None
    for coef, x in terms:
        if abs(coef) < 1e-12:
            continue
        if total is None:
            total = scaled(coef, x)
        elif coef < 0:
            total = total - scaled(-coef, x)
        else:
            total = total + scaled(coef, x)
    return zero if total is None else total


def kernel(
    n, nsec, chunk, steps,
    gq_hbm, gk_hbm, vi_hbm, fr_hbm, go_hbm, rate_hbm, skip_hbm, fwd_hbm, inv_hbm,
    oq_ref, ok_ref, op_ref, of_ref, orate_ref, oskip_ref,
    gq_ref, gk_ref, vi_ref, fr_ref, go_ref, rate_ref, skip_ref, fwd_ref, inv_ref,
    in_sem, row_sem,
    sbuf, rbuf, obuf, hbuf, pbuf, part, fold, sstat, gstat,
    s_send, s_recv, o_send, o_recv, p_send, p_recv, t_send, t_recv,
):
    rows = gq_ref.shape[0]
    width = chunk * steps
    seq = rows * n
    me = lax.axis_index("ctx")
    sec = lax.axis_index("section")
    before = lax.rem(sec + nsec - 1, nsec)
    after = lax.rem(sec + 1, nsec)

    def columns(owner, k):
        return pl.ds(pl.multiple_of(owner * width + k * chunk, chunk), chunk)

    tokens = (
        (gk_hbm, gk_ref), (vi_hbm, vi_ref), (gq_hbm, gq_ref), (go_hbm, go_ref), (fr_hbm, fr_ref)
    )
    whole = (
        (rate_hbm, rate_ref), (skip_hbm, skip_ref), (fwd_hbm, fwd_ref), (inv_hbm, inv_ref)
    )

    def load_first(g, d):
        hbm, ref = tokens[g]
        return pltpu.make_async_copy(
            hbm.at[:, columns(d, 0)], ref.at[:, columns(d, 0)], in_sem.at[g, 0, d]
        )

    def load_rest(g, d):
        hbm, ref = tokens[g]
        cols = pl.ds(pl.multiple_of(d * width + chunk, chunk), width - chunk)
        return pltpu.make_async_copy(hbm.at[:, cols], ref.at[:, cols], in_sem.at[g, 1, d])

    def load_whole(g):
        return pltpu.make_async_copy(whole[g][0], whole[g][1], row_sem.at[g])

    load_whole(0).start()
    for o in range(n):
        for g in range(5):
            load_first(g, lax.rem(me + 1 + o, n)).start()
    if steps > 1:
        for d in range(n):
            for g in range(5):
                load_rest(g, d).start()
    for g in range(1, 4):
        load_whole(g).start()

    barrier = pltpu.get_barrier_semaphore()
    for o in range(1, n):
        pl.semaphore_signal(
            barrier, inc=1, device_id={"ctx": lax.rem(me + o, n)}, device_id_type=MESH
        )
    for other in (before, after):
        pl.semaphore_signal(barrier, inc=1, device_id={"section": other}, device_id_type=MESH)
    pl.semaphore_wait(barrier, n + 1)
    load_whole(0).wait()

    def here(row0, count):
        row = lax.broadcasted_iota(jnp.int32, (count, 1), 0) + (row0 + me * rows)
        return row.astype(F32) * np.float32(1.0 / seq)

    def send_in(k, d):
        return pltpu.make_async_remote_copy(
            src_ref=sbuf.at[k, d], dst_ref=rbuf.at[k, me], send_sem=s_send.at[k, d],
            recv_sem=s_recv.at[k, me], device_id={"ctx": d}, device_id_type=MESH,
        )

    def got_in(k, m):
        return pltpu.make_async_remote_copy(
            src_ref=sbuf.at[k, m], dst_ref=rbuf.at[k, m], send_sem=s_send.at[k, m],
            recv_sem=s_recv.at[k, m], device_id={"ctx": m}, device_id_type=MESH,
        )

    def send_out(k, m):
        return pltpu.make_async_remote_copy(
            src_ref=obuf.at[k, m], dst_ref=hbuf.at[k, me], send_sem=o_send.at[k, m],
            recv_sem=o_recv.at[k, me], device_id={"ctx": m}, device_id_type=MESH,
        )

    def got_out(k, m):
        return pltpu.make_async_remote_copy(
            src_ref=obuf.at[k, m], dst_ref=hbuf.at[k, m], send_sem=o_send.at[k, m],
            recv_sem=o_recv.at[k, m], device_id={"ctx": m}, device_id_type=MESH,
        )

    def send_stat(d):
        return pltpu.make_async_remote_copy(
            src_ref=sstat, dst_ref=gstat.at[me], send_sem=t_send.at[d],
            recv_sem=t_recv.at[me], device_id={"ctx": d}, device_id_type=MESH,
        )

    def got_stat(m):
        return pltpu.make_async_remote_copy(
            src_ref=sstat, dst_ref=gstat.at[m], send_sem=t_send.at[m],
            recv_sem=t_recv.at[m], device_id={"ctx": m}, device_id_type=MESH,
        )

    def pass_copy(k, m):
        return pltpu.make_async_remote_copy(
            src_ref=pbuf.at[k, m], dst_ref=op_ref.at[:, columns(m, k)], send_sem=p_send.at[k, m],
            recv_sem=p_recv.at[k, m], device_id={"section": before}, device_id_type=MESH,
        )

    @pl.loop(0, steps * n)
    def _(i):
        k, o = i // n, lax.rem(i, n)
        d = lax.rem(me + 1 + o, n)
        cols = columns(d, k)

        @pl.when(k == 0)
        def _():
            for g in range(5):
                load_first(g, d).wait()

        if steps > 1:
            @pl.when(k == 1)
            def _():
                for g in range(5):
                    load_rest(g, d).wait()

        mixed = (gk_ref[:, cols].astype(F32) * vi_ref[:, cols].astype(F32)).astype(BF16)
        pulled = (gq_ref[:, cols].astype(F32) * go_ref[:, cols].astype(F32)).astype(BF16)
        envelope = jnp.exp(-rate_ref[:, cols] * here(0, rows))
        filt = (fr_ref[:, cols].astype(F32) * envelope).astype(BF16)
        sbuf[k, d, :, 0:chunk] = mixed
        sbuf[k, d, :, chunk:2 * chunk] = filt
        sbuf[k, d, :, 2 * chunk:3 * chunk] = pulled

        @pl.when(o < n - 1)
        def _():
            send_in(k, d).start()

        @pl.when(o == n - 1)
        def _():
            rbuf[k, me, :, 0:chunk] = mixed
            rbuf[k, me, :, chunk:2 * chunk] = filt
            rbuf[k, me, :, 2 * chunk:3 * chunk] = pulled

    @pl.when(sec == nsec - 1)
    def _():
        op_ref[...] = jnp.zeros_like(op_ref)

    for g in range(1, 4):
        load_whole(g).wait()

    tile = 16
    top = lax.broadcasted_iota(jnp.int32, (rows, 1), 0)

    @pl.loop(0, steps)
    def _(k):
        @pl.loop(0, n - 1)
        def _(o):
            got_in(k, lax.rem(me + 1 + o, n)).wait_recv()

        @pl.loop(0, rows // tile)
        def _(t):
            at = pl.ds(pl.multiple_of(t * tile, tile), tile)
            low = pl.ds(pl.multiple_of(rows + t * tile, tile), tile)
            for g in range(3):
                lanes = slice(g * chunk, (g + 1) * chunk)
                x = [rbuf[k, m, at, lanes].astype(F32) for m in range(n)]
                zero = jnp.zeros_like(x[0])
                even = combine([(1.0, x[m]) for m in range(0, n, 2)], zero)
                odd = combine([(1.0, x[m]) for m in range(1, n, 2)], zero)
                part[0, at, lanes] = (even + odd).astype(BF16)
                part[0, low, lanes] = (even - odd).astype(BF16)
                for a in range(1, n // 2 + 1):
                    cos = [math.cos(math.pi * m * a / n) for m in range(n)]
                    sin = [math.sin(math.pi * m * a / n) for m in range(n)]
                    ce = combine([(cos[m], x[m]) for m in range(0, n, 2)], zero)
                    co = combine([(cos[m], x[m]) for m in range(1, n, 2)], zero)
                    se = combine([(sin[m], x[m]) for m in range(0, n, 2)], zero)
                    so = combine([(sin[m], x[m]) for m in range(1, n, 2)], zero)
                    part[a, at, lanes] = (ce + co).astype(BF16)
                    part[a, low, lanes] = (-se - so).astype(BF16)
                    if n - a != a:
                        part[n - a, at, lanes] = (ce - co).astype(BF16)
                        part[n - a, low, lanes] = (se - so).astype(BF16)

        @pl.loop(0, n)
        def _(a):
            spec = jnp.dot(fwd_ref[a], part[a], preferred_element_type=F32)
            mr, fr, pr = (spec[:rows, g * chunk:(g + 1) * chunk] for g in range(3))
            mi, fi, pi = (spec[rows:, g * chunk:(g + 1) * chunk] for g in range(3))
            real_pair = jnp.logical_and(top == 0, a == 0)

            def product(ar, ai, br, bi, sign):
                cross = ai * bi
                re = ar * br + jnp.where(real_pair, 0.0, sign * cross)
                im = jnp.where(real_pair, cross, ar * bi - sign * ai * br)
                return re, im

            outs = (
                product(fr, fi, mr, mi, -1.0),
                product(fr, fi, pr, pi, 1.0),
                product(mr, mi, pr, pi, 1.0),
            )
            for g in range(3):
                lanes = slice(g * chunk, (g + 1) * chunk)
                part[a, 0:rows, lanes] = outs[g][0].astype(BF16)
                part[a, rows:2 * rows, lanes] = outs[g][1].astype(BF16)
            fold[a] = jnp.dot(inv_ref[a], part[a], preferred_element_type=F32)

        def unfold(t, carry):
            rate_sum, skip_sum = carry
            at = pl.ds(pl.multiple_of(t * tile, tile), tile)
            low = pl.ds(pl.multiple_of(rows + t * tile, tile), tile)
            for g in range(3):
                lanes = slice(g * chunk, (g + 1) * chunk)
                re = [fold[a, at, lanes] for a in range(n)]
                im = [fold[a, low, lanes] for a in range(n)]
                zero = jnp.zeros_like(re[0])
                for m in range(n):
                    terms = [(1.0, re[0]), ((-1.0) ** m, im[0])]
                    for a in range(1, n):
                        terms.append((math.cos(math.pi * m * a / n), re[a]))
                        terms.append((-math.sin(math.pi * m * a / n), im[a]))
                    value = combine(terms, zero).astype(BF16)
                    obuf[k, m, at, lanes] = value
                    if g == 2:
                        when = lax.broadcasted_iota(jnp.int32, (tile, 1), 0) + (t * tile + m * rows)
                        when = when.astype(F32) * np.float32(1.0 / seq)
                        mixed = rbuf[k, m, at, 0:chunk].astype(F32)
                        filt = rbuf[k, m, at, chunk:2 * chunk].astype(F32)
                        pulled = rbuf[k, m, at, 2 * chunk:3 * chunk].astype(F32)
                        rate_sum = rate_sum + when * value.astype(F32) * filt
                        skip_sum = skip_sum + mixed * pulled
            return rate_sum, skip_sum

        start = jnp.zeros((tile, chunk), F32)
        rate_sum, skip_sum = lax.fori_loop(0, rows // tile, unfold, (start, start))
        mine = pl.ds(pl.multiple_of(k * chunk, chunk), chunk)
        sstat[0:1, mine] = -jnp.sum(rate_sum, axis=0, keepdims=True)
        sstat[1:2, mine] = jnp.sum(skip_sum, axis=0, keepdims=True)

        @pl.loop(0, n - 1)
        def _(o):
            send_out(k, lax.rem(me + 1 + o, n)).start()

        hbuf[k, me] = obuf[k, me]

    for o in range(1, n):
        send_stat(lax.rem(me + o, n)).start()
    gstat[me] = sstat[...]

    @pl.loop(0, steps * n)
    def _(i):
        k, o = i // n, lax.rem(i, n)
        m = lax.rem(me + o, n)

        @pl.when(o > 0)
        def _():
            got_out(k, m).wait_recv()

        cols = columns(m, k)
        conv = hbuf[k, m, :, 0:chunk].astype(F32)
        adjoint = hbuf[k, m, :, chunk:2 * chunk].astype(F32)
        corr = hbuf[k, m, :, 2 * chunk:3 * chunk].astype(F32)
        mixed = sbuf[k, m, :, 0:chunk].astype(F32)
        pulled = sbuf[k, m, :, 2 * chunk:3 * chunk].astype(F32)
        skip = skip_ref[:, cols]
        oq_ref[:, cols] = (go_ref[:, cols].astype(F32) * (conv + skip * mixed)).astype(BF16)
        mixed_grad = adjoint + skip * pulled
        pbuf[k, m] = (mixed_grad * gk_ref[:, cols].astype(F32)).astype(BF16)

        @pl.when(sec > 0)
        def _():
            pass_copy(k, m).start()

        ok_ref[:, cols] = (mixed_grad * vi_ref[:, cols].astype(F32)).astype(BF16)
        envelope = jnp.exp(-rate_ref[:, cols] * here(0, rows))
        of_ref[:, cols] = (corr * envelope).astype(BF16)

    for o in range(1, n):
        got_stat(lax.rem(me + o, n)).wait_recv()
    for m in range(n):
        orate_ref[:, m * width:(m + 1) * width] = gstat[m, 0:1, :]
        oskip_ref[:, m * width:(m + 1) * width] = gstat[m, 1:2, :]

    for o in range(1, n):
        send_stat(lax.rem(me + o, n)).wait_send()

    @pl.loop(0, steps * (n - 1))
    def _(i):
        k, o = i // (n - 1), lax.rem(i, n - 1)
        d = lax.rem(me + 1 + o, n)
        send_in(k, d).wait_send()
        send_out(k, d).wait_send()

    @pl.loop(0, steps * n)
    def _(i):
        k, m = i // n, lax.rem(i, n)

        @pl.when(sec > 0)
        def _():
            pass_copy(k, m).wait_send()

        @pl.when(sec < nsec - 1)
        def _():
            pass_copy(k, m).wait_recv()


def make_local_tables(rows):
    length = 2 * rows
    j = np.arange(rows)[None, :]
    b = np.arange(rows)[:, None]
    angle = 2.0 * np.pi * ((j * b) % length) / length
    re, im = np.cos(angle), -np.sin(angle)
    im[0] = np.cos(np.pi * np.arange(rows))
    weight = np.full((rows, 1), 2.0 / length)
    weight[0] = 1.0 / length
    return np.concatenate([re, im]), np.concatenate([re * weight, im * weight]).T


def split(chunks):
    zero, first = chunks * 6 // 32, chunks // 4
    third = (chunks - zero - first) // 2
    counts = (zero, first, chunks - zero - first - third, third)
    bases = tuple(sum(counts[:o]) for o in range(4))
    return counts, bases, chunks // 16, chunks // 8


def quad_kernel(
    nsec, chunk,
    gq_hbm, gk_hbm, vi_hbm, fr_hbm, go_hbm, rate_hbm, skip_hbm, fwd_hbm, inv_hbm, fwdl_hbm, invl_hbm,
    oq_ref, ok_ref, op_ref, of_ref, orate_ref, oskip_ref,
    gq_ref, gk_ref, vi_ref, fr_ref, go_ref, rate_ref, skip_ref, fwd_ref, inv_ref, fwdl_ref, invl_ref,
    in_sem, row_sem,
    sbuf, rbuf, obuf, hbuf, pbuf, lbuf, relin, relout, part, fold, sown, sloc, gown, gloc,
    i_send, i_recv, ri_send, ri_recv, o_send, o_recv, ro_send, ro_recv, p_send, p_recv,
    t_send, t_recv,
):
    n = 4
    rows, channels = gq_ref.shape
    chunks = channels // chunk
    counts, bases, rin, rout = split(chunks)
    most = max(counts)
    seq = rows * n
    me = lax.axis_index("ctx")
    sec = lax.axis_index("section")
    before = lax.rem(sec + nsec - 1, nsec)
    after = lax.rem(sec + 1, nsec)
    is1 = me * (3 - me) * (2 - me) // 2
    is2 = me * (3 - me) * (me - 1) // 2
    is3 = me * (me - 1) * (me - 2) // 6
    is0 = 1 - is1 - is2 - is3
    own = is0 * counts[0] + is1 * counts[1] + is2 * counts[2] + is3 * counts[3]
    base = is1 * bases[1] + is2 * bases[2] + is3 * bases[3]

    def lanes_of(c):
        return pl.ds(pl.multiple_of(c * chunk, chunk), chunk)

    tokens = (
        (gk_hbm, gk_ref), (vi_hbm, vi_ref), (gq_hbm, gq_ref), (go_hbm, go_ref), (fr_hbm, fr_ref)
    )
    whole = (
        (rate_hbm, rate_ref), (skip_hbm, skip_ref), (fwd_hbm, fwd_ref), (inv_hbm, inv_ref),
        (fwdl_hbm, fwdl_ref), (invl_hbm, invl_ref),
    )

    def load(g, o, rest):
        hbm, ref = tokens[g]
        lo = bases[o] + rest
        hi = bases[o] + counts[o] if rest else lo + 1
        cols = slice(lo * chunk, hi * chunk)
        return pltpu.make_async_copy(hbm.at[:, cols], ref.at[:, cols], in_sem.at[g, rest, o])

    def load_whole(g):
        return pltpu.make_async_copy(whole[g][0], whole[g][1], row_sem.at[g])

    load_whole(0).start()
    for rest in range(2):
        for o in range(n):
            for g in range(5):
                load(g, o, rest).start()
    for g in range(1, 6):
        load_whole(g).start()

    barrier = pltpu.get_barrier_semaphore()
    for o in range(1, n):
        pl.semaphore_signal(
            barrier, inc=1, device_id={"ctx": lax.rem(me + o, n)}, device_id_type=MESH
        )
    for other in (before, after):
        pl.semaphore_signal(barrier, inc=1, device_id={"section": other}, device_id_type=MESH)
    pl.semaphore_wait(barrier, n + 1)
    load_whole(0).wait()

    def to(d):
        return {"ctx": jnp.int32(d)}

    def remote(src, dst, send, recv, where):
        return pltpu.make_async_remote_copy(
            src_ref=src, dst_ref=dst, send_sem=send, recv_sem=recv,
            device_id=where, device_id_type=MESH,
        )

    def give_pair(o, k):
        c = bases[o] + k
        return remote(
            sbuf.at[c, 0:2], rbuf.at[k, 0, 0:2], i_send.at[c], i_recv.at[k, 0], to(o)
        )

    def give_all(o, k):
        c = bases[o] + k
        return remote(sbuf.at[c], rbuf.at[k, me], i_send.at[c], i_recv.at[k, me], to(o))

    def give_relay(k):
        c = bases[1] + k
        return remote(sbuf.at[c], relin.at[k], i_send.at[c], ri_recv.at[k], to(0))

    def forward_in(i):
        return remote(
            relin.at[i], rbuf.at[i, 2], ri_send.at[i], i_recv.at[i, 2], to(1)
        )

    def got_in(k, s):
        at = rbuf.at[k, 0, 0:2] if s == 0 else rbuf.at[k, s]
        src = sbuf.at[0, 0:2] if s == 0 else sbuf.at[0]
        return remote(src, at, i_send.at[0], i_recv.at[k, s], to(s))

    def back_first(k, m):
        return remote(
            obuf.at[k, m, 2], hbuf.at[base + k, 2], o_send.at[k, m, 0], o_recv.at[base + k, 0],
            to(m),
        )

    def back_corr(k):
        return remote(
            obuf.at[k, 0, 1], hbuf.at[base + k, 1], o_send.at[k, 0, 1], o_recv.at[base + k, 1],
            to(0),
        )

    def back_rest(k, m):
        return remote(
            obuf.at[k, m, 0:2], hbuf.at[base + k, 0:2], o_send.at[k, m, 1],
            o_recv.at[base + k, 1], to(m),
        )

    def back_relay(i):
        k = counts[2] - rout + i
        return remote(obuf.at[k, 1, 0:2], relout.at[i], o_send.at[k, 1, 1], ro_recv.at[i], to(0))

    def forward_out(i):
        c = bases[2] + counts[2] - rout + i
        return remote(relout.at[i], hbuf.at[c, 0:2], ro_send.at[i], o_recv.at[c, 1], to(1))

    def got_first(c):
        return remote(
            obuf.at[0, 0, 2], hbuf.at[c, 2], o_send.at[0, 0, 0], o_recv.at[c, 0], to(1)
        )

    def got_corr(c):
        return remote(
            obuf.at[0, 0, 1], hbuf.at[c, 1], o_send.at[0, 0, 1], o_recv.at[c, 1], to(1)
        )

    def got_rest(c):
        return remote(
            obuf.at[0, 0, 0:2], hbuf.at[c, 0:2], o_send.at[0, 0, 1], o_recv.at[c, 1], to(1)
        )

    def stat_own(o, d):
        cols = slice(bases[o] * chunk, (bases[o] + counts[o]) * chunk)
        return remote(
            sown.at[:, cols], gown.at[:, cols], t_send.at[0, d], t_recv.at[0, o], to(d)
        )

    def stat_local(d):
        return remote(sloc, gloc, t_send.at[1, d], t_recv.at[1, 0], to(d))

    def pass_copy(c):
        return remote(
            pbuf.at[c], op_ref.at[:, lanes_of(c)], p_send.at[c], p_recv.at[c],
            {"section": before},
        )

    when = lax.broadcasted_iota(jnp.int32, (rows, 1), 0) + me * rows
    when = when.astype(F32) * np.float32(1.0 / seq)

    @pl.loop(0, most)
    def _(step):
        for o in range(n):
            k = step * counts[o] // most

            @pl.when((step + 1) * counts[o] // most > k)
            def _(o=o, k=k):
                for rest in range(2):
                    @pl.when(k == rest)
                    def _():
                        for g in range(5):
                            load(g, o, rest).wait()

                c = bases[o] + k
                cols = lanes_of(c)
                mixed = (gk_ref[:, cols].astype(F32) * vi_ref[:, cols].astype(F32)).astype(BF16)
                pulled = (gq_ref[:, cols].astype(F32) * go_ref[:, cols].astype(F32)).astype(BF16)
                envelope = jnp.exp(-rate_ref[:, cols] * when)
                filt = (fr_ref[:, cols].astype(F32) * envelope).astype(BF16)
                sbuf[c, 0] = mixed
                sbuf[c, 1] = filt
                sbuf[c, 2] = pulled

                @pl.when(me == o)
                def _():
                    rbuf[k, o, 0] = mixed
                    rbuf[k, o, 1] = filt
                    if o:
                        rbuf[k, o, 2] = pulled

                if o:
                    @pl.when(me == 0)
                    def _():
                        give_pair(o, k).start()

                if o == 1:
                    @pl.when(jnp.logical_and(me == 2, k < rin))
                    def _():
                        give_relay(k).start()

                    @pl.when(jnp.logical_or(me == 3, jnp.logical_and(me == 2, k >= rin)))
                    def _():
                        give_all(o, k).start()
                else:
                    @pl.when(jnp.logical_and(me != 0, me != o))
                    def _():
                        give_all(o, k).start()

    @pl.when(sec == nsec - 1)
    def _():
        op_ref[...] = jnp.zeros_like(op_ref)

    for g in range(1, 6):
        load_whole(g).wait()

    tile = 16
    top = lax.broadcasted_iota(jnp.int32, (rows, 1), 0)

    def product(real_pair, ar, ai, br, bi, sign):
        cross = ai * bi
        re = ar * br + jnp.where(real_pair, 0.0, sign * cross)
        im = jnp.where(real_pair, cross, ar * bi - sign * ai * br)
        return re, im

    def products(spec, real_pair):
        mr, fr, pr = (spec[:rows, g * chunk:(g + 1) * chunk] for g in range(3))
        mi, fi, pi = (spec[rows:, g * chunk:(g + 1) * chunk] for g in range(3))
        return (
            product(real_pair, fr, fi, mr, mi, -1.0),
            product(real_pair, fr, fi, pr, pi, 1.0),
            product(real_pair, mr, mi, pr, pi, 1.0),
        )

    @pl.when(me == 0)
    def _():
        @pl.loop(0, chunks)
        def _(c):
            if rin:
                @pl.when(c < rin)
                def _():
                    give_relay(c).wait_recv()
                    forward_in(c).start()

            for g in range(3):
                part[0, 0:rows, g * chunk:(g + 1) * chunk] = sbuf[c, g]
            spec = jnp.dot(fwdl_ref[...], part[0, 0:rows, :], preferred_element_type=F32)
            outs = products(spec, top == 0)
            for g in range(3):
                lanes = slice(g * chunk, (g + 1) * chunk)
                part[1, 0:rows, lanes] = outs[g][0].astype(BF16)
                part[1, rows:2 * rows, lanes] = outs[g][1].astype(BF16)
            back = jnp.dot(invl_ref[...], part[1], preferred_element_type=F32).astype(BF16)
            corr = back[:, 2 * chunk:3 * chunk]
            hbuf[c, 0] = back[:, 0:chunk]
            lbuf[c, 0] = back[:, chunk:2 * chunk]
            lbuf[c, 1] = corr
            rate = when * corr.astype(F32) * sbuf[c, 1].astype(F32)
            skip = sbuf[c, 0].astype(F32) * sbuf[c, 2].astype(F32)
            cols = lanes_of(c)
            sloc[0:1, cols] = -jnp.sum(rate, axis=0, keepdims=True)
            sloc[1:2, cols] = jnp.sum(skip, axis=0, keepdims=True)

        for d in range(1, n):
            stat_local(d).start()
        gloc[...] = sloc[...]

    @pl.loop(0, own)
    def _(k):
        for s in range(n):
            @pl.when(me != s)
            def _():
                got_in(k, s).wait_recv()

        @pl.loop(0, rows // tile)
        def _(t):
            at = pl.ds(pl.multiple_of(t * tile, tile), tile)
            low = pl.ds(pl.multiple_of(rows + t * tile, tile), tile)
            for g in range(3):
                lanes = slice(g * chunk, (g + 1) * chunk)
                held = range(1, n) if g == 2 else range(n)
                x = {m: rbuf[k, m, g, at, :].astype(F32) for m in held}
                even = [m for m in held if m % 2 == 0]
                odd = [m for m in held if m % 2 == 1]
                zero = jnp.zeros_like(x[1])
                e = combine([(1.0, x[m]) for m in even], zero)
                d = combine([(1.0, x[m]) for m in odd], zero)
                part[0, at, lanes] = (e + d).astype(BF16)
                part[0, low, lanes] = (e - d).astype(BF16)
                for a in range(1, n // 2 + 1):
                    cos = [math.cos(math.pi * m * a / n) for m in range(n)]
                    sin = [math.sin(math.pi * m * a / n) for m in range(n)]
                    ce = combine([(cos[m], x[m]) for m in even], zero)
                    co = combine([(cos[m], x[m]) for m in odd], zero)
                    se = combine([(sin[m], x[m]) for m in even], zero)
                    so = combine([(sin[m], x[m]) for m in odd], zero)
                    part[a, at, lanes] = (ce + co).astype(BF16)
                    part[a, low, lanes] = (-se - so).astype(BF16)
                    if n - a != a:
                        part[n - a, at, lanes] = (ce - co).astype(BF16)
                        part[n - a, low, lanes] = (se - so).astype(BF16)

        @pl.loop(0, n)
        def _(a):
            spec = jnp.dot(fwd_ref[a], part[a], preferred_element_type=F32)
            outs = products(spec, jnp.logical_and(top == 0, a == 0))
            for g in range(3):
                lanes = slice(g * chunk, (g + 1) * chunk)
                part[a, 0:rows, lanes] = outs[g][0].astype(BF16)
                part[a, rows:2 * rows, lanes] = outs[g][1].astype(BF16)
            fold[a] = jnp.dot(inv_ref[a], part[a], preferred_element_type=F32)

        def unfold(t, carry):
            rate_sum, skip_sum = carry
            at = pl.ds(pl.multiple_of(t * tile, tile), tile)
            low = pl.ds(pl.multiple_of(rows + t * tile, tile), tile)
            for g in range(3):
                lanes = slice(g * chunk, (g + 1) * chunk)
                re = [fold[a, at, lanes] for a in range(n)]
                im = [fold[a, low, lanes] for a in range(n)]
                zero = jnp.zeros_like(re[0])
                for m in range(1 if g == 0 else 0, n):
                    terms = [(1.0, re[0]), ((-1.0) ** m, im[0])]
                    for a in range(1, n):
                        terms.append((math.cos(math.pi * m * a / n), re[a]))
                        terms.append((-math.sin(math.pi * m * a / n), im[a]))
                    value = combine(terms, zero).astype(BF16)
                    obuf[k, m, (0, 2, 1)[g], at, :] = value
                    if g == 2:
                        pos = lax.broadcasted_iota(jnp.int32, (tile, 1), 0) + (t * tile + m * rows)
                        pos = pos.astype(F32) * np.float32(1.0 / seq)
                        filt = rbuf[k, m, 1, at, :].astype(F32)
                        rate_sum = rate_sum + pos * value.astype(F32) * filt
                        if m:
                            mixed = rbuf[k, m, 0, at, :].astype(F32)
                            pulled = rbuf[k, m, 2, at, :].astype(F32)
                            skip_sum = skip_sum + mixed * pulled
            return rate_sum, skip_sum

        start = jnp.zeros((tile, chunk), F32)
        rate_sum, skip_sum = lax.fori_loop(0, rows // tile, unfold, (start, start))
        mine = lanes_of(base + k)
        sown[0:1, mine] = -jnp.sum(rate_sum, axis=0, keepdims=True)
        sown[1:2, mine] = jnp.sum(skip_sum, axis=0, keepdims=True)

        for m in range(n):
            @pl.when(me != m)
            def _():
                back_first(k, m).start()

        @pl.when(me == 0)
        def _():
            hbuf[base + k, 1:3] = obuf[k, 0, 1:3]

        @pl.when(me != 0)
        def _():
            hbuf[base + k] = obuf[k, me]

    for o in range(n):
        @pl.when(me == o)
        def _():
            cols = slice(bases[o] * chunk, (bases[o] + counts[o]) * chunk)
            for d in range(n):
                if d != o:
                    stat_own(o, d).start()
            gown[:, cols] = sown[:, cols]

    @pl.when(me == 2)
    def _():
        @pl.loop(0, rout)
        def _(i):
            back_relay(i).start()

    @pl.loop(0, own)
    def _(k):
        @pl.when(me != 0)
        def _():
            back_corr(k).start()

        direct = jnp.logical_or(me != 2, k < counts[2] - rout)

        @pl.when(jnp.logical_and(me != 1, direct))
        def _():
            back_rest(k, 1).start()

        for m in range(2, n):
            @pl.when(me != m)
            def _():
                back_rest(k, m).start()

    @pl.loop(0, most)
    def _(step):
        for o in range(n):
            k = step * counts[o] // most

            @pl.when((step + 1) * counts[o] // most > k)
            def _(o=o, k=k):
                c = bases[o] + k

                @pl.when(me != o)
                def _():
                    got_first(c).wait_recv()

                @pl.when(me == 0)
                def _():
                    both = hbuf[c, 2].astype(F32) + lbuf[c, 0].astype(F32)
                    hbuf[c, 2] = both.astype(BF16)

                cols = lanes_of(c)
                pulled = sbuf[c, 2].astype(F32)
                mixed_grad = hbuf[c, 2].astype(F32) + skip_ref[:, cols] * pulled
                pbuf[c] = (mixed_grad * gk_ref[:, cols].astype(F32)).astype(BF16)

                @pl.when(sec > 0)
                def _():
                    pass_copy(c).start()

                ok_ref[:, cols] = (mixed_grad * vi_ref[:, cols].astype(F32)).astype(BF16)

    @pl.when(me == 0)
    def _():
        @pl.loop(0, rout)
        def _(i):
            back_relay(i).wait_recv()
            forward_out(i).start()

    @pl.loop(0, most)
    def _(step):
        for o in range(n):
            k = step * counts[o] // most

            @pl.when((step + 1) * counts[o] // most > k)
            def _(o=o, k=k):
                c = bases[o] + k

                @pl.when(me == 0)
                def _():
                    if o:
                        got_corr(c).wait_recv()
                    both = hbuf[c, 1].astype(F32) + lbuf[c, 1].astype(F32)
                    hbuf[c, 1] = both.astype(BF16)

                @pl.when(jnp.logical_and(me != 0, me != o))
                def _():
                    got_rest(c).wait_recv()

                cols = lanes_of(c)
                conv = hbuf[c, 0].astype(F32)
                mixed = sbuf[c, 0].astype(F32)
                oq_ref[:, cols] = (
                    go_ref[:, cols].astype(F32) * (conv + skip_ref[:, cols] * mixed)
                ).astype(BF16)
                envelope = jnp.exp(-rate_ref[:, cols] * when)
                of_ref[:, cols] = (hbuf[c, 1].astype(F32) * envelope).astype(BF16)

    @pl.when(me != 0)
    def _():
        stat_local(1).wait_recv()

    for o in range(n):
        @pl.when(me != o)
        def _():
            stat_own(o, 0).wait_recv()
    orate_ref[...] = gown[0:1, :] + gloc[0:1, :]
    oskip_ref[...] = gown[1:2, :] + gloc[1:2, :]

    for d in range(1, n):
        @pl.when(me == 0)
        def _():
            stat_local(d).wait_send()
    for o in range(n):
        @pl.when(me == o)
        def _():
            for d in range(n):
                if d != o:
                    stat_own(o, d).wait_send()

    @pl.loop(0, most)
    def _(k):
        for o in range(n):
            @pl.when(k < counts[o])
            def _():
                if o:
                    @pl.when(me == 0)
                    def _():
                        give_pair(o, k).wait_send()

                @pl.when(jnp.logical_and(me != 0, me != o))
                def _():
                    give_all(o, k).wait_send()

    @pl.loop(0, own)
    def _(k):
        for m in range(n):
            @pl.when(me != m)
            def _():
                back_first(k, m).wait_send()
                (back_rest(k, m) if m else back_corr(k)).wait_send()

    @pl.when(me == 0)
    def _():
        for i in range(rin):
            forward_in(i).wait_send()

        @pl.loop(0, rout)
        def _(k):
            forward_out(k).wait_send()

    @pl.loop(0, chunks)
    def _(c):
        @pl.when(sec > 0)
        def _():
            pass_copy(c).wait_send()

        @pl.when(sec < nsec - 1)
        def _():
            pass_copy(c).wait_recv()


def quad_call(nsec, shapes, chunk, args, decay_rate, skip_gain):
    rows, channels = shapes[0].shape
    chunks = channels // chunk
    counts, _, rin, rout = split(chunks)
    most = max(counts)
    tables = (*make_tables(4, rows), *make_local_tables(rows))
    tables = tuple(jnp.asarray(table, BF16) for table in tables)
    dma = pltpu.SemaphoreType.DMA
    block = pltpu.VMEM((rows, channels), BF16)
    row = pltpu.VMEM((1, channels), F32)
    stat = pltpu.VMEM((2, channels), F32)
    return pl.pallas_call(
        functools.partial(quad_kernel, nsec, chunk),
        out_shape=tuple(pltpu.VMEM(shape.shape, shape.dtype) for shape in shapes),
        in_specs=[pl.BlockSpec(memory_space=pl.ANY)] * 11,
        out_specs=(pl.BlockSpec(memory_space=pltpu.VMEM),) * 6,
        scratch_shapes=[
            *([block] * 5), row, row, *(pltpu.VMEM(table.shape, BF16) for table in tables),
            dma((5, 2, 4)), dma((6,)),
            pltpu.VMEM((chunks, 3, rows, chunk), BF16),
            pltpu.VMEM((most, 4, 3, rows, chunk), BF16),
            pltpu.VMEM((most, 4, 3, rows, chunk), BF16),
            pltpu.VMEM((chunks, 3, rows, chunk), BF16),
            pltpu.VMEM((chunks, rows, chunk), BF16),
            pltpu.VMEM((chunks, 2, rows, chunk), BF16),
            pltpu.VMEM((max(rin, 1), 3, rows, chunk), BF16),
            pltpu.VMEM((rout, 2, rows, chunk), BF16),
            pltpu.VMEM((4, 2 * rows, 3 * chunk), BF16),
            pltpu.VMEM((4, 2 * rows, 3 * chunk), F32),
            stat, stat, stat, stat,
            dma((chunks,)), dma((most, 4)), dma((max(rin, 1),)), dma((max(rin, 1),)),
            dma((most, 4, 2)), dma((chunks, 2)), dma((rout,)), dma((rout,)),
            dma((chunks,)), dma((chunks,)), dma((2, 4)), dma((2, 4)),
        ],
        compiler_params=pltpu.CompilerParams(
            collective_id=0, has_side_effects=True, vmem_limit_bytes=58 * 1024 * 1024
        ),
        name="hyena_backward_quad",
    )(*args, decay_rate, skip_gain, *tables)


def finish(*refs):
    count = (len(refs) - 1) // 2
    sem = refs[-1]
    copies = [
        pltpu.make_async_copy(refs[g], refs[count + g], sem.at[g]) for g in range(count)
    ]
    for copy in copies:
        copy.start()
    for copy in copies:
        copy.wait()


def general_call(n, nsec, shapes, chunk, args, decay_rate, skip_gain):
    rows, channels = shapes[0].shape
    width = channels // n
    steps = width // chunk
    fwd, inv = make_tables(n, rows)
    fwd, inv = jnp.asarray(fwd, BF16), jnp.asarray(inv, BF16)
    message = (steps, n, rows, 3 * chunk)
    dma = pltpu.SemaphoreType.DMA
    anywhere = pl.BlockSpec(memory_space=pl.ANY)
    inside = pl.BlockSpec(memory_space=pltpu.VMEM)
    return pl.pallas_call(
        functools.partial(kernel, n, nsec, chunk, steps),
        out_shape=tuple(pltpu.VMEM(shape.shape, shape.dtype) for shape in shapes),
        in_specs=[anywhere] * 9,
        out_specs=(inside,) * 6,
        scratch_shapes=[
            *([pltpu.VMEM((rows, channels), BF16)] * 5),
            *([pltpu.VMEM((1, channels), F32)] * 2),
            *([pltpu.VMEM(fwd.shape, BF16)] * 2),
            dma((5, 2, n)), dma((4,)),
            pltpu.VMEM(message, BF16),
            pltpu.VMEM(message, BF16),
            pltpu.VMEM(message, BF16),
            pltpu.VMEM(message, BF16),
            pltpu.VMEM((steps, n, rows, chunk), BF16),
            pltpu.VMEM((n, 2 * rows, 3 * chunk), BF16),
            pltpu.VMEM((n, 2 * rows, 3 * chunk), F32),
            pltpu.VMEM((2, width), F32),
            pltpu.VMEM((n, 2, width), F32),
            dma((steps, n)), dma((steps, n)), dma((steps, n)), dma((steps, n)),
            dma((steps, n)), dma((steps, n)), dma((n,)), dma((n,)),
        ],
        compiler_params=pltpu.CompilerParams(
            collective_id=0, has_side_effects=True, vmem_limit_bytes=58 * 1024 * 1024
        ),
        name="hyena_backward",
    )(
        *args, decay_rate, skip_gain, fwd, inv,
    )


def shards(n, nsec, gate_q, gate_k, value_in, filter_raw, decay_rate, skip_gain, grad_out):
    rows, channels = gate_q.shape[1:]
    block = jax.ShapeDtypeStruct((rows, channels), BF16)
    row = jax.ShapeDtypeStruct((1, channels), F32)
    dma = pltpu.SemaphoreType.DMA
    anywhere = pl.BlockSpec(memory_space=pl.ANY)
    inside = pl.BlockSpec(memory_space=pltpu.VMEM)
    shapes = (block, block, block, block, row, row)
    args = (gate_q[0], gate_k[0], value_in[0], filter_raw[0], grad_out[0])
    call = quad_call if n == 4 and channels >= 16 * 128 else functools.partial(general_call, n)
    outs = call(nsec, shapes, 128, args, decay_rate, skip_gain)
    oq, ok, op, of, orate, oskip = pl.pallas_call(
        finish,
        out_shape=shapes,
        in_specs=[inside] * 6,
        out_specs=(anywhere,) * 6,
        scratch_shapes=[dma((6,))],
        compiler_params=pltpu.CompilerParams(vmem_limit_bytes=4 * 1024 * 1024),
        name="hand_over",
    )(*(pltpu.with_memory_space_constraint(out, pltpu.VMEM) for out in outs))
    return oq[None], ok[None], op[None], of[None], orate, oskip


def solution(mesh):
    n, nsec = mesh.shape["ctx"], mesh.shape["section"]
    tokens = P("section", "ctx", None)
    return jax.shard_map(
        functools.partial(shards, n, nsec),
        mesh=mesh,
        in_specs=(tokens, tokens, tokens, tokens, P("section", None), P("section", None), tokens),
        out_specs=(tokens, tokens, tokens, tokens, P("section", None), P("section", None)),
        check_vma=False,
    )
```

```python
import functools
import math

import jax
import jax.numpy as jnp
import numpy as np
from jax import lax
from jax.experimental import pallas as pl
from jax.experimental.pallas import tpu as pltpu
from jax.sharding import PartitionSpec as P

MESH = pl.DeviceIdType.MESH
F32 = jnp.float32
BF16 = jnp.bfloat16


def make_tables(n, rows):
    length = 2 * n * rows
    half = rows // 2
    j = np.arange(rows)[None, :]
    b = np.arange(rows)[:, None]

    def angle(a):
        return 2.0 * np.pi * ((j * (a + 2 * n * b)) % length) / length

    fwd = np.zeros((n, 2 * rows, 2 * rows))
    inv = np.zeros((n, 2 * rows, 2 * rows))
    for a in range(1, n):
        c, s = np.cos(angle(a)), np.sin(angle(a))
        fwd[a] = np.block([[c, s], [-s, c]])
        inv[a] = np.block([[c.T, -s.T], [s.T, c.T]]) * (2.0 / length)
    for slot, a in ((0, 0), (1, n)):
        c, s = np.cos(angle(a))[:half], np.sin(angle(a))[:half]
        weight = np.full((half, 1), 2.0 / length)
        re_rows = slice(slot * half, (slot + 1) * half)
        im_rows = slice(rows + slot * half, rows + (slot + 1) * half)
        cols = slice(slot * rows, (slot + 1) * rows)
        im = -s
        if slot == 0:
            im = im.copy()
            im[0] = np.cos(np.pi * np.arange(rows))
            weight[0] = 1.0 / length
        fwd[0, re_rows, cols] = c
        fwd[0, im_rows, cols] = im
        inv[0, cols, re_rows] = (c * weight).T
        inv[0, cols, im_rows] = (im * weight).T
    return fwd, inv


def scaled(coef, x):
    if abs(coef - 1.0) < 1e-12:
        return x
    if abs(coef + 1.0) < 1e-12:
        return -x
    return x * np.float32(coef)


def combine(terms, zero):
    total = None
    for coef, x in terms:
        if abs(coef) < 1e-12:
            continue
        if total is None:
            total = scaled(coef, x)
        elif coef < 0:
            total = total - scaled(-coef, x)
        else:
            total = total + scaled(coef, x)
    return zero if total is None else total


def kernel(
    n, nsec, chunk, steps,
    gq_hbm, gk_hbm, vi_hbm, fr_hbm, go_hbm, rate_hbm, skip_hbm, fwd_hbm, inv_hbm,
    oq_ref, ok_ref, op_ref, of_ref, orate_ref, oskip_ref,
    gq_ref, gk_ref, vi_ref, fr_ref, go_ref, rate_ref, skip_ref, fwd_ref, inv_ref,
    in_sem, row_sem,
    sbuf, rbuf, obuf, hbuf, pbuf, part, fold, sstat, gstat,
    s_send, s_recv, o_send, o_recv, p_send, p_recv, t_send, t_recv,
):
    rows = gq_ref.shape[0]
    width = chunk * steps
    seq = rows * n
    me = lax.axis_index("ctx")
    sec = lax.axis_index("section")
    before = lax.rem(sec + nsec - 1, nsec)
    after = lax.rem(sec + 1, nsec)

    def columns(owner, k):
        return pl.ds(pl.multiple_of(owner * width + k * chunk, chunk), chunk)

    tokens = (
        (gk_hbm, gk_ref), (vi_hbm, vi_ref), (gq_hbm, gq_ref), (go_hbm, go_ref), (fr_hbm, fr_ref)
    )
    whole = (
        (rate_hbm, rate_ref), (skip_hbm, skip_ref), (fwd_hbm, fwd_ref), (inv_hbm, inv_ref)
    )

    def load_first(g, d):
        hbm, ref = tokens[g]
        return pltpu.make_async_copy(
            hbm.at[:, columns(d, 0)], ref.at[:, columns(d, 0)], in_sem.at[g, 0, d]
        )

    def load_rest(g, d):
        hbm, ref = tokens[g]
        cols = pl.ds(pl.multiple_of(d * width + chunk, chunk), width - chunk)
        return pltpu.make_async_copy(hbm.at[:, cols], ref.at[:, cols], in_sem.at[g, 1, d])

    def load_whole(g):
        return pltpu.make_async_copy(whole[g][0], whole[g][1], row_sem.at[g])

    load_whole(0).start()
    for o in range(n):
        for g in range(5):
            load_first(g, lax.rem(me + 1 + o, n)).start()
    if steps > 1:
        for d in range(n):
            for g in range(5):
                load_rest(g, d).start()
    for g in range(1, 4):
        load_whole(g).start()

    barrier = pltpu.get_barrier_semaphore()
    for o in range(1, n):
        pl.semaphore_signal(
            barrier, inc=1, device_id={"ctx": lax.rem(me + o, n)}, device_id_type=MESH
        )
    for other in (before, after):
        pl.semaphore_signal(barrier, inc=1, device_id={"section": other}, device_id_type=MESH)
    pl.semaphore_wait(barrier, n + 1)
    load_whole(0).wait()

    def here(row0, count):
        row = lax.broadcasted_iota(jnp.int32, (count, 1), 0) + (row0 + me * rows)
        return row.astype(F32) * np.float32(1.0 / seq)

    def send_in(k, d):
        return pltpu.make_async_remote_copy(
            src_ref=sbuf.at[k, d], dst_ref=rbuf.at[k, me], send_sem=s_send.at[k, d],
            recv_sem=s_recv.at[k, me], device_id={"ctx": d}, device_id_type=MESH,
        )

    def got_in(k, m):
        return pltpu.make_async_remote_copy(
            src_ref=sbuf.at[k, m], dst_ref=rbuf.at[k, m], send_sem=s_send.at[k, m],
            recv_sem=s_recv.at[k, m], device_id={"ctx": m}, device_id_type=MESH,
        )

    def send_out(k, m):
        return pltpu.make_async_remote_copy(
            src_ref=obuf.at[k, m], dst_ref=hbuf.at[k, me], send_sem=o_send.at[k, m],
            recv_sem=o_recv.at[k, me], device_id={"ctx": m}, device_id_type=MESH,
        )

    def got_out(k, m):
        return pltpu.make_async_remote_copy(
            src_ref=obuf.at[k, m], dst_ref=hbuf.at[k, m], send_sem=o_send.at[k, m],
            recv_sem=o_recv.at[k, m], device_id={"ctx": m}, device_id_type=MESH,
        )

    def send_stat(d):
        return pltpu.make_async_remote_copy(
            src_ref=sstat, dst_ref=gstat.at[me], send_sem=t_send.at[d],
            recv_sem=t_recv.at[me], device_id={"ctx": d}, device_id_type=MESH,
        )

    def got_stat(m):
        return pltpu.make_async_remote_copy(
            src_ref=sstat, dst_ref=gstat.at[m], send_sem=t_send.at[m],
            recv_sem=t_recv.at[m], device_id={"ctx": m}, device_id_type=MESH,
        )

    def pass_copy(k, m):
        return pltpu.make_async_remote_copy(
            src_ref=pbuf.at[k, m], dst_ref=op_ref.at[:, columns(m, k)], send_sem=p_send.at[k, m],
            recv_sem=p_recv.at[k, m], device_id={"section": before}, device_id_type=MESH,
        )

    @pl.loop(0, steps * n)
    def _(i):
        k, o = i // n, lax.rem(i, n)
        d = lax.rem(me + 1 + o, n)
        cols = columns(d, k)

        @pl.when(k == 0)
        def _():
            for g in range(5):
                load_first(g, d).wait()

        if steps > 1:
            @pl.when(k == 1)
            def _():
                for g in range(5):
                    load_rest(g, d).wait()

        mixed = (gk_ref[:, cols].astype(F32) * vi_ref[:, cols].astype(F32)).astype(BF16)
        pulled = (gq_ref[:, cols].astype(F32) * go_ref[:, cols].astype(F32)).astype(BF16)
        envelope = jnp.exp(-rate_ref[:, cols] * here(0, rows))
        filt = (fr_ref[:, cols].astype(F32) * envelope).astype(BF16)
        sbuf[k, d, :, 0:chunk] = mixed
        sbuf[k, d, :, chunk:2 * chunk] = filt
        sbuf[k, d, :, 2 * chunk:3 * chunk] = pulled

        @pl.when(o < n - 1)
        def _():
            send_in(k, d).start()

        @pl.when(o == n - 1)
        def _():
            rbuf[k, me, :, 0:chunk] = mixed
            rbuf[k, me, :, chunk:2 * chunk] = filt
            rbuf[k, me, :, 2 * chunk:3 * chunk] = pulled

    @pl.when(sec == nsec - 1)
    def _():
        op_ref[...] = jnp.zeros_like(op_ref)

    for g in range(1, 4):
        load_whole(g).wait()

    tile = 16
    top = lax.broadcasted_iota(jnp.int32, (rows, 1), 0)

    @pl.loop(0, steps)
    def _(k):
        @pl.loop(0, n - 1)
        def _(o):
            got_in(k, lax.rem(me + 1 + o, n)).wait_recv()

        @pl.loop(0, rows // tile)
        def _(t):
            at = pl.ds(pl.multiple_of(t * tile, tile), tile)
            low = pl.ds(pl.multiple_of(rows + t * tile, tile), tile)
            for g in range(3):
                lanes = slice(g * chunk, (g + 1) * chunk)
                x = [rbuf[k, m, at, lanes].astype(F32) for m in range(n)]
                zero = jnp.zeros_like(x[0])
                even = combine([(1.0, x[m]) for m in range(0, n, 2)], zero)
                odd = combine([(1.0, x[m]) for m in range(1, n, 2)], zero)
                part[0, at, lanes] = (even + odd).astype(BF16)
                part[0, low, lanes] = (even - odd).astype(BF16)
                for a in range(1, n // 2 + 1):
                    cos = [math.cos(math.pi * m * a / n) for m in range(n)]
                    sin = [math.sin(math.pi * m * a / n) for m in range(n)]
                    ce = combine([(cos[m], x[m]) for m in range(0, n, 2)], zero)
                    co = combine([(cos[m], x[m]) for m in range(1, n, 2)], zero)
                    se = combine([(sin[m], x[m]) for m in range(0, n, 2)], zero)
                    so = combine([(sin[m], x[m]) for m in range(1, n, 2)], zero)
                    part[a, at, lanes] = (ce + co).astype(BF16)
                    part[a, low, lanes] = (-se - so).astype(BF16)
                    if n - a != a:
                        part[n - a, at, lanes] = (ce - co).astype(BF16)
                        part[n - a, low, lanes] = (se - so).astype(BF16)

        @pl.loop(0, n)
        def _(a):
            spec = jnp.dot(fwd_ref[a], part[a], preferred_element_type=F32)
            mr, fr, pr = (spec[:rows, g * chunk:(g + 1) * chunk] for g in range(3))
            mi, fi, pi = (spec[rows:, g * chunk:(g + 1) * chunk] for g in range(3))
            real_pair = jnp.logical_and(top == 0, a == 0)

            def product(ar, ai, br, bi, sign):
                cross = ai * bi
                re = ar * br + jnp.where(real_pair, 0.0, sign * cross)
                im = jnp.where(real_pair, cross, ar * bi - sign * ai * br)
                return re, im

            outs = (
                product(fr, fi, mr, mi, -1.0),
                product(fr, fi, pr, pi, 1.0),
                product(mr, mi, pr, pi, 1.0),
            )
            for g in range(3):
                lanes = slice(g * chunk, (g + 1) * chunk)
                part[a, 0:rows, lanes] = outs[g][0].astype(BF16)
                part[a, rows:2 * rows, lanes] = outs[g][1].astype(BF16)
            fold[a] = jnp.dot(inv_ref[a], part[a], preferred_element_type=F32)

        def unfold(t, carry):
            rate_sum, skip_sum = carry
            at = pl.ds(pl.multiple_of(t * tile, tile), tile)
            low = pl.ds(pl.multiple_of(rows + t * tile, tile), tile)
            for g in range(3):
                lanes = slice(g * chunk, (g + 1) * chunk)
                re = [fold[a, at, lanes] for a in range(n)]
                im = [fold[a, low, lanes] for a in range(n)]
                zero = jnp.zeros_like(re[0])
                for m in range(n):
                    terms = [(1.0, re[0]), ((-1.0) ** m, im[0])]
                    for a in range(1, n):
                        terms.append((math.cos(math.pi * m * a / n), re[a]))
                        terms.append((-math.sin(math.pi * m * a / n), im[a]))
                    value = combine(terms, zero).astype(BF16)
                    obuf[k, m, at, lanes] = value
                    if g == 2:
                        when = lax.broadcasted_iota(jnp.int32, (tile, 1), 0) + (t * tile + m * rows)
                        when = when.astype(F32) * np.float32(1.0 / seq)
                        mixed = rbuf[k, m, at, 0:chunk].astype(F32)
                        filt = rbuf[k, m, at, chunk:2 * chunk].astype(F32)
                        pulled = rbuf[k, m, at, 2 * chunk:3 * chunk].astype(F32)
                        rate_sum = rate_sum + when * value.astype(F32) * filt
                        skip_sum = skip_sum + mixed * pulled
            return rate_sum, skip_sum

        start = jnp.zeros((tile, chunk), F32)
        rate_sum, skip_sum = lax.fori_loop(0, rows // tile, unfold, (start, start))
        mine = pl.ds(pl.multiple_of(k * chunk, chunk), chunk)
        sstat[0:1, mine] = -jnp.sum(rate_sum, axis=0, keepdims=True)
        sstat[1:2, mine] = jnp.sum(skip_sum, axis=0, keepdims=True)

        @pl.loop(0, n - 1)
        def _(o):
            send_out(k, lax.rem(me + 1 + o, n)).start()

        hbuf[k, me] = obuf[k, me]

    for o in range(1, n):
        send_stat(lax.rem(me + o, n)).start()
    gstat[me] = sstat[...]

    @pl.loop(0, steps * n)
    def _(i):
        k, o = i // n, lax.rem(i, n)
        m = lax.rem(me + o, n)

        @pl.when(o > 0)
        def _():
            got_out(k, m).wait_recv()

        cols = columns(m, k)
        conv = hbuf[k, m, :, 0:chunk].astype(F32)
        adjoint = hbuf[k, m, :, chunk:2 * chunk].astype(F32)
        corr = hbuf[k, m, :, 2 * chunk:3 * chunk].astype(F32)
        mixed = sbuf[k, m, :, 0:chunk].astype(F32)
        pulled = sbuf[k, m, :, 2 * chunk:3 * chunk].astype(F32)
        skip = skip_ref[:, cols]
        oq_ref[:, cols] = (go_ref[:, cols].astype(F32) * (conv + skip * mixed)).astype(BF16)
        mixed_grad = adjoint + skip * pulled
        pbuf[k, m] = (mixed_grad * gk_ref[:, cols].astype(F32)).astype(BF16)

        @pl.when(sec > 0)
        def _():
            pass_copy(k, m).start()

        ok_ref[:, cols] = (mixed_grad * vi_ref[:, cols].astype(F32)).astype(BF16)
        envelope = jnp.exp(-rate_ref[:, cols] * here(0, rows))
        of_ref[:, cols] = (corr * envelope).astype(BF16)

    for o in range(1, n):
        got_stat(lax.rem(me + o, n)).wait_recv()
    for m in range(n):
        orate_ref[:, m * width:(m + 1) * width] = gstat[m, 0:1, :]
        oskip_ref[:, m * width:(m + 1) * width] = gstat[m, 1:2, :]

    for o in range(1, n):
        send_stat(lax.rem(me + o, n)).wait_send()

    @pl.loop(0, steps * (n - 1))
    def _(i):
        k, o = i // (n - 1), lax.rem(i, n - 1)
        d = lax.rem(me + 1 + o, n)
        send_in(k, d).wait_send()
        send_out(k, d).wait_send()

    @pl.loop(0, steps * n)
    def _(i):
        k, m = i // n, lax.rem(i, n)

        @pl.when(sec > 0)
        def _():
            pass_copy(k, m).wait_send()

        @pl.when(sec < nsec - 1)
        def _():
            pass_copy(k, m).wait_recv()


def make_local_tables(rows):
    length = 2 * rows
    j = np.arange(rows)[None, :]
    b = np.arange(rows)[:, None]
    angle = 2.0 * np.pi * ((j * b) % length) / length
    re, im = np.cos(angle), -np.sin(angle)
    im[0] = np.cos(np.pi * np.arange(rows))
    weight = np.full((rows, 1), 2.0 / length)
    weight[0] = 1.0 / length
    return np.concatenate([re, im]), np.concatenate([re * weight, im * weight]).T


def split(chunks):
    zero, first = chunks * 6 // 32, chunks // 4
    third = (chunks - zero - first) // 2
    counts = (zero, first, chunks - zero - first - third, third)
    bases = tuple(sum(counts[:o]) for o in range(4))
    return counts, bases, chunks // 16, chunks // 8


def quad_kernel(
    nsec, chunk,
    gq_hbm, gk_hbm, vi_hbm, fr_hbm, go_hbm, rate_hbm, skip_hbm, fwd_hbm, inv_hbm, fwdl_hbm, invl_hbm,
    oq_ref, ok_ref, op_ref, of_ref, orate_ref, oskip_ref,
    gq_ref, gk_ref, vi_ref, fr_ref, go_ref, rate_ref, skip_ref, fwd_ref, inv_ref, fwdl_ref, invl_ref,
    in_sem, row_sem,
    sbuf, rbuf, obuf, hbuf, pbuf, lbuf, relin, relout, part, fold, sown, sloc, gown, gloc,
    i_send, i_recv, ri_send, ri_recv, o_send, o_recv, ro_send, ro_recv, p_send, p_recv,
    t_send, t_recv,
):
    n = 4
    rows, channels = gq_ref.shape
    chunks = channels // chunk
    counts, bases, rin, rout = split(chunks)
    most = max(counts)
    seq = rows * n
    me = lax.axis_index("ctx")
    sec = lax.axis_index("section")
    before = lax.rem(sec + nsec - 1, nsec)
    after = lax.rem(sec + 1, nsec)
    is1 = me * (3 - me) * (2 - me) // 2
    is2 = me * (3 - me) * (me - 1) // 2
    is3 = me * (me - 1) * (me - 2) // 6
    is0 = 1 - is1 - is2 - is3
    own = is0 * counts[0] + is1 * counts[1] + is2 * counts[2] + is3 * counts[3]
    base = is1 * bases[1] + is2 * bases[2] + is3 * bases[3]

    def lanes_of(c):
        return pl.ds(pl.multiple_of(c * chunk, chunk), chunk)

    tokens = (
        (gk_hbm, gk_ref), (vi_hbm, vi_ref), (gq_hbm, gq_ref), (go_hbm, go_ref), (fr_hbm, fr_ref)
    )
    whole = (
        (rate_hbm, rate_ref), (skip_hbm, skip_ref), (fwd_hbm, fwd_ref), (inv_hbm, inv_ref),
        (fwdl_hbm, fwdl_ref), (invl_hbm, invl_ref),
    )

    def load(g, o, rest):
        hbm, ref = tokens[g]
        lo = bases[o] + rest
        hi = bases[o] + counts[o] if rest else lo + 1
        cols = slice(lo * chunk, hi * chunk)
        return pltpu.make_async_copy(hbm.at[:, cols], ref.at[:, cols], in_sem.at[g, rest, o])

    def load_whole(g):
        return pltpu.make_async_copy(whole[g][0], whole[g][1], row_sem.at[g])

    load_whole(0).start()
    for rest in range(2):
        for o in range(n):
            for g in range(5):
                load(g, o, rest).start()
    for g in range(1, 6):
        load_whole(g).start()

    barrier = pltpu.get_barrier_semaphore()
    for o in range(1, n):
        pl.semaphore_signal(
            barrier, inc=1, device_id={"ctx": lax.rem(me + o, n)}, device_id_type=MESH
        )
    for other in (before, after):
        pl.semaphore_signal(barrier, inc=1, device_id={"section": other}, device_id_type=MESH)
    pl.semaphore_wait(barrier, n + 1)
    load_whole(0).wait()

    def to(d):
        return {"ctx": jnp.int32(d)}

    def remote(src, dst, send, recv, where):
        return pltpu.make_async_remote_copy(
            src_ref=src, dst_ref=dst, send_sem=send, recv_sem=recv,
            device_id=where, device_id_type=MESH,
        )

    def give_pair(o, k):
        c = bases[o] + k
        return remote(
            sbuf.at[c, 0:2], rbuf.at[k, 0, 0:2], i_send.at[c], i_recv.at[k, 0], to(o)
        )

    def give_all(o, k):
        c = bases[o] + k
        return remote(sbuf.at[c], rbuf.at[k, me], i_send.at[c], i_recv.at[k, me], to(o))

    def give_relay(k):
        c = bases[1] + k
        return remote(sbuf.at[c], relin.at[k], i_send.at[c], ri_recv.at[k], to(0))

    def forward_in(i):
        return remote(
            relin.at[i], rbuf.at[i, 2], ri_send.at[i], i_recv.at[i, 2], to(1)
        )

    def got_in(k, s):
        at = rbuf.at[k, 0, 0:2] if s == 0 else rbuf.at[k, s]
        src = sbuf.at[0, 0:2] if s == 0 else sbuf.at[0]
        return remote(src, at, i_send.at[0], i_recv.at[k, s], to(s))

    def back_first(k, m):
        return remote(
            obuf.at[k, m, 2], hbuf.at[base + k, 2], o_send.at[k, m, 0], o_recv.at[base + k, 0],
            to(m),
        )

    def back_corr(k):
        return remote(
            obuf.at[k, 0, 1], hbuf.at[base + k, 1], o_send.at[k, 0, 1], o_recv.at[base + k, 1],
            to(0),
        )

    def back_rest(k, m):
        return remote(
            obuf.at[k, m, 0:2], hbuf.at[base + k, 0:2], o_send.at[k, m, 1],
            o_recv.at[base + k, 1], to(m),
        )

    def back_relay(i):
        k = counts[2] - rout + i
        return remote(obuf.at[k, 1, 0:2], relout.at[i], o_send.at[k, 1, 1], ro_recv.at[i], to(0))

    def forward_out(i):
        c = bases[2] + counts[2] - rout + i
        return remote(relout.at[i], hbuf.at[c, 0:2], ro_send.at[i], o_recv.at[c, 1], to(1))

    def got_first(c):
        return remote(
            obuf.at[0, 0, 2], hbuf.at[c, 2], o_send.at[0, 0, 0], o_recv.at[c, 0], to(1)
        )

    def got_corr(c):
        return remote(
            obuf.at[0, 0, 1], hbuf.at[c, 1], o_send.at[0, 0, 1], o_recv.at[c, 1], to(1)
        )

    def got_rest(c):
        return remote(
            obuf.at[0, 0, 0:2], hbuf.at[c, 0:2], o_send.at[0, 0, 1], o_recv.at[c, 1], to(1)
        )

    def stat_own(o, d):
        cols = slice(bases[o] * chunk, (bases[o] + counts[o]) * chunk)
        return remote(
            sown.at[:, cols], gown.at[:, cols], t_send.at[0, d], t_recv.at[0, o], to(d)
        )

    def stat_local(d):
        return remote(sloc, gloc, t_send.at[1, d], t_recv.at[1, 0], to(d))

    def pass_copy(c):
        return remote(
            pbuf.at[c], op_ref.at[:, lanes_of(c)], p_send.at[c], p_recv.at[c],
            {"section": before},
        )

    when = lax.broadcasted_iota(jnp.int32, (rows, 1), 0) + me * rows
    when = when.astype(F32) * np.float32(1.0 / seq)

    @pl.loop(0, most)
    def _(step):
        for o in reversed(range(n)):
            k = step * counts[o] // most

            @pl.when((step + 1) * counts[o] // most > k)
            def _(o=o, k=k):
                for rest in range(2):
                    @pl.when(k == rest)
                    def _():
                        for g in range(5):
                            load(g, o, rest).wait()

                c = bases[o] + k
                cols = lanes_of(c)
                mixed = (gk_ref[:, cols].astype(F32) * vi_ref[:, cols].astype(F32)).astype(BF16)
                pulled = (gq_ref[:, cols].astype(F32) * go_ref[:, cols].astype(F32)).astype(BF16)
                envelope = jnp.exp(-rate_ref[:, cols] * when)
                filt = (fr_ref[:, cols].astype(F32) * envelope).astype(BF16)
                sbuf[c, 0] = mixed
                sbuf[c, 1] = filt
                sbuf[c, 2] = pulled

                @pl.when(me == o)
                def _():
                    rbuf[k, o, 0] = mixed
                    rbuf[k, o, 1] = filt
                    if o:
                        rbuf[k, o, 2] = pulled

                if o:
                    @pl.when(me == 0)
                    def _():
                        give_pair(o, k).start()

                if o == 1:
                    @pl.when(jnp.logical_and(me == 2, k < rin))
                    def _():
                        give_relay(k).start()

                    @pl.when(jnp.logical_or(me == 3, jnp.logical_and(me == 2, k >= rin)))
                    def _():
                        give_all(o, k).start()
                else:
                    @pl.when(jnp.logical_and(me != 0, me != o))
                    def _():
                        give_all(o, k).start()

    @pl.when(sec == nsec - 1)
    def _():
        op_ref[...] = jnp.zeros_like(op_ref)

    for g in range(1, 6):
        load_whole(g).wait()

    tile = 16
    top = lax.broadcasted_iota(jnp.int32, (rows, 1), 0)

    def product(real_pair, ar, ai, br, bi, sign):
        cross = ai * bi
        re = ar * br + jnp.where(real_pair, 0.0, sign * cross)
        im = jnp.where(real_pair, cross, ar * bi - sign * ai * br)
        return re, im

    def products(spec, real_pair):
        mr, fr, pr = (spec[:rows, g * chunk:(g + 1) * chunk] for g in range(3))
        mi, fi, pi = (spec[rows:, g * chunk:(g + 1) * chunk] for g in range(3))
        return (
            product(real_pair, fr, fi, mr, mi, -1.0),
            product(real_pair, fr, fi, pr, pi, 1.0),
            product(real_pair, mr, mi, pr, pi, 1.0),
        )

    @pl.when(me == 0)
    def _():
        @pl.loop(0, chunks)
        def _(c):
            if rin:
                @pl.when(c < rin)
                def _():
                    give_relay(c).wait_recv()
                    forward_in(c).start()

            for g in range(3):
                part[0, 0:rows, g * chunk:(g + 1) * chunk] = sbuf[c, g]
            spec = jnp.dot(fwdl_ref[...], part[0, 0:rows, :], preferred_element_type=F32)
            outs = products(spec, top == 0)
            for g in range(3):
                lanes = slice(g * chunk, (g + 1) * chunk)
                part[1, 0:rows, lanes] = outs[g][0].astype(BF16)
                part[1, rows:2 * rows, lanes] = outs[g][1].astype(BF16)
            back = jnp.dot(invl_ref[...], part[1], preferred_element_type=F32).astype(BF16)
            corr = back[:, 2 * chunk:3 * chunk]
            hbuf[c, 0] = back[:, 0:chunk]
            lbuf[c, 0] = back[:, chunk:2 * chunk]
            lbuf[c, 1] = corr
            rate = when * corr.astype(F32) * sbuf[c, 1].astype(F32)
            skip = sbuf[c, 0].astype(F32) * sbuf[c, 2].astype(F32)
            cols = lanes_of(c)
            sloc[0:1, cols] = -jnp.sum(rate, axis=0, keepdims=True)
            sloc[1:2, cols] = jnp.sum(skip, axis=0, keepdims=True)

        for d in range(1, n):
            stat_local(d).start()
        gloc[...] = sloc[...]

    @pl.loop(0, own)
    def _(k):
        for s in range(n):
            @pl.when(me != s)
            def _():
                got_in(k, s).wait_recv()

        @pl.loop(0, rows // tile)
        def _(t):
            at = pl.ds(pl.multiple_of(t * tile, tile), tile)
            low = pl.ds(pl.multiple_of(rows + t * tile, tile), tile)
            for g in range(3):
                lanes = slice(g * chunk, (g + 1) * chunk)
                held = range(1, n) if g == 2 else range(n)
                x = {m: rbuf[k, m, g, at, :].astype(F32) for m in held}
                even = [m for m in held if m % 2 == 0]
                odd = [m for m in held if m % 2 == 1]
                zero = jnp.zeros_like(x[1])
                e = combine([(1.0, x[m]) for m in even], zero)
                d = combine([(1.0, x[m]) for m in odd], zero)
                part[0, at, lanes] = (e + d).astype(BF16)
                part[0, low, lanes] = (e - d).astype(BF16)
                for a in range(1, n // 2 + 1):
                    cos = [math.cos(math.pi * m * a / n) for m in range(n)]
                    sin = [math.sin(math.pi * m * a / n) for m in range(n)]
                    ce = combine([(cos[m], x[m]) for m in even], zero)
                    co = combine([(cos[m], x[m]) for m in odd], zero)
                    se = combine([(sin[m], x[m]) for m in even], zero)
                    so = combine([(sin[m], x[m]) for m in odd], zero)
                    part[a, at, lanes] = (ce + co).astype(BF16)
                    part[a, low, lanes] = (-se - so).astype(BF16)
                    if n - a != a:
                        part[n - a, at, lanes] = (ce - co).astype(BF16)
                        part[n - a, low, lanes] = (se - so).astype(BF16)

        @pl.loop(0, n)
        def _(a):
            spec = jnp.dot(fwd_ref[a], part[a], preferred_element_type=F32)
            outs = products(spec, jnp.logical_and(top == 0, a == 0))
            for g in range(3):
                lanes = slice(g * chunk, (g + 1) * chunk)
                part[a, 0:rows, lanes] = outs[g][0].astype(BF16)
                part[a, rows:2 * rows, lanes] = outs[g][1].astype(BF16)
            fold[a] = jnp.dot(inv_ref[a], part[a], preferred_element_type=F32)

        def unfold(t, carry):
            rate_sum, skip_sum = carry
            at = pl.ds(pl.multiple_of(t * tile, tile), tile)
            low = pl.ds(pl.multiple_of(rows + t * tile, tile), tile)
            for g in range(3):
                lanes = slice(g * chunk, (g + 1) * chunk)
                re = [fold[a, at, lanes] for a in range(n)]
                im = [fold[a, low, lanes] for a in range(n)]
                zero = jnp.zeros_like(re[0])
                for m in range(1 if g == 0 else 0, n):
                    terms = [(1.0, re[0]), ((-1.0) ** m, im[0])]
                    for a in range(1, n):
                        terms.append((math.cos(math.pi * m * a / n), re[a]))
                        terms.append((-math.sin(math.pi * m * a / n), im[a]))
                    value = combine(terms, zero).astype(BF16)
                    obuf[k, m, (0, 2, 1)[g], at, :] = value
                    if g == 2:
                        pos = lax.broadcasted_iota(jnp.int32, (tile, 1), 0) + (t * tile + m * rows)
                        pos = pos.astype(F32) * np.float32(1.0 / seq)
                        filt = rbuf[k, m, 1, at, :].astype(F32)
                        rate_sum = rate_sum + pos * value.astype(F32) * filt
                        if m:
                            mixed = rbuf[k, m, 0, at, :].astype(F32)
                            pulled = rbuf[k, m, 2, at, :].astype(F32)
                            skip_sum = skip_sum + mixed * pulled
            return rate_sum, skip_sum

        start = jnp.zeros((tile, chunk), F32)
        rate_sum, skip_sum = lax.fori_loop(0, rows // tile, unfold, (start, start))
        mine = lanes_of(base + k)
        sown[0:1, mine] = -jnp.sum(rate_sum, axis=0, keepdims=True)
        sown[1:2, mine] = jnp.sum(skip_sum, axis=0, keepdims=True)

        for m in range(n):
            @pl.when(me != m)
            def _():
                back_first(k, m).start()

        @pl.when(me == 0)
        def _():
            hbuf[base + k, 1:3] = obuf[k, 0, 1:3]

        @pl.when(me != 0)
        def _():
            hbuf[base + k] = obuf[k, me]

    for o in range(n):
        @pl.when(me == o)
        def _():
            cols = slice(bases[o] * chunk, (bases[o] + counts[o]) * chunk)
            for d in range(n):
                if d != o:
                    stat_own(o, d).start()
            gown[:, cols] = sown[:, cols]

    @pl.when(me == 2)
    def _():
        @pl.loop(0, rout)
        def _(i):
            back_relay(i).start()

    @pl.loop(0, own)
    def _(k):
        @pl.when(me != 0)
        def _():
            back_corr(k).start()

        direct = jnp.logical_or(me != 2, k < counts[2] - rout)

        @pl.when(jnp.logical_and(me != 1, direct))
        def _():
            back_rest(k, 1).start()

        for m in range(2, n):
            @pl.when(me != m)
            def _():
                back_rest(k, m).start()

    @pl.loop(0, most)
    def _(step):
        @pl.when(jnp.logical_and(me == 0, step >= most - rout))
        def _():
            back_relay(step - (most - rout)).wait_recv()
            forward_out(step - (most - rout)).start()

        for o in range(n):
            k = step * counts[o] // most

            @pl.when((step + 1) * counts[o] // most > k)
            def _(o=o, k=k):
                c = bases[o] + k

                @pl.when(me != o)
                def _():
                    got_first(c).wait_recv()

                @pl.when(me == 0)
                def _():
                    both = hbuf[c, 2].astype(F32) + lbuf[c, 0].astype(F32)
                    hbuf[c, 2] = both.astype(BF16)

                cols = lanes_of(c)
                pulled = sbuf[c, 2].astype(F32)
                mixed_grad = hbuf[c, 2].astype(F32) + skip_ref[:, cols] * pulled
                pbuf[c] = (mixed_grad * gk_ref[:, cols].astype(F32)).astype(BF16)

                @pl.when(sec > 0)
                def _():
                    pass_copy(c).start()

                ok_ref[:, cols] = (mixed_grad * vi_ref[:, cols].astype(F32)).astype(BF16)

    @pl.loop(0, most)
    def _(step):
        for o in range(n):
            k = step * counts[o] // most

            @pl.when((step + 1) * counts[o] // most > k)
            def _(o=o, k=k):
                c = bases[o] + k

                @pl.when(me == 0)
                def _():
                    if o:
                        got_corr(c).wait_recv()
                    both = hbuf[c, 1].astype(F32) + lbuf[c, 1].astype(F32)
                    hbuf[c, 1] = both.astype(BF16)

                @pl.when(jnp.logical_and(me != 0, me != o))
                def _():
                    got_rest(c).wait_recv()

                cols = lanes_of(c)
                conv = hbuf[c, 0].astype(F32)
                mixed = sbuf[c, 0].astype(F32)
                oq_ref[:, cols] = (
                    go_ref[:, cols].astype(F32) * (conv + skip_ref[:, cols] * mixed)
                ).astype(BF16)
                envelope = jnp.exp(-rate_ref[:, cols] * when)
                of_ref[:, cols] = (hbuf[c, 1].astype(F32) * envelope).astype(BF16)

    @pl.when(me != 0)
    def _():
        stat_local(1).wait_recv()

    for o in range(n):
        @pl.when(me != o)
        def _():
            stat_own(o, 0).wait_recv()
    orate_ref[...] = gown[0:1, :] + gloc[0:1, :]
    oskip_ref[...] = gown[1:2, :] + gloc[1:2, :]

    for d in range(1, n):
        @pl.when(me == 0)
        def _():
            stat_local(d).wait_send()
    for o in range(n):
        @pl.when(me == o)
        def _():
            for d in range(n):
                if d != o:
                    stat_own(o, d).wait_send()

    @pl.loop(0, most)
    def _(k):
        for o in range(n):
            @pl.when(k < counts[o])
            def _():
                if o:
                    @pl.when(me == 0)
                    def _():
                        give_pair(o, k).wait_send()

                @pl.when(jnp.logical_and(me != 0, me != o))
                def _():
                    give_all(o, k).wait_send()

    @pl.loop(0, own)
    def _(k):
        for m in range(n):
            @pl.when(me != m)
            def _():
                back_first(k, m).wait_send()
                (back_rest(k, m) if m else back_corr(k)).wait_send()

    @pl.when(me == 0)
    def _():
        for i in range(rin):
            forward_in(i).wait_send()

        @pl.loop(0, rout)
        def _(k):
            forward_out(k).wait_send()

    @pl.loop(0, chunks)
    def _(c):
        @pl.when(sec > 0)
        def _():
            pass_copy(c).wait_send()

        @pl.when(sec < nsec - 1)
        def _():
            pass_copy(c).wait_recv()


def quad_call(nsec, shapes, chunk, args, decay_rate, skip_gain):
    rows, channels = shapes[0].shape
    chunks = channels // chunk
    counts, _, rin, rout = split(chunks)
    most = max(counts)
    tables = (*make_tables(4, rows), *make_local_tables(rows))
    tables = tuple(jnp.asarray(table, BF16) for table in tables)
    dma = pltpu.SemaphoreType.DMA
    block = pltpu.VMEM((rows, channels), BF16)
    row = pltpu.VMEM((1, channels), F32)
    stat = pltpu.VMEM((2, channels), F32)
    return pl.pallas_call(
        functools.partial(quad_kernel, nsec, chunk),
        out_shape=tuple(pltpu.VMEM(shape.shape, shape.dtype) for shape in shapes),
        in_specs=[pl.BlockSpec(memory_space=pl.ANY)] * 11,
        out_specs=(pl.BlockSpec(memory_space=pltpu.VMEM),) * 6,
        scratch_shapes=[
            *([block] * 5), row, row, *(pltpu.VMEM(table.shape, BF16) for table in tables),
            dma((5, 2, 4)), dma((6,)),
            pltpu.VMEM((chunks, 3, rows, chunk), BF16),
            pltpu.VMEM((most, 4, 3, rows, chunk), BF16),
            pltpu.VMEM((most, 4, 3, rows, chunk), BF16),
            pltpu.VMEM((chunks, 3, rows, chunk), BF16),
            pltpu.VMEM((chunks, rows, chunk), BF16),
            pltpu.VMEM((chunks, 2, rows, chunk), BF16),
            pltpu.VMEM((max(rin, 1), 3, rows, chunk), BF16),
            pltpu.VMEM((rout, 2, rows, chunk), BF16),
            pltpu.VMEM((4, 2 * rows, 3 * chunk), BF16),
            pltpu.VMEM((4, 2 * rows, 3 * chunk), F32),
            stat, stat, stat, stat,
            dma((chunks,)), dma((most, 4)), dma((max(rin, 1),)), dma((max(rin, 1),)),
            dma((most, 4, 2)), dma((chunks, 2)), dma((rout,)), dma((rout,)),
            dma((chunks,)), dma((chunks,)), dma((2, 4)), dma((2, 4)),
        ],
        compiler_params=pltpu.CompilerParams(
            collective_id=0, has_side_effects=True, vmem_limit_bytes=58 * 1024 * 1024
        ),
        name="hyena_backward_quad",
    )(*args, decay_rate, skip_gain, *tables)


def finish(*refs):
    count = (len(refs) - 1) // 2
    sem = refs[-1]
    copies = [
        pltpu.make_async_copy(refs[g], refs[count + g], sem.at[g]) for g in range(count)
    ]
    for copy in copies:
        copy.start()
    for copy in copies:
        copy.wait()


def general_call(n, nsec, shapes, chunk, args, decay_rate, skip_gain):
    rows, channels = shapes[0].shape
    width = channels // n
    steps = width // chunk
    fwd, inv = make_tables(n, rows)
    fwd, inv = jnp.asarray(fwd, BF16), jnp.asarray(inv, BF16)
    message = (steps, n, rows, 3 * chunk)
    dma = pltpu.SemaphoreType.DMA
    anywhere = pl.BlockSpec(memory_space=pl.ANY)
    inside = pl.BlockSpec(memory_space=pltpu.VMEM)
    return pl.pallas_call(
        functools.partial(kernel, n, nsec, chunk, steps),
        out_shape=tuple(pltpu.VMEM(shape.shape, shape.dtype) for shape in shapes),
        in_specs=[anywhere] * 9,
        out_specs=(inside,) * 6,
        scratch_shapes=[
            *([pltpu.VMEM((rows, channels), BF16)] * 5),
            *([pltpu.VMEM((1, channels), F32)] * 2),
            *([pltpu.VMEM(fwd.shape, BF16)] * 2),
            dma((5, 2, n)), dma((4,)),
            pltpu.VMEM(message, BF16),
            pltpu.VMEM(message, BF16),
            pltpu.VMEM(message, BF16),
            pltpu.VMEM(message, BF16),
            pltpu.VMEM((steps, n, rows, chunk), BF16),
            pltpu.VMEM((n, 2 * rows, 3 * chunk), BF16),
            pltpu.VMEM((n, 2 * rows, 3 * chunk), F32),
            pltpu.VMEM((2, width), F32),
            pltpu.VMEM((n, 2, width), F32),
            dma((steps, n)), dma((steps, n)), dma((steps, n)), dma((steps, n)),
            dma((steps, n)), dma((steps, n)), dma((n,)), dma((n,)),
        ],
        compiler_params=pltpu.CompilerParams(
            collective_id=0, has_side_effects=True, vmem_limit_bytes=58 * 1024 * 1024
        ),
        name="hyena_backward",
    )(
        *args, decay_rate, skip_gain, fwd, inv,
    )


def shards(n, nsec, gate_q, gate_k, value_in, filter_raw, decay_rate, skip_gain, grad_out):
    rows, channels = gate_q.shape[1:]
    block = jax.ShapeDtypeStruct((rows, channels), BF16)
    row = jax.ShapeDtypeStruct((1, channels), F32)
    dma = pltpu.SemaphoreType.DMA
    anywhere = pl.BlockSpec(memory_space=pl.ANY)
    inside = pl.BlockSpec(memory_space=pltpu.VMEM)
    shapes = (block, block, block, block, row, row)
    args = (gate_q[0], gate_k[0], value_in[0], filter_raw[0], grad_out[0])
    call = quad_call if n == 4 and channels >= 16 * 128 else functools.partial(general_call, n)
    outs = call(nsec, shapes, 128, args, decay_rate, skip_gain)
    oq, ok, op, of, orate, oskip = pl.pallas_call(
        finish,
        out_shape=shapes,
        in_specs=[inside] * 6,
        out_specs=(anywhere,) * 6,
        scratch_shapes=[dma((6,))],
        compiler_params=pltpu.CompilerParams(vmem_limit_bytes=4 * 1024 * 1024),
        name="hand_over",
    )(*(pltpu.with_memory_space_constraint(out, pltpu.VMEM) for out in outs))
    return oq[None], ok[None], op[None], of[None], orate, oskip


def solution(mesh):
    n, nsec = mesh.shape["ctx"], mesh.shape["section"]
    tokens = P("section", "ctx", None)
    return jax.shard_map(
        functools.partial(shards, n, nsec),
        mesh=mesh,
        in_specs=(tokens, tokens, tokens, tokens, P("section", None), P("section", None), tokens),
        out_specs=(tokens, tokens, tokens, tokens, P("section", None), P("section", None)),
        check_vma=False,
    )
```

```python
import functools
import math

import jax
import jax.numpy as jnp
import numpy as np
from jax import lax
from jax.experimental import pallas as pl
from jax.experimental.pallas import tpu as pltpu
from jax.sharding import PartitionSpec as P

MESH = pl.DeviceIdType.MESH
F32 = jnp.float32
BF16 = jnp.bfloat16


def make_tables(n, rows):
    length = 2 * n * rows
    half = rows // 2
    j = np.arange(rows)[None, :]
    b = np.arange(rows)[:, None]

    def angle(a):
        return 2.0 * np.pi * ((j * (a + 2 * n * b)) % length) / length

    fwd = np.zeros((n, 2 * rows, 2 * rows))
    inv = np.zeros((n, 2 * rows, 2 * rows))
    for a in range(1, n):
        c, s = np.cos(angle(a)), np.sin(angle(a))
        fwd[a] = np.block([[c, s], [-s, c]])
        inv[a] = np.block([[c.T, -s.T], [s.T, c.T]]) * (2.0 / length)
    for slot, a in ((0, 0), (1, n)):
        c, s = np.cos(angle(a))[:half], np.sin(angle(a))[:half]
        weight = np.full((half, 1), 2.0 / length)
        re_rows = slice(slot * half, (slot + 1) * half)
        im_rows = slice(rows + slot * half, rows + (slot + 1) * half)
        cols = slice(slot * rows, (slot + 1) * rows)
        im = -s
        if slot == 0:
            im = im.copy()
            im[0] = np.cos(np.pi * np.arange(rows))
            weight[0] = 1.0 / length
        fwd[0, re_rows, cols] = c
        fwd[0, im_rows, cols] = im
        inv[0, cols, re_rows] = (c * weight).T
        inv[0, cols, im_rows] = (im * weight).T
    return fwd, inv


def scaled(coef, x):
    if abs(coef - 1.0) < 1e-12:
        return x
    if abs(coef + 1.0) < 1e-12:
        return -x
    return x * np.float32(coef)


def combine(terms, zero):
    total = None
    for coef, x in terms:
        if abs(coef) < 1e-12:
            continue
        if total is None:
            total = scaled(coef, x)
        elif coef < 0:
            total = total - scaled(-coef, x)
        else:
            total = total + scaled(coef, x)
    return zero if total is None else total


def kernel(
    n, nsec, chunk, steps,
    gq_hbm, gk_hbm, vi_hbm, fr_hbm, go_hbm, rate_hbm, skip_hbm, fwd_hbm, inv_hbm,
    oq_ref, ok_ref, op_ref, of_ref, orate_ref, oskip_ref,
    gq_ref, gk_ref, vi_ref, fr_ref, go_ref, rate_ref, skip_ref, fwd_ref, inv_ref,
    in_sem, row_sem,
    sbuf, rbuf, obuf, hbuf, pbuf, part, fold, sstat, gstat,
    s_send, s_recv, o_send, o_recv, p_send, p_recv, t_send, t_recv,
):
    rows = gq_ref.shape[0]
    width = chunk * steps
    seq = rows * n
    me = lax.axis_index("ctx")
    sec = lax.axis_index("section")
    before = lax.rem(sec + nsec - 1, nsec)
    after = lax.rem(sec + 1, nsec)

    def columns(owner, k):
        return pl.ds(pl.multiple_of(owner * width + k * chunk, chunk), chunk)

    tokens = (
        (gk_hbm, gk_ref), (vi_hbm, vi_ref), (gq_hbm, gq_ref), (go_hbm, go_ref), (fr_hbm, fr_ref)
    )
    whole = (
        (rate_hbm, rate_ref), (skip_hbm, skip_ref), (fwd_hbm, fwd_ref), (inv_hbm, inv_ref)
    )

    def load_first(g, d):
        hbm, ref = tokens[g]
        return pltpu.make_async_copy(
            hbm.at[:, columns(d, 0)], ref.at[:, columns(d, 0)], in_sem.at[g, 0, d]
        )

    def load_rest(g, d):
        hbm, ref = tokens[g]
        cols = pl.ds(pl.multiple_of(d * width + chunk, chunk), width - chunk)
        return pltpu.make_async_copy(hbm.at[:, cols], ref.at[:, cols], in_sem.at[g, 1, d])

    def load_whole(g):
        return pltpu.make_async_copy(whole[g][0], whole[g][1], row_sem.at[g])

    load_whole(0).start()
    for o in range(n):
        for g in range(5):
            load_first(g, lax.rem(me + 1 + o, n)).start()
    if steps > 1:
        for d in range(n):
            for g in range(5):
                load_rest(g, d).start()
    for g in range(1, 4):
        load_whole(g).start()

    barrier = pltpu.get_barrier_semaphore()
    for o in range(1, n):
        pl.semaphore_signal(
            barrier, inc=1, device_id={"ctx": lax.rem(me + o, n)}, device_id_type=MESH
        )
    for other in (before, after):
        pl.semaphore_signal(barrier, inc=1, device_id={"section": other}, device_id_type=MESH)
    pl.semaphore_wait(barrier, n + 1)
    load_whole(0).wait()

    def here(row0, count):
        row = lax.broadcasted_iota(jnp.int32, (count, 1), 0) + (row0 + me * rows)
        return row.astype(F32) * np.float32(1.0 / seq)

    def send_in(k, d):
        return pltpu.make_async_remote_copy(
            src_ref=sbuf.at[k, d], dst_ref=rbuf.at[k, me], send_sem=s_send.at[k, d],
            recv_sem=s_recv.at[k, me], device_id={"ctx": d}, device_id_type=MESH,
        )

    def got_in(k, m):
        return pltpu.make_async_remote_copy(
            src_ref=sbuf.at[k, m], dst_ref=rbuf.at[k, m], send_sem=s_send.at[k, m],
            recv_sem=s_recv.at[k, m], device_id={"ctx": m}, device_id_type=MESH,
        )

    def send_out(k, m):
        return pltpu.make_async_remote_copy(
            src_ref=obuf.at[k, m], dst_ref=hbuf.at[k, me], send_sem=o_send.at[k, m],
            recv_sem=o_recv.at[k, me], device_id={"ctx": m}, device_id_type=MESH,
        )

    def got_out(k, m):
        return pltpu.make_async_remote_copy(
            src_ref=obuf.at[k, m], dst_ref=hbuf.at[k, m], send_sem=o_send.at[k, m],
            recv_sem=o_recv.at[k, m], device_id={"ctx": m}, device_id_type=MESH,
        )

    def send_stat(d):
        return pltpu.make_async_remote_copy(
            src_ref=sstat, dst_ref=gstat.at[me], send_sem=t_send.at[d],
            recv_sem=t_recv.at[me], device_id={"ctx": d}, device_id_type=MESH,
        )

    def got_stat(m):
        return pltpu.make_async_remote_copy(
            src_ref=sstat, dst_ref=gstat.at[m], send_sem=t_send.at[m],
            recv_sem=t_recv.at[m], device_id={"ctx": m}, device_id_type=MESH,
        )

    def pass_copy(k, m):
        return pltpu.make_async_remote_copy(
            src_ref=pbuf.at[k, m], dst_ref=op_ref.at[:, columns(m, k)], send_sem=p_send.at[k, m],
            recv_sem=p_recv.at[k, m], device_id={"section": before}, device_id_type=MESH,
        )

    @pl.loop(0, steps * n)
    def _(i):
        k, o = i // n, lax.rem(i, n)
        d = lax.rem(me + 1 + o, n)
        cols = columns(d, k)

        @pl.when(k == 0)
        def _():
            for g in range(5):
                load_first(g, d).wait()

        if steps > 1:
            @pl.when(k == 1)
            def _():
                for g in range(5):
                    load_rest(g, d).wait()

        mixed = (gk_ref[:, cols].astype(F32) * vi_ref[:, cols].astype(F32)).astype(BF16)
        pulled = (gq_ref[:, cols].astype(F32) * go_ref[:, cols].astype(F32)).astype(BF16)
        envelope = jnp.exp(-rate_ref[:, cols] * here(0, rows))
        filt = (fr_ref[:, cols].astype(F32) * envelope).astype(BF16)
        sbuf[k, d, :, 0:chunk] = mixed
        sbuf[k, d, :, chunk:2 * chunk] = filt
        sbuf[k, d, :, 2 * chunk:3 * chunk] = pulled

        @pl.when(o < n - 1)
        def _():
            send_in(k, d).start()

        @pl.when(o == n - 1)
        def _():
            rbuf[k, me, :, 0:chunk] = mixed
            rbuf[k, me, :, chunk:2 * chunk] = filt
            rbuf[k, me, :, 2 * chunk:3 * chunk] = pulled

    @pl.when(sec == nsec - 1)
    def _():
        op_ref[...] = jnp.zeros_like(op_ref)

    for g in range(1, 4):
        load_whole(g).wait()

    tile = 16
    top = lax.broadcasted_iota(jnp.int32, (rows, 1), 0)

    @pl.loop(0, steps)
    def _(k):
        @pl.loop(0, n - 1)
        def _(o):
            got_in(k, lax.rem(me + 1 + o, n)).wait_recv()

        @pl.loop(0, rows // tile)
        def _(t):
            at = pl.ds(pl.multiple_of(t * tile, tile), tile)
            low = pl.ds(pl.multiple_of(rows + t * tile, tile), tile)
            for g in range(3):
                lanes = slice(g * chunk, (g + 1) * chunk)
                x = [rbuf[k, m, at, lanes].astype(F32) for m in range(n)]
                zero = jnp.zeros_like(x[0])
                even = combine([(1.0, x[m]) for m in range(0, n, 2)], zero)
                odd = combine([(1.0, x[m]) for m in range(1, n, 2)], zero)
                part[0, at, lanes] = (even + odd).astype(BF16)
                part[0, low, lanes] = (even - odd).astype(BF16)
                for a in range(1, n // 2 + 1):
                    cos = [math.cos(math.pi * m * a / n) for m in range(n)]
                    sin = [math.sin(math.pi * m * a / n) for m in range(n)]
                    ce = combine([(cos[m], x[m]) for m in range(0, n, 2)], zero)
                    co = combine([(cos[m], x[m]) for m in range(1, n, 2)], zero)
                    se = combine([(sin[m], x[m]) for m in range(0, n, 2)], zero)
                    so = combine([(sin[m], x[m]) for m in range(1, n, 2)], zero)
                    part[a, at, lanes] = (ce + co).astype(BF16)
                    part[a, low, lanes] = (-se - so).astype(BF16)
                    if n - a != a:
                        part[n - a, at, lanes] = (ce - co).astype(BF16)
                        part[n - a, low, lanes] = (se - so).astype(BF16)

        @pl.loop(0, n)
        def _(a):
            spec = jnp.dot(fwd_ref[a], part[a], preferred_element_type=F32)
            mr, fr, pr = (spec[:rows, g * chunk:(g + 1) * chunk] for g in range(3))
            mi, fi, pi = (spec[rows:, g * chunk:(g + 1) * chunk] for g in range(3))
            real_pair = jnp.logical_and(top == 0, a == 0)

            def product(ar, ai, br, bi, sign):
                cross = ai * bi
                re = ar * br + jnp.where(real_pair, 0.0, sign * cross)
                im = jnp.where(real_pair, cross, ar * bi - sign * ai * br)
                return re, im

            outs = (
                product(fr, fi, mr, mi, -1.0),
                product(fr, fi, pr, pi, 1.0),
                product(mr, mi, pr, pi, 1.0),
            )
            for g in range(3):
                lanes = slice(g * chunk, (g + 1) * chunk)
                part[a, 0:rows, lanes] = outs[g][0].astype(BF16)
                part[a, rows:2 * rows, lanes] = outs[g][1].astype(BF16)
            fold[a] = jnp.dot(inv_ref[a], part[a], preferred_element_type=F32)

        def unfold(t, carry):
            rate_sum, skip_sum = carry
            at = pl.ds(pl.multiple_of(t * tile, tile), tile)
            low = pl.ds(pl.multiple_of(rows + t * tile, tile), tile)
            for g in range(3):
                lanes = slice(g * chunk, (g + 1) * chunk)
                re = [fold[a, at, lanes] for a in range(n)]
                im = [fold[a, low, lanes] for a in range(n)]
                zero = jnp.zeros_like(re[0])
                for m in range(n):
                    terms = [(1.0, re[0]), ((-1.0) ** m, im[0])]
                    for a in range(1, n):
                        terms.append((math.cos(math.pi * m * a / n), re[a]))
                        terms.append((-math.sin(math.pi * m * a / n), im[a]))
                    value = combine(terms, zero).astype(BF16)
                    obuf[k, m, at, lanes] = value
                    if g == 2:
                        when = lax.broadcasted_iota(jnp.int32, (tile, 1), 0) + (t * tile + m * rows)
                        when = when.astype(F32) * np.float32(1.0 / seq)
                        mixed = rbuf[k, m, at, 0:chunk].astype(F32)
                        filt = rbuf[k, m, at, chunk:2 * chunk].astype(F32)
                        pulled = rbuf[k, m, at, 2 * chunk:3 * chunk].astype(F32)
                        rate_sum = rate_sum + when * value.astype(F32) * filt
                        skip_sum = skip_sum + mixed * pulled
            return rate_sum, skip_sum

        start = jnp.zeros((tile, chunk), F32)
        rate_sum, skip_sum = lax.fori_loop(0, rows // tile, unfold, (start, start))
        mine = pl.ds(pl.multiple_of(k * chunk, chunk), chunk)
        sstat[0:1, mine] = -jnp.sum(rate_sum, axis=0, keepdims=True)
        sstat[1:2, mine] = jnp.sum(skip_sum, axis=0, keepdims=True)

        @pl.loop(0, n - 1)
        def _(o):
            send_out(k, lax.rem(me + 1 + o, n)).start()

        hbuf[k, me] = obuf[k, me]

    for o in range(1, n):
        send_stat(lax.rem(me + o, n)).start()
    gstat[me] = sstat[...]

    @pl.loop(0, steps * n)
    def _(i):
        k, o = i // n, lax.rem(i, n)
        m = lax.rem(me + o, n)

        @pl.when(o > 0)
        def _():
            got_out(k, m).wait_recv()

        cols = columns(m, k)
        conv = hbuf[k, m, :, 0:chunk].astype(F32)
        adjoint = hbuf[k, m, :, chunk:2 * chunk].astype(F32)
        corr = hbuf[k, m, :, 2 * chunk:3 * chunk].astype(F32)
        mixed = sbuf[k, m, :, 0:chunk].astype(F32)
        pulled = sbuf[k, m, :, 2 * chunk:3 * chunk].astype(F32)
        skip = skip_ref[:, cols]
        oq_ref[:, cols] = (go_ref[:, cols].astype(F32) * (conv + skip * mixed)).astype(BF16)
        mixed_grad = adjoint + skip * pulled
        pbuf[k, m] = (mixed_grad * gk_ref[:, cols].astype(F32)).astype(BF16)

        @pl.when(sec > 0)
        def _():
            pass_copy(k, m).start()

        ok_ref[:, cols] = (mixed_grad * vi_ref[:, cols].astype(F32)).astype(BF16)
        envelope = jnp.exp(-rate_ref[:, cols] * here(0, rows))
        of_ref[:, cols] = (corr * envelope).astype(BF16)

    for o in range(1, n):
        got_stat(lax.rem(me + o, n)).wait_recv()
    for m in range(n):
        orate_ref[:, m * width:(m + 1) * width] = gstat[m, 0:1, :]
        oskip_ref[:, m * width:(m + 1) * width] = gstat[m, 1:2, :]

    for o in range(1, n):
        send_stat(lax.rem(me + o, n)).wait_send()

    @pl.loop(0, steps * (n - 1))
    def _(i):
        k, o = i // (n - 1), lax.rem(i, n - 1)
        d = lax.rem(me + 1 + o, n)
        send_in(k, d).wait_send()
        send_out(k, d).wait_send()

    @pl.loop(0, steps * n)
    def _(i):
        k, m = i // n, lax.rem(i, n)

        @pl.when(sec > 0)
        def _():
            pass_copy(k, m).wait_send()

        @pl.when(sec < nsec - 1)
        def _():
            pass_copy(k, m).wait_recv()


def make_local_tables(rows):
    length = 2 * rows
    j = np.arange(rows)[None, :]
    b = np.arange(rows)[:, None]
    angle = 2.0 * np.pi * ((j * b) % length) / length
    re, im = np.cos(angle), -np.sin(angle)
    im[0] = np.cos(np.pi * np.arange(rows))
    weight = np.full((rows, 1), 2.0 / length)
    weight[0] = 1.0 / length
    return np.concatenate([re, im]), np.concatenate([re * weight, im * weight]).T


def split(chunks):
    zero, first = chunks * 6 // 32, chunks // 4
    third = (chunks - zero - first) // 2
    counts = (zero, first, chunks - zero - first - third, third)
    bases = tuple(sum(counts[:o]) for o in range(4))
    return counts, bases, chunks // 16, chunks // 8


def quad_kernel(
    nsec, chunk,
    gq_hbm, gk_hbm, vi_hbm, fr_hbm, go_hbm, rate_hbm, skip_hbm, fwd_hbm, inv_hbm, fwdl_hbm, invl_hbm,
    oq_ref, ok_ref, op_ref, of_ref, orate_ref, oskip_ref,
    gq_ref, gk_ref, vi_ref, fr_ref, go_ref, rate_ref, skip_ref, fwd_ref, inv_ref, fwdl_ref, invl_ref,
    in_sem, row_sem,
    sbuf, rbuf, obuf, hbuf, pbuf, lbuf, relin, relout, part, fold, sown, sloc, gown, gloc,
    i_send, i_recv, ri_send, ri_recv, o_send, o_recv, ro_send, ro_recv, p_send, p_recv,
    t_send, t_recv,
):
    n = 4
    rows, channels = gq_ref.shape
    chunks = channels // chunk
    counts, bases, rin, rout = split(chunks)
    most = max(counts)
    seq = rows * n
    me = lax.axis_index("ctx")
    sec = lax.axis_index("section")
    before = lax.rem(sec + nsec - 1, nsec)
    after = lax.rem(sec + 1, nsec)
    is1 = me * (3 - me) * (2 - me) // 2
    is2 = me * (3 - me) * (me - 1) // 2
    is3 = me * (me - 1) * (me - 2) // 6
    is0 = 1 - is1 - is2 - is3
    own = is0 * counts[0] + is1 * counts[1] + is2 * counts[2] + is3 * counts[3]
    base = is1 * bases[1] + is2 * bases[2] + is3 * bases[3]

    def lanes_of(c):
        return pl.ds(pl.multiple_of(c * chunk, chunk), chunk)

    tokens = (
        (gk_hbm, gk_ref), (vi_hbm, vi_ref), (gq_hbm, gq_ref), (go_hbm, go_ref), (fr_hbm, fr_ref)
    )
    whole = (
        (rate_hbm, rate_ref), (skip_hbm, skip_ref), (fwd_hbm, fwd_ref), (inv_hbm, inv_ref),
        (fwdl_hbm, fwdl_ref), (invl_hbm, invl_ref),
    )

    def load(g, o, rest):
        hbm, ref = tokens[g]
        lo = bases[o] + rest
        hi = bases[o] + counts[o] if rest else lo + 1
        cols = slice(lo * chunk, hi * chunk)
        return pltpu.make_async_copy(hbm.at[:, cols], ref.at[:, cols], in_sem.at[g, rest, o])

    def load_whole(g):
        return pltpu.make_async_copy(whole[g][0], whole[g][1], row_sem.at[g])

    load_whole(0).start()
    for rest in range(2):
        for o in range(n):
            for g in range(5):
                load(g, o, rest).start()
    for g in range(1, 6):
        load_whole(g).start()

    barrier = pltpu.get_barrier_semaphore()
    for o in range(1, n):
        pl.semaphore_signal(
            barrier, inc=1, device_id={"ctx": lax.rem(me + o, n)}, device_id_type=MESH
        )
    for other in (before, after):
        pl.semaphore_signal(barrier, inc=1, device_id={"section": other}, device_id_type=MESH)
    pl.semaphore_wait(barrier, n + 1)
    load_whole(0).wait()

    def to(d):
        return {"ctx": jnp.int32(d)}

    def remote(src, dst, send, recv, where):
        return pltpu.make_async_remote_copy(
            src_ref=src, dst_ref=dst, send_sem=send, recv_sem=recv,
            device_id=where, device_id_type=MESH,
        )

    def give_pair(o, k):
        c = bases[o] + k
        return remote(
            sbuf.at[c, 0:2], rbuf.at[k, 0, 0:2], i_send.at[c], i_recv.at[k, 0], to(o)
        )

    def give_all(o, k):
        c = bases[o] + k
        return remote(sbuf.at[c], rbuf.at[k, me], i_send.at[c], i_recv.at[k, me], to(o))

    def give_relay(k):
        c = bases[1] + k
        return remote(sbuf.at[c], relin.at[k], i_send.at[c], ri_recv.at[k], to(0))

    def forward_in(i):
        return remote(
            relin.at[i], rbuf.at[i, 2], ri_send.at[i], i_recv.at[i, 2], to(1)
        )

    def got_in(k, s):
        at = rbuf.at[k, 0, 0:2] if s == 0 else rbuf.at[k, s]
        src = sbuf.at[0, 0:2] if s == 0 else sbuf.at[0]
        return remote(src, at, i_send.at[0], i_recv.at[k, s], to(s))

    def back_first(k, m):
        return remote(
            obuf.at[k, m, 2], hbuf.at[base + k, 2], o_send.at[k, m, 0], o_recv.at[base + k, 0],
            to(m),
        )

    def back_corr(k):
        return remote(
            obuf.at[k, 0, 1], hbuf.at[base + k, 1], o_send.at[k, 0, 1], o_recv.at[base + k, 1],
            to(0),
        )

    def back_rest(k, m):
        return remote(
            obuf.at[k, m, 0:2], hbuf.at[base + k, 0:2], o_send.at[k, m, 1],
            o_recv.at[base + k, 1], to(m),
        )

    def back_relay(i):
        k = counts[2] - rout + i
        return remote(obuf.at[k, 1, 0:2], relout.at[i], o_send.at[k, 1, 1], ro_recv.at[i], to(0))

    def forward_out(i):
        c = bases[2] + counts[2] - rout + i
        return remote(relout.at[i], hbuf.at[c, 0:2], ro_send.at[i], o_recv.at[c, 1], to(1))

    def got_first(c):
        return remote(
            obuf.at[0, 0, 2], hbuf.at[c, 2], o_send.at[0, 0, 0], o_recv.at[c, 0], to(1)
        )

    def got_corr(c):
        return remote(
            obuf.at[0, 0, 1], hbuf.at[c, 1], o_send.at[0, 0, 1], o_recv.at[c, 1], to(1)
        )

    def got_rest(c):
        return remote(
            obuf.at[0, 0, 0:2], hbuf.at[c, 0:2], o_send.at[0, 0, 1], o_recv.at[c, 1], to(1)
        )

    def stat_own(o, d):
        cols = slice(bases[o] * chunk, (bases[o] + counts[o]) * chunk)
        return remote(
            sown.at[:, cols], gown.at[:, cols], t_send.at[0, d], t_recv.at[0, o], to(d)
        )

    def stat_local(d):
        return remote(sloc, gloc, t_send.at[1, d], t_recv.at[1, 0], to(d))

    def pass_copy(c):
        return remote(
            pbuf.at[c], op_ref.at[:, lanes_of(c)], p_send.at[c], p_recv.at[c],
            {"section": before},
        )

    when = lax.broadcasted_iota(jnp.int32, (rows, 1), 0) + me * rows
    when = when.astype(F32) * np.float32(1.0 / seq)

    @pl.loop(0, most)
    def _(step):
        for o in reversed(range(n)):
            k = step * counts[o] // most

            @pl.when((step + 1) * counts[o] // most > k)
            def _(o=o, k=k):
                for rest in range(2):
                    @pl.when(k == rest)
                    def _():
                        for g in range(5):
                            load(g, o, rest).wait()

                c = bases[o] + k
                cols = lanes_of(c)
                mixed = (gk_ref[:, cols].astype(F32) * vi_ref[:, cols].astype(F32)).astype(BF16)
                pulled = (gq_ref[:, cols].astype(F32) * go_ref[:, cols].astype(F32)).astype(BF16)
                envelope = jnp.exp(-rate_ref[:, cols] * when)
                filt = (fr_ref[:, cols].astype(F32) * envelope).astype(BF16)
                sbuf[c, 0] = mixed
                sbuf[c, 1] = filt
                sbuf[c, 2] = pulled

                @pl.when(me == o)
                def _():
                    rbuf[k, o, 0] = mixed
                    rbuf[k, o, 1] = filt
                    if o:
                        rbuf[k, o, 2] = pulled

                if o:
                    @pl.when(me == 0)
                    def _():
                        give_pair(o, k).start()

                if o == 1:
                    @pl.when(jnp.logical_and(me == 2, k < rin))
                    def _():
                        give_relay(k).start()

                    @pl.when(jnp.logical_or(me == 3, jnp.logical_and(me == 2, k >= rin)))
                    def _():
                        give_all(o, k).start()
                else:
                    @pl.when(jnp.logical_and(me != 0, me != o))
                    def _():
                        give_all(o, k).start()

    @pl.when(sec == nsec - 1)
    def _():
        op_ref[...] = jnp.zeros_like(op_ref)

    for g in range(1, 6):
        load_whole(g).wait()

    tile = 16
    top = lax.broadcasted_iota(jnp.int32, (rows, 1), 0)

    def product(real_pair, ar, ai, br, bi, sign):
        cross = ai * bi
        re = ar * br + jnp.where(real_pair, 0.0, sign * cross)
        im = jnp.where(real_pair, cross, ar * bi - sign * ai * br)
        return re, im

    def products(spec, real_pair):
        mr, fr, pr = (spec[:rows, g * chunk:(g + 1) * chunk] for g in range(3))
        mi, fi, pi = (spec[rows:, g * chunk:(g + 1) * chunk] for g in range(3))
        return (
            product(real_pair, fr, fi, mr, mi, -1.0),
            product(real_pair, fr, fi, pr, pi, 1.0),
            product(real_pair, mr, mi, pr, pi, 1.0),
        )

    @pl.when(me == 0)
    def _():
        @pl.loop(0, chunks)
        def _(c):
            if rin:
                @pl.when(c < rin)
                def _():
                    give_relay(c).wait_recv()
                    forward_in(c).start()

            for g in range(3):
                part[0, 0:rows, g * chunk:(g + 1) * chunk] = sbuf[c, g]
            spec = jnp.dot(fwdl_ref[...], part[0, 0:rows, :], preferred_element_type=F32)
            outs = products(spec, top == 0)
            for g in range(3):
                lanes = slice(g * chunk, (g + 1) * chunk)
                part[1, 0:rows, lanes] = outs[g][0].astype(BF16)
                part[1, rows:2 * rows, lanes] = outs[g][1].astype(BF16)
            back = jnp.dot(invl_ref[...], part[1], preferred_element_type=F32).astype(BF16)
            corr = back[:, 2 * chunk:3 * chunk]
            hbuf[c, 0] = back[:, 0:chunk]
            lbuf[c, 0] = back[:, chunk:2 * chunk]
            lbuf[c, 1] = corr
            rate = when * corr.astype(F32) * sbuf[c, 1].astype(F32)
            skip = sbuf[c, 0].astype(F32) * sbuf[c, 2].astype(F32)
            cols = lanes_of(c)
            sloc[0:1, cols] = -jnp.sum(rate, axis=0, keepdims=True)
            sloc[1:2, cols] = jnp.sum(skip, axis=0, keepdims=True)

        for d in range(1, n):
            stat_local(d).start()
        gloc[...] = sloc[...]

    @pl.loop(0, own)
    def _(k):
        for s in range(n):
            @pl.when(me != s)
            def _():
                got_in(k, s).wait_recv()

        @pl.loop(0, rows // tile)
        def _(t):
            at = pl.ds(pl.multiple_of(t * tile, tile), tile)
            low = pl.ds(pl.multiple_of(rows + t * tile, tile), tile)
            for g in range(3):
                lanes = slice(g * chunk, (g + 1) * chunk)
                held = range(1, n) if g == 2 else range(n)
                x = {m: rbuf[k, m, g, at, :].astype(F32) for m in held}
                even = [m for m in held if m % 2 == 0]
                odd = [m for m in held if m % 2 == 1]
                zero = jnp.zeros_like(x[1])
                e = combine([(1.0, x[m]) for m in even], zero)
                d = combine([(1.0, x[m]) for m in odd], zero)
                part[0, at, lanes] = (e + d).astype(BF16)
                part[0, low, lanes] = (e - d).astype(BF16)
                for a in range(1, n // 2 + 1):
                    cos = [math.cos(math.pi * m * a / n) for m in range(n)]
                    sin = [math.sin(math.pi * m * a / n) for m in range(n)]
                    ce = combine([(cos[m], x[m]) for m in even], zero)
                    co = combine([(cos[m], x[m]) for m in odd], zero)
                    se = combine([(sin[m], x[m]) for m in even], zero)
                    so = combine([(sin[m], x[m]) for m in odd], zero)
                    part[a, at, lanes] = (ce + co).astype(BF16)
                    part[a, low, lanes] = (-se - so).astype(BF16)
                    if n - a != a:
                        part[n - a, at, lanes] = (ce - co).astype(BF16)
                        part[n - a, low, lanes] = (se - so).astype(BF16)

        @pl.loop(0, n)
        def _(a):
            spec = jnp.dot(fwd_ref[a], part[a], preferred_element_type=F32)
            outs = products(spec, jnp.logical_and(top == 0, a == 0))
            for g in range(3):
                lanes = slice(g * chunk, (g + 1) * chunk)
                part[a, 0:rows, lanes] = outs[g][0].astype(BF16)
                part[a, rows:2 * rows, lanes] = outs[g][1].astype(BF16)
            fold[a] = jnp.dot(inv_ref[a], part[a], preferred_element_type=F32)

        def unfold(t, carry):
            rate_sum, skip_sum = carry
            at = pl.ds(pl.multiple_of(t * tile, tile), tile)
            low = pl.ds(pl.multiple_of(rows + t * tile, tile), tile)
            for g in range(3):
                lanes = slice(g * chunk, (g + 1) * chunk)
                re = [fold[a, at, lanes] for a in range(n)]
                im = [fold[a, low, lanes] for a in range(n)]
                zero = jnp.zeros_like(re[0])
                for m in range(1 if g == 0 else 0, n):
                    terms = [(1.0, re[0]), ((-1.0) ** m, im[0])]
                    for a in range(1, n):
                        terms.append((math.cos(math.pi * m * a / n), re[a]))
                        terms.append((-math.sin(math.pi * m * a / n), im[a]))
                    value = combine(terms, zero).astype(BF16)
                    obuf[k, m, (0, 2, 1)[g], at, :] = value
                    if g == 2:
                        pos = lax.broadcasted_iota(jnp.int32, (tile, 1), 0) + (t * tile + m * rows)
                        pos = pos.astype(F32) * np.float32(1.0 / seq)
                        filt = rbuf[k, m, 1, at, :].astype(F32)
                        rate_sum = rate_sum + pos * value.astype(F32) * filt
                        if m:
                            mixed = rbuf[k, m, 0, at, :].astype(F32)
                            pulled = rbuf[k, m, 2, at, :].astype(F32)
                            skip_sum = skip_sum + mixed * pulled
            return rate_sum, skip_sum

        start = jnp.zeros((tile, chunk), F32)
        rate_sum, skip_sum = lax.fori_loop(0, rows // tile, unfold, (start, start))
        mine = lanes_of(base + k)
        sown[0:1, mine] = -jnp.sum(rate_sum, axis=0, keepdims=True)
        sown[1:2, mine] = jnp.sum(skip_sum, axis=0, keepdims=True)

        for m in range(n):
            @pl.when(me != m)
            def _():
                back_first(k, m).start()

        @pl.when(me == 0)
        def _():
            hbuf[base + k, 1:3] = obuf[k, 0, 1:3]

        @pl.when(me != 0)
        def _():
            hbuf[base + k] = obuf[k, me]

    for o in range(n):
        @pl.when(me == o)
        def _():
            cols = slice(bases[o] * chunk, (bases[o] + counts[o]) * chunk)
            for d in range(n):
                if d != o:
                    stat_own(o, d).start()
            gown[:, cols] = sown[:, cols]

    @pl.when(me == 2)
    def _():
        @pl.loop(0, rout)
        def _(i):
            back_relay(i).start()

    @pl.loop(0, own)
    def _(k):
        @pl.when(me != 0)
        def _():
            back_corr(k).start()

        direct = jnp.logical_or(me != 2, k < counts[2] - rout)

        @pl.when(jnp.logical_and(me != 1, direct))
        def _():
            back_rest(k, 1).start()

        for m in range(2, n):
            @pl.when(me != m)
            def _():
                back_rest(k, m).start()

    @pl.loop(0, most)
    def _(k):
        for o in range(n):
            @pl.when(k < counts[o])
            def _():
                if o:
                    @pl.when(me == 0)
                    def _():
                        give_pair(o, k).wait_send()

                @pl.when(jnp.logical_and(me != 0, me != o))
                def _():
                    give_all(o, k).wait_send()

    @pl.loop(0, most)
    def _(step):
        @pl.when(jnp.logical_and(me == 0, step >= most - rout))
        def _():
            back_relay(step - (most - rout)).wait_recv()
            forward_out(step - (most - rout)).start()

        for o in range(n):
            k = step * counts[o] // most

            @pl.when((step + 1) * counts[o] // most > k)
            def _(o=o, k=k):
                c = bases[o] + k

                @pl.when(me != o)
                def _():
                    got_first(c).wait_recv()

                @pl.when(me == 0)
                def _():
                    both = hbuf[c, 2].astype(F32) + lbuf[c, 0].astype(F32)
                    hbuf[c, 2] = both.astype(BF16)

                cols = lanes_of(c)
                pulled = sbuf[c, 2].astype(F32)
                mixed_grad = hbuf[c, 2].astype(F32) + skip_ref[:, cols] * pulled
                pbuf[c] = (mixed_grad * gk_ref[:, cols].astype(F32)).astype(BF16)

                @pl.when(sec > 0)
                def _():
                    pass_copy(c).start()

                ok_ref[:, cols] = (mixed_grad * vi_ref[:, cols].astype(F32)).astype(BF16)

    @pl.when(me != 0)
    def _():
        stat_local(1).wait_recv()

    for o in range(n):
        @pl.when(me != o)
        def _():
            stat_own(o, 0).wait_recv()
    orate_ref[...] = gown[0:1, :] + gloc[0:1, :]
    oskip_ref[...] = gown[1:2, :] + gloc[1:2, :]

    for d in range(1, n):
        @pl.when(me == 0)
        def _():
            stat_local(d).wait_send()
    for o in range(n):
        @pl.when(me == o)
        def _():
            for d in range(n):
                if d != o:
                    stat_own(o, d).wait_send()

    @pl.loop(0, own)
    def _(k):
        for m in range(n):
            @pl.when(me != m)
            def _():
                back_first(k, m).wait_send()

    @pl.loop(0, most)
    def _(step):
        for o in range(n):
            k = step * counts[o] // most

            @pl.when((step + 1) * counts[o] // most > k)
            def _(o=o, k=k):
                c = bases[o] + k

                @pl.when(me == 0)
                def _():
                    if o:
                        got_corr(c).wait_recv()
                    both = hbuf[c, 1].astype(F32) + lbuf[c, 1].astype(F32)
                    hbuf[c, 1] = both.astype(BF16)

                @pl.when(jnp.logical_and(me != 0, me != o))
                def _():
                    got_rest(c).wait_recv()

                cols = lanes_of(c)
                conv = hbuf[c, 0].astype(F32)
                mixed = sbuf[c, 0].astype(F32)
                oq_ref[:, cols] = (
                    go_ref[:, cols].astype(F32) * (conv + skip_ref[:, cols] * mixed)
                ).astype(BF16)
                envelope = jnp.exp(-rate_ref[:, cols] * when)
                of_ref[:, cols] = (hbuf[c, 1].astype(F32) * envelope).astype(BF16)

                @pl.when(sec > 0)
                def _():
                    pass_copy(c).wait_send()

                @pl.when(sec < nsec - 1)
                def _():
                    pass_copy(c).wait_recv()

    @pl.loop(0, own)
    def _(k):
        for m in range(n):
            @pl.when(me != m)
            def _():
                (back_rest(k, m) if m else back_corr(k)).wait_send()

    @pl.when(me == 0)
    def _():
        for i in range(rin):
            forward_in(i).wait_send()

        @pl.loop(0, rout)
        def _(k):
            forward_out(k).wait_send()


def quad_call(nsec, shapes, chunk, args, decay_rate, skip_gain):
    rows, channels = shapes[0].shape
    chunks = channels // chunk
    counts, _, rin, rout = split(chunks)
    most = max(counts)
    tables = (*make_tables(4, rows), *make_local_tables(rows))
    tables = tuple(jnp.asarray(table, BF16) for table in tables)
    dma = pltpu.SemaphoreType.DMA
    block = pltpu.VMEM((rows, channels), BF16)
    row = pltpu.VMEM((1, channels), F32)
    stat = pltpu.VMEM((2, channels), F32)
    return pl.pallas_call(
        functools.partial(quad_kernel, nsec, chunk),
        out_shape=tuple(pltpu.VMEM(shape.shape, shape.dtype) for shape in shapes),
        in_specs=[pl.BlockSpec(memory_space=pl.ANY)] * 11,
        out_specs=(pl.BlockSpec(memory_space=pltpu.VMEM),) * 6,
        scratch_shapes=[
            *([block] * 5), row, row, *(pltpu.VMEM(table.shape, BF16) for table in tables),
            dma((5, 2, 4)), dma((6,)),
            pltpu.VMEM((chunks, 3, rows, chunk), BF16),
            pltpu.VMEM((most, 4, 3, rows, chunk), BF16),
            pltpu.VMEM((most, 4, 3, rows, chunk), BF16),
            pltpu.VMEM((chunks, 3, rows, chunk), BF16),
            pltpu.VMEM((chunks, rows, chunk), BF16),
            pltpu.VMEM((chunks, 2, rows, chunk), BF16),
            pltpu.VMEM((max(rin, 1), 3, rows, chunk), BF16),
            pltpu.VMEM((rout, 2, rows, chunk), BF16),
            pltpu.VMEM((4, 2 * rows, 3 * chunk), BF16),
            pltpu.VMEM((4, 2 * rows, 3 * chunk), F32),
            stat, stat, stat, stat,
            dma((chunks,)), dma((most, 4)), dma((max(rin, 1),)), dma((max(rin, 1),)),
            dma((most, 4, 2)), dma((chunks, 2)), dma((rout,)), dma((rout,)),
            dma((chunks,)), dma((chunks,)), dma((2, 4)), dma((2, 4)),
        ],
        compiler_params=pltpu.CompilerParams(
            collective_id=0, has_side_effects=True, vmem_limit_bytes=58 * 1024 * 1024
        ),
        name="hyena_backward_quad",
    )(*args, decay_rate, skip_gain, *tables)


def finish(*refs):
    count = (len(refs) - 1) // 2
    sem = refs[-1]
    copies = [
        pltpu.make_async_copy(refs[g], refs[count + g], sem.at[g]) for g in range(count)
    ]
    for copy in copies:
        copy.start()
    for copy in copies:
        copy.wait()


def general_call(n, nsec, shapes, chunk, args, decay_rate, skip_gain):
    rows, channels = shapes[0].shape
    width = channels // n
    steps = width // chunk
    fwd, inv = make_tables(n, rows)
    fwd, inv = jnp.asarray(fwd, BF16), jnp.asarray(inv, BF16)
    message = (steps, n, rows, 3 * chunk)
    dma = pltpu.SemaphoreType.DMA
    anywhere = pl.BlockSpec(memory_space=pl.ANY)
    inside = pl.BlockSpec(memory_space=pltpu.VMEM)
    return pl.pallas_call(
        functools.partial(kernel, n, nsec, chunk, steps),
        out_shape=tuple(pltpu.VMEM(shape.shape, shape.dtype) for shape in shapes),
        in_specs=[anywhere] * 9,
        out_specs=(inside,) * 6,
        scratch_shapes=[
            *([pltpu.VMEM((rows, channels), BF16)] * 5),
            *([pltpu.VMEM((1, channels), F32)] * 2),
            *([pltpu.VMEM(fwd.shape, BF16)] * 2),
            dma((5, 2, n)), dma((4,)),
            pltpu.VMEM(message, BF16),
            pltpu.VMEM(message, BF16),
            pltpu.VMEM(message, BF16),
            pltpu.VMEM(message, BF16),
            pltpu.VMEM((steps, n, rows, chunk), BF16),
            pltpu.VMEM((n, 2 * rows, 3 * chunk), BF16),
            pltpu.VMEM((n, 2 * rows, 3 * chunk), F32),
            pltpu.VMEM((2, width), F32),
            pltpu.VMEM((n, 2, width), F32),
            dma((steps, n)), dma((steps, n)), dma((steps, n)), dma((steps, n)),
            dma((steps, n)), dma((steps, n)), dma((n,)), dma((n,)),
        ],
        compiler_params=pltpu.CompilerParams(
            collective_id=0, has_side_effects=True, vmem_limit_bytes=58 * 1024 * 1024
        ),
        name="hyena_backward",
    )(
        *args, decay_rate, skip_gain, fwd, inv,
    )


def shards(n, nsec, gate_q, gate_k, value_in, filter_raw, decay_rate, skip_gain, grad_out):
    rows, channels = gate_q.shape[1:]
    block = jax.ShapeDtypeStruct((rows, channels), BF16)
    row = jax.ShapeDtypeStruct((1, channels), F32)
    dma = pltpu.SemaphoreType.DMA
    anywhere = pl.BlockSpec(memory_space=pl.ANY)
    inside = pl.BlockSpec(memory_space=pltpu.VMEM)
    shapes = (block, block, block, block, row, row)
    args = (gate_q[0], gate_k[0], value_in[0], filter_raw[0], grad_out[0])
    call = quad_call if n == 4 and channels >= 16 * 128 else functools.partial(general_call, n)
    outs = call(nsec, shapes, 128, args, decay_rate, skip_gain)
    oq, ok, op, of, orate, oskip = pl.pallas_call(
        finish,
        out_shape=shapes,
        in_specs=[inside] * 6,
        out_specs=(anywhere,) * 6,
        scratch_shapes=[dma((6,))],
        compiler_params=pltpu.CompilerParams(vmem_limit_bytes=4 * 1024 * 1024),
        name="hand_over",
    )(*(pltpu.with_memory_space_constraint(out, pltpu.VMEM) for out in outs))
    return oq[None], ok[None], op[None], of[None], orate, oskip


def solution(mesh):
    n, nsec = mesh.shape["ctx"], mesh.shape["section"]
    tokens = P("section", "ctx", None)
    return jax.shard_map(
        functools.partial(shards, n, nsec),
        mesh=mesh,
        in_specs=(tokens, tokens, tokens, tokens, P("section", None), P("section", None), tokens),
        out_specs=(tokens, tokens, tokens, tokens, P("section", None), P("section", None)),
        check_vma=False,
    )
```

```python
import functools
import math

import jax
import jax.numpy as jnp
import numpy as np
from jax import lax
from jax.experimental import pallas as pl
from jax.experimental.pallas import tpu as pltpu
from jax.sharding import PartitionSpec as P

MESH = pl.DeviceIdType.MESH
F32 = jnp.float32
BF16 = jnp.bfloat16


def make_tables(n, rows):
    length = 2 * n * rows
    half = rows // 2
    j = np.arange(rows)[None, :]
    b = np.arange(rows)[:, None]

    def angle(a):
        return 2.0 * np.pi * ((j * (a + 2 * n * b)) % length) / length

    fwd = np.zeros((n, 2 * rows, 2 * rows))
    inv = np.zeros((n, 2 * rows, 2 * rows))
    for a in range(1, n):
        c, s = np.cos(angle(a)), np.sin(angle(a))
        fwd[a] = np.block([[c, s], [-s, c]])
        inv[a] = np.block([[c.T, -s.T], [s.T, c.T]]) * (2.0 / length)
    for slot, a in ((0, 0), (1, n)):
        c, s = np.cos(angle(a))[:half], np.sin(angle(a))[:half]
        weight = np.full((half, 1), 2.0 / length)
        re_rows = slice(slot * half, (slot + 1) * half)
        im_rows = slice(rows + slot * half, rows + (slot + 1) * half)
        cols = slice(slot * rows, (slot + 1) * rows)
        im = -s
        if slot == 0:
            im = im.copy()
            im[0] = np.cos(np.pi * np.arange(rows))
            weight[0] = 1.0 / length
        fwd[0, re_rows, cols] = c
        fwd[0, im_rows, cols] = im
        inv[0, cols, re_rows] = (c * weight).T
        inv[0, cols, im_rows] = (im * weight).T
    return fwd, inv


def scaled(coef, x):
    if abs(coef - 1.0) < 1e-12:
        return x
    if abs(coef + 1.0) < 1e-12:
        return -x
    return x * np.float32(coef)


def combine(terms, zero):
    total = None
    for coef, x in terms:
        if abs(coef) < 1e-12:
            continue
        if total is None:
            total = scaled(coef, x)
        elif coef < 0:
            total = total - scaled(-coef, x)
        else:
            total = total + scaled(coef, x)
    return zero if total is None else total


def kernel(
    n, nsec, chunk, steps,
    gq_hbm, gk_hbm, vi_hbm, fr_hbm, go_hbm, rate_hbm, skip_hbm, fwd_hbm, inv_hbm,
    oq_ref, ok_ref, op_ref, of_ref, orate_ref, oskip_ref,
    gq_ref, gk_ref, vi_ref, fr_ref, go_ref, rate_ref, skip_ref, fwd_ref, inv_ref,
    in_sem, row_sem,
    sbuf, rbuf, obuf, hbuf, pbuf, part, fold, sstat, gstat,
    s_send, s_recv, o_send, o_recv, p_send, p_recv, t_send, t_recv,
):
    rows = gq_ref.shape[0]
    width = chunk * steps
    seq = rows * n
    me = lax.axis_index("ctx")
    sec = lax.axis_index("section")
    before = lax.rem(sec + nsec - 1, nsec)
    after = lax.rem(sec + 1, nsec)

    def columns(owner, k):
        return pl.ds(pl.multiple_of(owner * width + k * chunk, chunk), chunk)

    tokens = (
        (gk_hbm, gk_ref), (vi_hbm, vi_ref), (gq_hbm, gq_ref), (go_hbm, go_ref), (fr_hbm, fr_ref)
    )
    whole = (
        (rate_hbm, rate_ref), (skip_hbm, skip_ref), (fwd_hbm, fwd_ref), (inv_hbm, inv_ref)
    )

    def load_first(g, d):
        hbm, ref = tokens[g]
        return pltpu.make_async_copy(
            hbm.at[:, columns(d, 0)], ref.at[:, columns(d, 0)], in_sem.at[g, 0, d]
        )

    def load_rest(g, d):
        hbm, ref = tokens[g]
        cols = pl.ds(pl.multiple_of(d * width + chunk, chunk), width - chunk)
        return pltpu.make_async_copy(hbm.at[:, cols], ref.at[:, cols], in_sem.at[g, 1, d])

    def load_whole(g):
        return pltpu.make_async_copy(whole[g][0], whole[g][1], row_sem.at[g])

    load_whole(0).start()
    for o in range(n):
        for g in range(5):
            load_first(g, lax.rem(me + 1 + o, n)).start()
    if steps > 1:
        for d in range(n):
            for g in range(5):
                load_rest(g, d).start()
    for g in range(1, 4):
        load_whole(g).start()

    barrier = pltpu.get_barrier_semaphore()
    for o in range(1, n):
        pl.semaphore_signal(
            barrier, inc=1, device_id={"ctx": lax.rem(me + o, n)}, device_id_type=MESH
        )
    for other in (before, after):
        pl.semaphore_signal(barrier, inc=1, device_id={"section": other}, device_id_type=MESH)
    pl.semaphore_wait(barrier, n + 1)
    load_whole(0).wait()

    def here(row0, count):
        row = lax.broadcasted_iota(jnp.int32, (count, 1), 0) + (row0 + me * rows)
        return row.astype(F32) * np.float32(1.0 / seq)

    def send_in(k, d):
        return pltpu.make_async_remote_copy(
            src_ref=sbuf.at[k, d], dst_ref=rbuf.at[k, me], send_sem=s_send.at[k, d],
            recv_sem=s_recv.at[k, me], device_id={"ctx": d}, device_id_type=MESH,
        )

    def got_in(k, m):
        return pltpu.make_async_remote_copy(
            src_ref=sbuf.at[k, m], dst_ref=rbuf.at[k, m], send_sem=s_send.at[k, m],
            recv_sem=s_recv.at[k, m], device_id={"ctx": m}, device_id_type=MESH,
        )

    def send_out(k, m):
        return pltpu.make_async_remote_copy(
            src_ref=obuf.at[k, m], dst_ref=hbuf.at[k, me], send_sem=o_send.at[k, m],
            recv_sem=o_recv.at[k, me], device_id={"ctx": m}, device_id_type=MESH,
        )

    def got_out(k, m):
        return pltpu.make_async_remote_copy(
            src_ref=obuf.at[k, m], dst_ref=hbuf.at[k, m], send_sem=o_send.at[k, m],
            recv_sem=o_recv.at[k, m], device_id={"ctx": m}, device_id_type=MESH,
        )

    def send_stat(d):
        return pltpu.make_async_remote_copy(
            src_ref=sstat, dst_ref=gstat.at[me], send_sem=t_send.at[d],
            recv_sem=t_recv.at[me], device_id={"ctx": d}, device_id_type=MESH,
        )

    def got_stat(m):
        return pltpu.make_async_remote_copy(
            src_ref=sstat, dst_ref=gstat.at[m], send_sem=t_send.at[m],
            recv_sem=t_recv.at[m], device_id={"ctx": m}, device_id_type=MESH,
        )

    def pass_copy(k, m):
        return pltpu.make_async_remote_copy(
            src_ref=pbuf.at[k, m], dst_ref=op_ref.at[:, columns(m, k)], send_sem=p_send.at[k, m],
            recv_sem=p_recv.at[k, m], device_id={"section": before}, device_id_type=MESH,
        )

    @pl.loop(0, steps * n)
    def _(i):
        k, o = i // n, lax.rem(i, n)
        d = lax.rem(me + 1 + o, n)
        cols = columns(d, k)

        @pl.when(k == 0)
        def _():
            for g in range(5):
                load_first(g, d).wait()

        if steps > 1:
            @pl.when(k == 1)
            def _():
                for g in range(5):
                    load_rest(g, d).wait()

        mixed = (gk_ref[:, cols].astype(F32) * vi_ref[:, cols].astype(F32)).astype(BF16)
        pulled = (gq_ref[:, cols].astype(F32) * go_ref[:, cols].astype(F32)).astype(BF16)
        envelope = jnp.exp(-rate_ref[:, cols] * here(0, rows))
        filt = (fr_ref[:, cols].astype(F32) * envelope).astype(BF16)
        sbuf[k, d, :, 0:chunk] = mixed
        sbuf[k, d, :, chunk:2 * chunk] = filt
        sbuf[k, d, :, 2 * chunk:3 * chunk] = pulled

        @pl.when(o < n - 1)
        def _():
            send_in(k, d).start()

        @pl.when(o == n - 1)
        def _():
            rbuf[k, me, :, 0:chunk] = mixed
            rbuf[k, me, :, chunk:2 * chunk] = filt
            rbuf[k, me, :, 2 * chunk:3 * chunk] = pulled

    @pl.when(sec == nsec - 1)
    def _():
        op_ref[...] = jnp.zeros_like(op_ref)

    for g in range(1, 4):
        load_whole(g).wait()

    tile = 16
    top = lax.broadcasted_iota(jnp.int32, (rows, 1), 0)

    @pl.loop(0, steps)
    def _(k):
        @pl.loop(0, n - 1)
        def _(o):
            got_in(k, lax.rem(me + 1 + o, n)).wait_recv()

        @pl.loop(0, rows // tile)
        def _(t):
            at = pl.ds(pl.multiple_of(t * tile, tile), tile)
            low = pl.ds(pl.multiple_of(rows + t * tile, tile), tile)
            for g in range(3):
                lanes = slice(g * chunk, (g + 1) * chunk)
                x = [rbuf[k, m, at, lanes].astype(F32) for m in range(n)]
                zero = jnp.zeros_like(x[0])
                even = combine([(1.0, x[m]) for m in range(0, n, 2)], zero)
                odd = combine([(1.0, x[m]) for m in range(1, n, 2)], zero)
                part[0, at, lanes] = (even + odd).astype(BF16)
                part[0, low, lanes] = (even - odd).astype(BF16)
                for a in range(1, n // 2 + 1):
                    cos = [math.cos(math.pi * m * a / n) for m in range(n)]
                    sin = [math.sin(math.pi * m * a / n) for m in range(n)]
                    ce = combine([(cos[m], x[m]) for m in range(0, n, 2)], zero)
                    co = combine([(cos[m], x[m]) for m in range(1, n, 2)], zero)
                    se = combine([(sin[m], x[m]) for m in range(0, n, 2)], zero)
                    so = combine([(sin[m], x[m]) for m in range(1, n, 2)], zero)
                    part[a, at, lanes] = (ce + co).astype(BF16)
                    part[a, low, lanes] = (-se - so).astype(BF16)
                    if n - a != a:
                        part[n - a, at, lanes] = (ce - co).astype(BF16)
                        part[n - a, low, lanes] = (se - so).astype(BF16)

        @pl.loop(0, n)
        def _(a):
            spec = jnp.dot(fwd_ref[a], part[a], preferred_element_type=F32)
            mr, fr, pr = (spec[:rows, g * chunk:(g + 1) * chunk] for g in range(3))
            mi, fi, pi = (spec[rows:, g * chunk:(g + 1) * chunk] for g in range(3))
            real_pair = jnp.logical_and(top == 0, a == 0)

            def product(ar, ai, br, bi, sign):
                cross = ai * bi
                re = ar * br + jnp.where(real_pair, 0.0, sign * cross)
                im = jnp.where(real_pair, cross, ar * bi - sign * ai * br)
                return re, im

            outs = (
                product(fr, fi, mr, mi, -1.0),
                product(fr, fi, pr, pi, 1.0),
                product(mr, mi, pr, pi, 1.0),
            )
            for g in range(3):
                lanes = slice(g * chunk, (g + 1) * chunk)
                part[a, 0:rows, lanes] = outs[g][0].astype(BF16)
                part[a, rows:2 * rows, lanes] = outs[g][1].astype(BF16)
            fold[a] = jnp.dot(inv_ref[a], part[a], preferred_element_type=F32)

        def unfold(t, carry):
            rate_sum, skip_sum = carry
            at = pl.ds(pl.multiple_of(t * tile, tile), tile)
            low = pl.ds(pl.multiple_of(rows + t * tile, tile), tile)
            for g in range(3):
                lanes = slice(g * chunk, (g + 1) * chunk)
                re = [fold[a, at, lanes] for a in range(n)]
                im = [fold[a, low, lanes] for a in range(n)]
                zero = jnp.zeros_like(re[0])
                for m in range(n):
                    terms = [(1.0, re[0]), ((-1.0) ** m, im[0])]
                    for a in range(1, n):
                        terms.append((math.cos(math.pi * m * a / n), re[a]))
                        terms.append((-math.sin(math.pi * m * a / n), im[a]))
                    value = combine(terms, zero).astype(BF16)
                    obuf[k, m, at, lanes] = value
                    if g == 2:
                        when = lax.broadcasted_iota(jnp.int32, (tile, 1), 0) + (t * tile + m * rows)
                        when = when.astype(F32) * np.float32(1.0 / seq)
                        mixed = rbuf[k, m, at, 0:chunk].astype(F32)
                        filt = rbuf[k, m, at, chunk:2 * chunk].astype(F32)
                        pulled = rbuf[k, m, at, 2 * chunk:3 * chunk].astype(F32)
                        rate_sum = rate_sum + when * value.astype(F32) * filt
                        skip_sum = skip_sum + mixed * pulled
            return rate_sum, skip_sum

        start = jnp.zeros((tile, chunk), F32)
        rate_sum, skip_sum = lax.fori_loop(0, rows // tile, unfold, (start, start))
        mine = pl.ds(pl.multiple_of(k * chunk, chunk), chunk)
        sstat[0:1, mine] = -jnp.sum(rate_sum, axis=0, keepdims=True)
        sstat[1:2, mine] = jnp.sum(skip_sum, axis=0, keepdims=True)

        @pl.loop(0, n - 1)
        def _(o):
            send_out(k, lax.rem(me + 1 + o, n)).start()

        hbuf[k, me] = obuf[k, me]

    for o in range(1, n):
        send_stat(lax.rem(me + o, n)).start()
    gstat[me] = sstat[...]

    @pl.loop(0, steps * n)
    def _(i):
        k, o = i // n, lax.rem(i, n)
        m = lax.rem(me + o, n)

        @pl.when(o > 0)
        def _():
            got_out(k, m).wait_recv()

        cols = columns(m, k)
        conv = hbuf[k, m, :, 0:chunk].astype(F32)
        adjoint = hbuf[k, m, :, chunk:2 * chunk].astype(F32)
        corr = hbuf[k, m, :, 2 * chunk:3 * chunk].astype(F32)
        mixed = sbuf[k, m, :, 0:chunk].astype(F32)
        pulled = sbuf[k, m, :, 2 * chunk:3 * chunk].astype(F32)
        skip = skip_ref[:, cols]
        oq_ref[:, cols] = (go_ref[:, cols].astype(F32) * (conv + skip * mixed)).astype(BF16)
        mixed_grad = adjoint + skip * pulled
        pbuf[k, m] = (mixed_grad * gk_ref[:, cols].astype(F32)).astype(BF16)

        @pl.when(sec > 0)
        def _():
            pass_copy(k, m).start()

        ok_ref[:, cols] = (mixed_grad * vi_ref[:, cols].astype(F32)).astype(BF16)
        envelope = jnp.exp(-rate_ref[:, cols] * here(0, rows))
        of_ref[:, cols] = (corr * envelope).astype(BF16)

    for o in range(1, n):
        got_stat(lax.rem(me + o, n)).wait_recv()
    for m in range(n):
        orate_ref[:, m * width:(m + 1) * width] = gstat[m, 0:1, :]
        oskip_ref[:, m * width:(m + 1) * width] = gstat[m, 1:2, :]

    for o in range(1, n):
        send_stat(lax.rem(me + o, n)).wait_send()

    @pl.loop(0, steps * (n - 1))
    def _(i):
        k, o = i // (n - 1), lax.rem(i, n - 1)
        d = lax.rem(me + 1 + o, n)
        send_in(k, d).wait_send()
        send_out(k, d).wait_send()

    @pl.loop(0, steps * n)
    def _(i):
        k, m = i // n, lax.rem(i, n)

        @pl.when(sec > 0)
        def _():
            pass_copy(k, m).wait_send()

        @pl.when(sec < nsec - 1)
        def _():
            pass_copy(k, m).wait_recv()


def make_local_tables(rows):
    length = 2 * rows
    j = np.arange(rows)[None, :]
    b = np.arange(rows)[:, None]
    angle = 2.0 * np.pi * ((j * b) % length) / length
    re, im = np.cos(angle), -np.sin(angle)
    im[0] = np.cos(np.pi * np.arange(rows))
    weight = np.full((rows, 1), 2.0 / length)
    weight[0] = 1.0 / length
    return np.concatenate([re, im]), np.concatenate([re * weight, im * weight]).T


def split(chunks):
    zero, first = chunks * 6 // 32, chunks // 4
    third = (chunks - zero - first) // 2
    counts = (zero, first, chunks - zero - first - third, third)
    bases = tuple(sum(counts[:o]) for o in range(4))
    return counts, bases, chunks // 16, chunks // 8


def quad_kernel(
    nsec, chunk,
    gq_hbm, gk_hbm, vi_hbm, fr_hbm, go_hbm, rate_hbm, skip_hbm, fwd_hbm, inv_hbm, fwdl_hbm, invl_hbm,
    oq_ref, ok_ref, op_ref, of_ref, orate_ref, oskip_ref,
    gq_ref, gk_ref, vi_ref, fr_ref, go_ref, rate_ref, skip_ref, fwd_ref, inv_ref, fwdl_ref, invl_ref,
    in_sem, row_sem,
    sbuf, rbuf, obuf, hbuf, pbuf, lbuf, relin, relout, part, fold, sown, sloc, gown, gloc,
    i_send, i_recv, ri_send, ri_recv, o_send, o_recv, ro_send, ro_recv, p_send, p_recv,
    t_send, t_recv,
):
    n = 4
    rows, channels = gq_ref.shape
    chunks = channels // chunk
    counts, bases, rin, rout = split(chunks)
    most = max(counts)
    seq = rows * n
    me = lax.axis_index("ctx")
    sec = lax.axis_index("section")
    before = lax.rem(sec + nsec - 1, nsec)
    after = lax.rem(sec + 1, nsec)
    is1 = me * (3 - me) * (2 - me) // 2
    is2 = me * (3 - me) * (me - 1) // 2
    is3 = me * (me - 1) * (me - 2) // 6
    is0 = 1 - is1 - is2 - is3
    own = is0 * counts[0] + is1 * counts[1] + is2 * counts[2] + is3 * counts[3]
    base = is1 * bases[1] + is2 * bases[2] + is3 * bases[3]

    def lanes_of(c):
        return pl.ds(pl.multiple_of(c * chunk, chunk), chunk)

    tokens = (
        (gk_hbm, gk_ref), (vi_hbm, vi_ref), (gq_hbm, gq_ref), (go_hbm, go_ref), (fr_hbm, fr_ref)
    )
    whole = (
        (rate_hbm, rate_ref), (skip_hbm, skip_ref), (fwd_hbm, fwd_ref), (inv_hbm, inv_ref),
        (fwdl_hbm, fwdl_ref), (invl_hbm, invl_ref),
    )

    def load(g, o, rest):
        hbm, ref = tokens[g]
        lo = bases[o] + rest
        hi = bases[o] + counts[o] if rest else lo + 1
        cols = slice(lo * chunk, hi * chunk)
        return pltpu.make_async_copy(hbm.at[:, cols], ref.at[:, cols], in_sem.at[g, rest, o])

    def load_whole(g):
        return pltpu.make_async_copy(whole[g][0], whole[g][1], row_sem.at[g])

    load_whole(0).start()
    for rest in range(2):
        for o in reversed(range(n)):
            for g in range(5):
                load(g, o, rest).start()
    for g in range(1, 6):
        load_whole(g).start()

    barrier = pltpu.get_barrier_semaphore()
    for o in range(1, n):
        pl.semaphore_signal(
            barrier, inc=1, device_id={"ctx": lax.rem(me + o, n)}, device_id_type=MESH
        )
    for other in (before, after):
        pl.semaphore_signal(barrier, inc=1, device_id={"section": other}, device_id_type=MESH)
    pl.semaphore_wait(barrier, n + 1)
    load_whole(0).wait()

    def to(d):
        return {"ctx": jnp.int32(d)}

    def remote(src, dst, send, recv, where):
        return pltpu.make_async_remote_copy(
            src_ref=src, dst_ref=dst, send_sem=send, recv_sem=recv,
            device_id=where, device_id_type=MESH,
        )

    def give_pair(o, k):
        c = bases[o] + k
        return remote(
            sbuf.at[c, 0:2], rbuf.at[k, 0, 0:2], i_send.at[c], i_recv.at[k, 0], to(o)
        )

    def give_all(o, k):
        c = bases[o] + k
        return remote(sbuf.at[c], rbuf.at[k, me], i_send.at[c], i_recv.at[k, me], to(o))

    def give_relay(k):
        c = bases[1] + k
        return remote(sbuf.at[c], relin.at[k], i_send.at[c], ri_recv.at[k], to(0))

    def forward_in(i):
        return remote(
            relin.at[i], rbuf.at[i, 2], ri_send.at[i], i_recv.at[i, 2], to(1)
        )

    def got_in(k, s):
        at = rbuf.at[k, 0, 0:2] if s == 0 else rbuf.at[k, s]
        src = sbuf.at[0, 0:2] if s == 0 else sbuf.at[0]
        return remote(src, at, i_send.at[0], i_recv.at[k, s], to(s))

    def back_first(k, m):
        return remote(
            obuf.at[k, m, 2], hbuf.at[base + k, 2], o_send.at[k, m, 0], o_recv.at[base + k, 0],
            to(m),
        )

    def back_corr(k):
        return remote(
            obuf.at[k, 0, 1], hbuf.at[base + k, 1], o_send.at[k, 0, 1], o_recv.at[base + k, 1],
            to(0),
        )

    def back_rest(k, m):
        return remote(
            obuf.at[k, m, 0:2], hbuf.at[base + k, 0:2], o_send.at[k, m, 1],
            o_recv.at[base + k, 1], to(m),
        )

    def back_relay(i):
        k = counts[2] - rout + i
        return remote(obuf.at[k, 1, 0:2], relout.at[i], o_send.at[k, 1, 1], ro_recv.at[i], to(0))

    def forward_out(i):
        c = bases[2] + counts[2] - rout + i
        return remote(relout.at[i], hbuf.at[c, 0:2], ro_send.at[i], o_recv.at[c, 1], to(1))

    def got_first(c):
        return remote(
            obuf.at[0, 0, 2], hbuf.at[c, 2], o_send.at[0, 0, 0], o_recv.at[c, 0], to(1)
        )

    def got_corr(c):
        return remote(
            obuf.at[0, 0, 1], hbuf.at[c, 1], o_send.at[0, 0, 1], o_recv.at[c, 1], to(1)
        )

    def got_rest(c):
        return remote(
            obuf.at[0, 0, 0:2], hbuf.at[c, 0:2], o_send.at[0, 0, 1], o_recv.at[c, 1], to(1)
        )

    def stat_own(o, d):
        cols = slice(bases[o] * chunk, (bases[o] + counts[o]) * chunk)
        return remote(
            sown.at[:, cols], gown.at[:, cols], t_send.at[0, d], t_recv.at[0, o], to(d)
        )

    def stat_local(d):
        return remote(sloc, gloc, t_send.at[1, d], t_recv.at[1, 0], to(d))

    def pass_copy(c):
        return remote(
            pbuf.at[c], op_ref.at[:, lanes_of(c)], p_send.at[c], p_recv.at[c],
            {"section": before},
        )

    when = lax.broadcasted_iota(jnp.int32, (rows, 1), 0) + me * rows
    when = when.astype(F32) * np.float32(1.0 / seq)

    @pl.loop(0, most)
    def _(step):
        for o in reversed(range(n)):
            k = step * counts[o] // most

            @pl.when((step + 1) * counts[o] // most > k)
            def _(o=o, k=k):
                for rest in range(2):
                    @pl.when(k == rest)
                    def _():
                        for g in range(5):
                            load(g, o, rest).wait()

                c = bases[o] + k
                cols = lanes_of(c)
                mixed = (gk_ref[:, cols].astype(F32) * vi_ref[:, cols].astype(F32)).astype(BF16)
                pulled = (gq_ref[:, cols].astype(F32) * go_ref[:, cols].astype(F32)).astype(BF16)
                envelope = jnp.exp(-rate_ref[:, cols] * when)
                filt = (fr_ref[:, cols].astype(F32) * envelope).astype(BF16)
                sbuf[c, 0] = mixed
                sbuf[c, 1] = filt
                sbuf[c, 2] = pulled

                @pl.when(me == o)
                def _():
                    rbuf[k, o, 0] = mixed
                    rbuf[k, o, 1] = filt
                    if o:
                        rbuf[k, o, 2] = pulled

                if o:
                    @pl.when(me == 0)
                    def _():
                        give_pair(o, k).start()

                if o == 1:
                    @pl.when(jnp.logical_and(me == 2, k < rin))
                    def _():
                        give_relay(k).start()

                    @pl.when(jnp.logical_or(me == 3, jnp.logical_and(me == 2, k >= rin)))
                    def _():
                        give_all(o, k).start()
                else:
                    @pl.when(jnp.logical_and(me != 0, me != o))
                    def _():
                        give_all(o, k).start()

    @pl.when(sec == nsec - 1)
    def _():
        op_ref[...] = jnp.zeros_like(op_ref)

    for g in range(1, 6):
        load_whole(g).wait()

    tile = 16
    top = lax.broadcasted_iota(jnp.int32, (rows, 1), 0)

    def product(real_pair, ar, ai, br, bi, sign):
        cross = ai * bi
        re = ar * br + jnp.where(real_pair, 0.0, sign * cross)
        im = jnp.where(real_pair, cross, ar * bi - sign * ai * br)
        return re, im

    def products(spec, real_pair):
        mr, fr, pr = (spec[:rows, g * chunk:(g + 1) * chunk] for g in range(3))
        mi, fi, pi = (spec[rows:, g * chunk:(g + 1) * chunk] for g in range(3))
        return (
            product(real_pair, fr, fi, mr, mi, -1.0),
            product(real_pair, fr, fi, pr, pi, 1.0),
            product(real_pair, mr, mi, pr, pi, 1.0),
        )

    @pl.when(me == 0)
    def _():
        @pl.loop(0, chunks)
        def _(c):
            if rin:
                @pl.when(c < rin)
                def _():
                    give_relay(c).wait_recv()
                    forward_in(c).start()

            for g in range(3):
                part[0, 0:rows, g * chunk:(g + 1) * chunk] = sbuf[c, g]
            spec = jnp.dot(fwdl_ref[...], part[0, 0:rows, :], preferred_element_type=F32)
            outs = products(spec, top == 0)
            for g in range(3):
                lanes = slice(g * chunk, (g + 1) * chunk)
                part[1, 0:rows, lanes] = outs[g][0].astype(BF16)
                part[1, rows:2 * rows, lanes] = outs[g][1].astype(BF16)
            back = jnp.dot(invl_ref[...], part[1], preferred_element_type=F32).astype(BF16)
            corr = back[:, 2 * chunk:3 * chunk]
            hbuf[c, 0] = back[:, 0:chunk]
            lbuf[c, 0] = back[:, chunk:2 * chunk]
            lbuf[c, 1] = corr
            rate = when * corr.astype(F32) * sbuf[c, 1].astype(F32)
            skip = sbuf[c, 0].astype(F32) * sbuf[c, 2].astype(F32)
            cols = lanes_of(c)
            sloc[0:1, cols] = -jnp.sum(rate, axis=0, keepdims=True)
            sloc[1:2, cols] = jnp.sum(skip, axis=0, keepdims=True)

        for d in range(1, n):
            stat_local(d).start()
        gloc[...] = sloc[...]

    @pl.loop(0, own)
    def _(k):
        for s in range(n):
            @pl.when(me != s)
            def _():
                got_in(k, s).wait_recv()

        @pl.loop(0, rows // tile)
        def _(t):
            at = pl.ds(pl.multiple_of(t * tile, tile), tile)
            low = pl.ds(pl.multiple_of(rows + t * tile, tile), tile)
            for g in range(3):
                lanes = slice(g * chunk, (g + 1) * chunk)
                held = range(1, n) if g == 2 else range(n)
                x = {m: rbuf[k, m, g, at, :].astype(F32) for m in held}
                even = [m for m in held if m % 2 == 0]
                odd = [m for m in held if m % 2 == 1]
                zero = jnp.zeros_like(x[1])
                e = combine([(1.0, x[m]) for m in even], zero)
                d = combine([(1.0, x[m]) for m in odd], zero)
                part[0, at, lanes] = (e + d).astype(BF16)
                part[0, low, lanes] = (e - d).astype(BF16)
                for a in range(1, n // 2 + 1):
                    cos = [math.cos(math.pi * m * a / n) for m in range(n)]
                    sin = [math.sin(math.pi * m * a / n) for m in range(n)]
                    ce = combine([(cos[m], x[m]) for m in even], zero)
                    co = combine([(cos[m], x[m]) for m in odd], zero)
                    se = combine([(sin[m], x[m]) for m in even], zero)
                    so = combine([(sin[m], x[m]) for m in odd], zero)
                    part[a, at, lanes] = (ce + co).astype(BF16)
                    part[a, low, lanes] = (-se - so).astype(BF16)
                    if n - a != a:
                        part[n - a, at, lanes] = (ce - co).astype(BF16)
                        part[n - a, low, lanes] = (se - so).astype(BF16)

        @pl.loop(0, n)
        def _(a):
            spec = jnp.dot(fwd_ref[a], part[a], preferred_element_type=F32)
            outs = products(spec, jnp.logical_and(top == 0, a == 0))
            for g in range(3):
                lanes = slice(g * chunk, (g + 1) * chunk)
                part[a, 0:rows, lanes] = outs[g][0].astype(BF16)
                part[a, rows:2 * rows, lanes] = outs[g][1].astype(BF16)
            fold[a] = jnp.dot(inv_ref[a], part[a], preferred_element_type=F32)

        def unfold(t, carry):
            rate_sum, skip_sum = carry
            at = pl.ds(pl.multiple_of(t * tile, tile), tile)
            low = pl.ds(pl.multiple_of(rows + t * tile, tile), tile)
            for g in range(3):
                lanes = slice(g * chunk, (g + 1) * chunk)
                re = [fold[a, at, lanes] for a in range(n)]
                im = [fold[a, low, lanes] for a in range(n)]
                zero = jnp.zeros_like(re[0])
                for m in range(1 if g == 0 else 0, n):
                    terms = [(1.0, re[0]), ((-1.0) ** m, im[0])]
                    for a in range(1, n):
                        terms.append((math.cos(math.pi * m * a / n), re[a]))
                        terms.append((-math.sin(math.pi * m * a / n), im[a]))
                    value = combine(terms, zero).astype(BF16)
                    obuf[k, m, (0, 2, 1)[g], at, :] = value
                    if g == 2:
                        pos = lax.broadcasted_iota(jnp.int32, (tile, 1), 0) + (t * tile + m * rows)
                        pos = pos.astype(F32) * np.float32(1.0 / seq)
                        filt = rbuf[k, m, 1, at, :].astype(F32)
                        rate_sum = rate_sum + pos * value.astype(F32) * filt
                        if m:
                            mixed = rbuf[k, m, 0, at, :].astype(F32)
                            pulled = rbuf[k, m, 2, at, :].astype(F32)
                            skip_sum = skip_sum + mixed * pulled
            return rate_sum, skip_sum

        start = jnp.zeros((tile, chunk), F32)
        rate_sum, skip_sum = lax.fori_loop(0, rows // tile, unfold, (start, start))
        mine = lanes_of(base + k)
        sown[0:1, mine] = -jnp.sum(rate_sum, axis=0, keepdims=True)
        sown[1:2, mine] = jnp.sum(skip_sum, axis=0, keepdims=True)

        for m in range(n):
            @pl.when(me != m)
            def _():
                back_first(k, m).start()

        @pl.when(me == 0)
        def _():
            hbuf[base + k, 1:3] = obuf[k, 0, 1:3]

        @pl.when(me != 0)
        def _():
            hbuf[base + k] = obuf[k, me]

    for o in range(n):
        @pl.when(me == o)
        def _():
            cols = slice(bases[o] * chunk, (bases[o] + counts[o]) * chunk)
            for d in range(n):
                if d != o:
                    stat_own(o, d).start()
            gown[:, cols] = sown[:, cols]

    @pl.when(me == 2)
    def _():
        @pl.loop(0, rout)
        def _(i):
            back_relay(i).start()

    @pl.loop(0, own)
    def _(k):
        @pl.when(me != 0)
        def _():
            back_corr(k).start()

        direct = jnp.logical_or(me != 2, k < counts[2] - rout)

        @pl.when(jnp.logical_and(me != 1, direct))
        def _():
            back_rest(k, 1).start()

        for m in range(2, n):
            @pl.when(me != m)
            def _():
                back_rest(k, m).start()

    @pl.loop(0, most)
    def _(k):
        for o in range(n):
            @pl.when(k < counts[o])
            def _():
                if o:
                    @pl.when(me == 0)
                    def _():
                        give_pair(o, k).wait_send()

                @pl.when(jnp.logical_and(me != 0, me != o))
                def _():
                    give_all(o, k).wait_send()

    @pl.loop(0, most)
    def _(step):
        @pl.when(jnp.logical_and(me == 0, step >= most - rout))
        def _():
            back_relay(step - (most - rout)).wait_recv()
            forward_out(step - (most - rout)).start()

        for o in range(n):
            k = step * counts[o] // most

            @pl.when((step + 1) * counts[o] // most > k)
            def _(o=o, k=k):
                c = bases[o] + k

                @pl.when(me != o)
                def _():
                    got_first(c).wait_recv()

                @pl.when(me == 0)
                def _():
                    both = hbuf[c, 2].astype(F32) + lbuf[c, 0].astype(F32)
                    hbuf[c, 2] = both.astype(BF16)

                cols = lanes_of(c)
                pulled = sbuf[c, 2].astype(F32)
                mixed_grad = hbuf[c, 2].astype(F32) + skip_ref[:, cols] * pulled
                pbuf[c] = (mixed_grad * gk_ref[:, cols].astype(F32)).astype(BF16)

                @pl.when(sec > 0)
                def _():
                    pass_copy(c).start()

                ok_ref[:, cols] = (mixed_grad * vi_ref[:, cols].astype(F32)).astype(BF16)

    @pl.when(me != 0)
    def _():
        stat_local(1).wait_recv()

    for o in range(n):
        @pl.when(me != o)
        def _():
            stat_own(o, 0).wait_recv()
    orate_ref[...] = gown[0:1, :] + gloc[0:1, :]
    oskip_ref[...] = gown[1:2, :] + gloc[1:2, :]

    for d in range(1, n):
        @pl.when(me == 0)
        def _():
            stat_local(d).wait_send()
    for o in range(n):
        @pl.when(me == o)
        def _():
            for d in range(n):
                if d != o:
                    stat_own(o, d).wait_send()

    @pl.loop(0, own)
    def _(k):
        for m in range(n):
            @pl.when(me != m)
            def _():
                back_first(k, m).wait_send()

    @pl.loop(0, most)
    def _(step):
        for o in range(n):
            k = step * counts[o] // most

            @pl.when((step + 1) * counts[o] // most > k)
            def _(o=o, k=k):
                c = bases[o] + k

                @pl.when(me == 0)
                def _():
                    if o:
                        got_corr(c).wait_recv()
                    both = hbuf[c, 1].astype(F32) + lbuf[c, 1].astype(F32)
                    hbuf[c, 1] = both.astype(BF16)

                @pl.when(jnp.logical_and(me != 0, me != o))
                def _():
                    got_rest(c).wait_recv()

                cols = lanes_of(c)
                conv = hbuf[c, 0].astype(F32)
                mixed = sbuf[c, 0].astype(F32)
                oq_ref[:, cols] = (
                    go_ref[:, cols].astype(F32) * (conv + skip_ref[:, cols] * mixed)
                ).astype(BF16)
                envelope = jnp.exp(-rate_ref[:, cols] * when)
                of_ref[:, cols] = (hbuf[c, 1].astype(F32) * envelope).astype(BF16)

                @pl.when(sec > 0)
                def _():
                    pass_copy(c).wait_send()

                @pl.when(sec < nsec - 1)
                def _():
                    pass_copy(c).wait_recv()

    @pl.loop(0, own)
    def _(k):
        for m in range(n):
            @pl.when(me != m)
            def _():
                (back_rest(k, m) if m else back_corr(k)).wait_send()

    @pl.when(me == 0)
    def _():
        for i in range(rin):
            forward_in(i).wait_send()

        @pl.loop(0, rout)
        def _(k):
            forward_out(k).wait_send()


def quad_call(nsec, shapes, chunk, args, decay_rate, skip_gain):
    rows, channels = shapes[0].shape
    chunks = channels // chunk
    counts, _, rin, rout = split(chunks)
    most = max(counts)
    tables = (*make_tables(4, rows), *make_local_tables(rows))
    tables = tuple(jnp.asarray(table, BF16) for table in tables)
    dma = pltpu.SemaphoreType.DMA
    block = pltpu.VMEM((rows, channels), BF16)
    row = pltpu.VMEM((1, channels), F32)
    stat = pltpu.VMEM((2, channels), F32)
    return pl.pallas_call(
        functools.partial(quad_kernel, nsec, chunk),
        out_shape=tuple(pltpu.VMEM(shape.shape, shape.dtype) for shape in shapes),
        in_specs=[pl.BlockSpec(memory_space=pl.ANY)] * 11,
        out_specs=(pl.BlockSpec(memory_space=pltpu.VMEM),) * 6,
        scratch_shapes=[
            *([block] * 5), row, row, *(pltpu.VMEM(table.shape, BF16) for table in tables),
            dma((5, 2, 4)), dma((6,)),
            pltpu.VMEM((chunks, 3, rows, chunk), BF16),
            pltpu.VMEM((most, 4, 3, rows, chunk), BF16),
            pltpu.VMEM((most, 4, 3, rows, chunk), BF16),
            pltpu.VMEM((chunks, 3, rows, chunk), BF16),
            pltpu.VMEM((chunks, rows, chunk), BF16),
            pltpu.VMEM((chunks, 2, rows, chunk), BF16),
            pltpu.VMEM((max(rin, 1), 3, rows, chunk), BF16),
            pltpu.VMEM((rout, 2, rows, chunk), BF16),
            pltpu.VMEM((4, 2 * rows, 3 * chunk), BF16),
            pltpu.VMEM((4, 2 * rows, 3 * chunk), F32),
            stat, stat, stat, stat,
            dma((chunks,)), dma((most, 4)), dma((max(rin, 1),)), dma((max(rin, 1),)),
            dma((most, 4, 2)), dma((chunks, 2)), dma((rout,)), dma((rout,)),
            dma((chunks,)), dma((chunks,)), dma((2, 4)), dma((2, 4)),
        ],
        compiler_params=pltpu.CompilerParams(
            collective_id=0, has_side_effects=True, vmem_limit_bytes=58 * 1024 * 1024
        ),
        name="hyena_backward_quad",
    )(*args, decay_rate, skip_gain, *tables)


def finish(*refs):
    count = (len(refs) - 1) // 2
    sem = refs[-1]
    copies = [
        pltpu.make_async_copy(refs[g], refs[count + g], sem.at[g]) for g in range(count)
    ]
    for copy in copies:
        copy.start()
    for copy in copies:
        copy.wait()


def general_call(n, nsec, shapes, chunk, args, decay_rate, skip_gain):
    rows, channels = shapes[0].shape
    width = channels // n
    steps = width // chunk
    fwd, inv = make_tables(n, rows)
    fwd, inv = jnp.asarray(fwd, BF16), jnp.asarray(inv, BF16)
    message = (steps, n, rows, 3 * chunk)
    dma = pltpu.SemaphoreType.DMA
    anywhere = pl.BlockSpec(memory_space=pl.ANY)
    inside = pl.BlockSpec(memory_space=pltpu.VMEM)
    return pl.pallas_call(
        functools.partial(kernel, n, nsec, chunk, steps),
        out_shape=tuple(pltpu.VMEM(shape.shape, shape.dtype) for shape in shapes),
        in_specs=[anywhere] * 9,
        out_specs=(inside,) * 6,
        scratch_shapes=[
            *([pltpu.VMEM((rows, channels), BF16)] * 5),
            *([pltpu.VMEM((1, channels), F32)] * 2),
            *([pltpu.VMEM(fwd.shape, BF16)] * 2),
            dma((5, 2, n)), dma((4,)),
            pltpu.VMEM(message, BF16),
            pltpu.VMEM(message, BF16),
            pltpu.VMEM(message, BF16),
            pltpu.VMEM(message, BF16),
            pltpu.VMEM((steps, n, rows, chunk), BF16),
            pltpu.VMEM((n, 2 * rows, 3 * chunk), BF16),
            pltpu.VMEM((n, 2 * rows, 3 * chunk), F32),
            pltpu.VMEM((2, width), F32),
            pltpu.VMEM((n, 2, width), F32),
            dma((steps, n)), dma((steps, n)), dma((steps, n)), dma((steps, n)),
            dma((steps, n)), dma((steps, n)), dma((n,)), dma((n,)),
        ],
        compiler_params=pltpu.CompilerParams(
            collective_id=0, has_side_effects=True, vmem_limit_bytes=58 * 1024 * 1024
        ),
        name="hyena_backward",
    )(
        *args, decay_rate, skip_gain, fwd, inv,
    )


def shards(n, nsec, gate_q, gate_k, value_in, filter_raw, decay_rate, skip_gain, grad_out):
    rows, channels = gate_q.shape[1:]
    block = jax.ShapeDtypeStruct((rows, channels), BF16)
    row = jax.ShapeDtypeStruct((1, channels), F32)
    dma = pltpu.SemaphoreType.DMA
    anywhere = pl.BlockSpec(memory_space=pl.ANY)
    inside = pl.BlockSpec(memory_space=pltpu.VMEM)
    shapes = (block, block, block, block, row, row)
    args = (gate_q[0], gate_k[0], value_in[0], filter_raw[0], grad_out[0])
    call = quad_call if n == 4 and channels >= 16 * 128 else functools.partial(general_call, n)
    outs = call(nsec, shapes, 128, args, decay_rate, skip_gain)
    oq, ok, op, of, orate, oskip = pl.pallas_call(
        finish,
        out_shape=shapes,
        in_specs=[inside] * 6,
        out_specs=(anywhere,) * 6,
        scratch_shapes=[dma((6,))],
        compiler_params=pltpu.CompilerParams(vmem_limit_bytes=4 * 1024 * 1024),
        name="hand_over",
    )(*(pltpu.with_memory_space_constraint(out, pltpu.VMEM) for out in outs))
    return oq[None], ok[None], op[None], of[None], orate, oskip


def solution(mesh):
    n, nsec = mesh.shape["ctx"], mesh.shape["section"]
    tokens = P("section", "ctx", None)
    return jax.shard_map(
        functools.partial(shards, n, nsec),
        mesh=mesh,
        in_specs=(tokens, tokens, tokens, tokens, P("section", None), P("section", None), tokens),
        out_specs=(tokens, tokens, tokens, tokens, P("section", None), P("section", None)),
        check_vma=False,
    )
```

```python
import functools
import math

import jax
import jax.numpy as jnp
import numpy as np
from jax import lax
from jax.experimental import pallas as pl
from jax.experimental.pallas import tpu as pltpu
from jax.sharding import PartitionSpec as P

MESH = pl.DeviceIdType.MESH
F32 = jnp.float32
BF16 = jnp.bfloat16


def make_tables(n, rows):
    length = 2 * n * rows
    half = rows // 2
    j = np.arange(rows)[None, :]
    b = np.arange(rows)[:, None]

    def angle(a):
        return 2.0 * np.pi * ((j * (a + 2 * n * b)) % length) / length

    fwd = np.zeros((n, 2 * rows, 2 * rows))
    inv = np.zeros((n, 2 * rows, 2 * rows))
    for a in range(1, n):
        c, s = np.cos(angle(a)), np.sin(angle(a))
        fwd[a] = np.block([[c, s], [-s, c]])
        inv[a] = np.block([[c.T, -s.T], [s.T, c.T]]) * (2.0 / length)
    for slot, a in ((0, 0), (1, n)):
        c, s = np.cos(angle(a))[:half], np.sin(angle(a))[:half]
        weight = np.full((half, 1), 2.0 / length)
        re_rows = slice(slot * half, (slot + 1) * half)
        im_rows = slice(rows + slot * half, rows + (slot + 1) * half)
        cols = slice(slot * rows, (slot + 1) * rows)
        im = -s
        if slot == 0:
            im = im.copy()
            im[0] = np.cos(np.pi * np.arange(rows))
            weight[0] = 1.0 / length
        fwd[0, re_rows, cols] = c
        fwd[0, im_rows, cols] = im
        inv[0, cols, re_rows] = (c * weight).T
        inv[0, cols, im_rows] = (im * weight).T
    return fwd, inv


def scaled(coef, x):
    if abs(coef - 1.0) < 1e-12:
        return x
    if abs(coef + 1.0) < 1e-12:
        return -x
    return x * np.float32(coef)


def combine(terms, zero):
    total = None
    for coef, x in terms:
        if abs(coef) < 1e-12:
            continue
        if total is None:
            total = scaled(coef, x)
        elif coef < 0:
            total = total - scaled(-coef, x)
        else:
            total = total + scaled(coef, x)
    return zero if total is None else total


def kernel(
    n, nsec, chunk, steps,
    gq_hbm, gk_hbm, vi_hbm, fr_hbm, go_hbm, rate_hbm, skip_hbm, fwd_hbm, inv_hbm,
    oq_ref, ok_ref, op_ref, of_ref, orate_ref, oskip_ref,
    gq_ref, gk_ref, vi_ref, fr_ref, go_ref, rate_ref, skip_ref, fwd_ref, inv_ref,
    in_sem, row_sem,
    sbuf, rbuf, obuf, hbuf, pbuf, part, fold, sstat, gstat,
    s_send, s_recv, o_send, o_recv, p_send, p_recv, t_send, t_recv,
):
    rows = gq_ref.shape[0]
    width = chunk * steps
    seq = rows * n
    me = lax.axis_index("ctx")
    sec = lax.axis_index("section")
    before = lax.rem(sec + nsec - 1, nsec)
    after = lax.rem(sec + 1, nsec)

    def columns(owner, k):
        return pl.ds(pl.multiple_of(owner * width + k * chunk, chunk), chunk)

    tokens = (
        (gk_hbm, gk_ref), (vi_hbm, vi_ref), (gq_hbm, gq_ref), (go_hbm, go_ref), (fr_hbm, fr_ref)
    )
    whole = (
        (rate_hbm, rate_ref), (skip_hbm, skip_ref), (fwd_hbm, fwd_ref), (inv_hbm, inv_ref)
    )

    def load_first(g, d):
        hbm, ref = tokens[g]
        return pltpu.make_async_copy(
            hbm.at[:, columns(d, 0)], ref.at[:, columns(d, 0)], in_sem.at[g, 0, d]
        )

    def load_rest(g, d):
        hbm, ref = tokens[g]
        cols = pl.ds(pl.multiple_of(d * width + chunk, chunk), width - chunk)
        return pltpu.make_async_copy(hbm.at[:, cols], ref.at[:, cols], in_sem.at[g, 1, d])

    def load_whole(g):
        return pltpu.make_async_copy(whole[g][0], whole[g][1], row_sem.at[g])

    load_whole(0).start()
    for o in range(n):
        for g in range(5):
            load_first(g, lax.rem(me + 1 + o, n)).start()
    if steps > 1:
        for d in range(n):
            for g in range(5):
                load_rest(g, d).start()
    for g in range(1, 4):
        load_whole(g).start()

    barrier = pltpu.get_barrier_semaphore()
    for o in range(1, n):
        pl.semaphore_signal(
            barrier, inc=1, device_id={"ctx": lax.rem(me + o, n)}, device_id_type=MESH
        )
    for other in (before, after):
        pl.semaphore_signal(barrier, inc=1, device_id={"section": other}, device_id_type=MESH)
    pl.semaphore_wait(barrier, n + 1)
    load_whole(0).wait()

    def here(row0, count):
        row = lax.broadcasted_iota(jnp.int32, (count, 1), 0) + (row0 + me * rows)
        return row.astype(F32) * np.float32(1.0 / seq)

    def send_in(k, d):
        return pltpu.make_async_remote_copy(
            src_ref=sbuf.at[k, d], dst_ref=rbuf.at[k, me], send_sem=s_send.at[k, d],
            recv_sem=s_recv.at[k, me], device_id={"ctx": d}, device_id_type=MESH,
        )

    def got_in(k, m):
        return pltpu.make_async_remote_copy(
            src_ref=sbuf.at[k, m], dst_ref=rbuf.at[k, m], send_sem=s_send.at[k, m],
            recv_sem=s_recv.at[k, m], device_id={"ctx": m}, device_id_type=MESH,
        )

    def send_out(k, m):
        return pltpu.make_async_remote_copy(
            src_ref=obuf.at[k, m], dst_ref=hbuf.at[k, me], send_sem=o_send.at[k, m],
            recv_sem=o_recv.at[k, me], device_id={"ctx": m}, device_id_type=MESH,
        )

    def got_out(k, m):
        return pltpu.make_async_remote_copy(
            src_ref=obuf.at[k, m], dst_ref=hbuf.at[k, m], send_sem=o_send.at[k, m],
            recv_sem=o_recv.at[k, m], device_id={"ctx": m}, device_id_type=MESH,
        )

    def send_stat(d):
        return pltpu.make_async_remote_copy(
            src_ref=sstat, dst_ref=gstat.at[me], send_sem=t_send.at[d],
            recv_sem=t_recv.at[me], device_id={"ctx": d}, device_id_type=MESH,
        )

    def got_stat(m):
        return pltpu.make_async_remote_copy(
            src_ref=sstat, dst_ref=gstat.at[m], send_sem=t_send.at[m],
            recv_sem=t_recv.at[m], device_id={"ctx": m}, device_id_type=MESH,
        )

    def pass_copy(k, m):
        return pltpu.make_async_remote_copy(
            src_ref=pbuf.at[k, m], dst_ref=op_ref.at[:, columns(m, k)], send_sem=p_send.at[k, m],
            recv_sem=p_recv.at[k, m], device_id={"section": before}, device_id_type=MESH,
        )

    @pl.loop(0, steps * n)
    def _(i):
        k, o = i // n, lax.rem(i, n)
        d = lax.rem(me + 1 + o, n)
        cols = columns(d, k)

        @pl.when(k == 0)
        def _():
            for g in range(5):
                load_first(g, d).wait()

        if steps > 1:
            @pl.when(k == 1)
            def _():
                for g in range(5):
                    load_rest(g, d).wait()

        mixed = (gk_ref[:, cols].astype(F32) * vi_ref[:, cols].astype(F32)).astype(BF16)
        pulled = (gq_ref[:, cols].astype(F32) * go_ref[:, cols].astype(F32)).astype(BF16)
        envelope = jnp.exp(-rate_ref[:, cols] * here(0, rows))
        filt = (fr_ref[:, cols].astype(F32) * envelope).astype(BF16)
        sbuf[k, d, :, 0:chunk] = mixed
        sbuf[k, d, :, chunk:2 * chunk] = filt
        sbuf[k, d, :, 2 * chunk:3 * chunk] = pulled

        @pl.when(o < n - 1)
        def _():
            send_in(k, d).start()

        @pl.when(o == n - 1)
        def _():
            rbuf[k, me, :, 0:chunk] = mixed
            rbuf[k, me, :, chunk:2 * chunk] = filt
            rbuf[k, me, :, 2 * chunk:3 * chunk] = pulled

    @pl.when(sec == nsec - 1)
    def _():
        op_ref[...] = jnp.zeros_like(op_ref)

    for g in range(1, 4):
        load_whole(g).wait()

    tile = 16
    top = lax.broadcasted_iota(jnp.int32, (rows, 1), 0)

    @pl.loop(0, steps)
    def _(k):
        @pl.loop(0, n - 1)
        def _(o):
            got_in(k, lax.rem(me + 1 + o, n)).wait_recv()

        @pl.loop(0, rows // tile)
        def _(t):
            at = pl.ds(pl.multiple_of(t * tile, tile), tile)
            low = pl.ds(pl.multiple_of(rows + t * tile, tile), tile)
            for g in range(3):
                lanes = slice(g * chunk, (g + 1) * chunk)
                x = [rbuf[k, m, at, lanes].astype(F32) for m in range(n)]
                zero = jnp.zeros_like(x[0])
                even = combine([(1.0, x[m]) for m in range(0, n, 2)], zero)
                odd = combine([(1.0, x[m]) for m in range(1, n, 2)], zero)
                part[0, at, lanes] = (even + odd).astype(BF16)
                part[0, low, lanes] = (even - odd).astype(BF16)
                for a in range(1, n // 2 + 1):
                    cos = [math.cos(math.pi * m * a / n) for m in range(n)]
                    sin = [math.sin(math.pi * m * a / n) for m in range(n)]
                    ce = combine([(cos[m], x[m]) for m in range(0, n, 2)], zero)
                    co = combine([(cos[m], x[m]) for m in range(1, n, 2)], zero)
                    se = combine([(sin[m], x[m]) for m in range(0, n, 2)], zero)
                    so = combine([(sin[m], x[m]) for m in range(1, n, 2)], zero)
                    part[a, at, lanes] = (ce + co).astype(BF16)
                    part[a, low, lanes] = (-se - so).astype(BF16)
                    if n - a != a:
                        part[n - a, at, lanes] = (ce - co).astype(BF16)
                        part[n - a, low, lanes] = (se - so).astype(BF16)

        @pl.loop(0, n)
        def _(a):
            spec = jnp.dot(fwd_ref[a], part[a], preferred_element_type=F32)
            mr, fr, pr = (spec[:rows, g * chunk:(g + 1) * chunk] for g in range(3))
            mi, fi, pi = (spec[rows:, g * chunk:(g + 1) * chunk] for g in range(3))
            real_pair = jnp.logical_and(top == 0, a == 0)

            def product(ar, ai, br, bi, sign):
                cross = ai * bi
                re = ar * br + jnp.where(real_pair, 0.0, sign * cross)
                im = jnp.where(real_pair, cross, ar * bi - sign * ai * br)
                return re, im

            outs = (
                product(fr, fi, mr, mi, -1.0),
                product(fr, fi, pr, pi, 1.0),
                product(mr, mi, pr, pi, 1.0),
            )
            for g in range(3):
                lanes = slice(g * chunk, (g + 1) * chunk)
                part[a, 0:rows, lanes] = outs[g][0].astype(BF16)
                part[a, rows:2 * rows, lanes] = outs[g][1].astype(BF16)
            fold[a] = jnp.dot(inv_ref[a], part[a], preferred_element_type=F32)

        def unfold(t, carry):
            rate_sum, skip_sum = carry
            at = pl.ds(pl.multiple_of(t * tile, tile), tile)
            low = pl.ds(pl.multiple_of(rows + t * tile, tile), tile)
            for g in range(3):
                lanes = slice(g * chunk, (g + 1) * chunk)
                re = [fold[a, at, lanes] for a in range(n)]
                im = [fold[a, low, lanes] for a in range(n)]
                zero = jnp.zeros_like(re[0])
                for m in range(n):
                    terms = [(1.0, re[0]), ((-1.0) ** m, im[0])]
                    for a in range(1, n):
                        terms.append((math.cos(math.pi * m * a / n), re[a]))
                        terms.append((-math.sin(math.pi * m * a / n), im[a]))
                    value = combine(terms, zero).astype(BF16)
                    obuf[k, m, at, lanes] = value
                    if g == 2:
                        when = lax.broadcasted_iota(jnp.int32, (tile, 1), 0) + (t * tile + m * rows)
                        when = when.astype(F32) * np.float32(1.0 / seq)
                        mixed = rbuf[k, m, at, 0:chunk].astype(F32)
                        filt = rbuf[k, m, at, chunk:2 * chunk].astype(F32)
                        pulled = rbuf[k, m, at, 2 * chunk:3 * chunk].astype(F32)
                        rate_sum = rate_sum + when * value.astype(F32) * filt
                        skip_sum = skip_sum + mixed * pulled
            return rate_sum, skip_sum

        start = jnp.zeros((tile, chunk), F32)
        rate_sum, skip_sum = lax.fori_loop(0, rows // tile, unfold, (start, start))
        mine = pl.ds(pl.multiple_of(k * chunk, chunk), chunk)
        sstat[0:1, mine] = -jnp.sum(rate_sum, axis=0, keepdims=True)
        sstat[1:2, mine] = jnp.sum(skip_sum, axis=0, keepdims=True)

        @pl.loop(0, n - 1)
        def _(o):
            send_out(k, lax.rem(me + 1 + o, n)).start()

        hbuf[k, me] = obuf[k, me]

    for o in range(1, n):
        send_stat(lax.rem(me + o, n)).start()
    gstat[me] = sstat[...]

    @pl.loop(0, steps * n)
    def _(i):
        k, o = i // n, lax.rem(i, n)
        m = lax.rem(me + o, n)

        @pl.when(o > 0)
        def _():
            got_out(k, m).wait_recv()

        cols = columns(m, k)
        conv = hbuf[k, m, :, 0:chunk].astype(F32)
        adjoint = hbuf[k, m, :, chunk:2 * chunk].astype(F32)
        corr = hbuf[k, m, :, 2 * chunk:3 * chunk].astype(F32)
        mixed = sbuf[k, m, :, 0:chunk].astype(F32)
        pulled = sbuf[k, m, :, 2 * chunk:3 * chunk].astype(F32)
        skip = skip_ref[:, cols]
        oq_ref[:, cols] = (go_ref[:, cols].astype(F32) * (conv + skip * mixed)).astype(BF16)
        mixed_grad = adjoint + skip * pulled
        pbuf[k, m] = (mixed_grad * gk_ref[:, cols].astype(F32)).astype(BF16)

        @pl.when(sec > 0)
        def _():
            pass_copy(k, m).start()

        ok_ref[:, cols] = (mixed_grad * vi_ref[:, cols].astype(F32)).astype(BF16)
        envelope = jnp.exp(-rate_ref[:, cols] * here(0, rows))
        of_ref[:, cols] = (corr * envelope).astype(BF16)

    for o in range(1, n):
        got_stat(lax.rem(me + o, n)).wait_recv()
    for m in range(n):
        orate_ref[:, m * width:(m + 1) * width] = gstat[m, 0:1, :]
        oskip_ref[:, m * width:(m + 1) * width] = gstat[m, 1:2, :]

    for o in range(1, n):
        send_stat(lax.rem(me + o, n)).wait_send()

    @pl.loop(0, steps * (n - 1))
    def _(i):
        k, o = i // (n - 1), lax.rem(i, n - 1)
        d = lax.rem(me + 1 + o, n)
        send_in(k, d).wait_send()
        send_out(k, d).wait_send()

    @pl.loop(0, steps * n)
    def _(i):
        k, m = i // n, lax.rem(i, n)

        @pl.when(sec > 0)
        def _():
            pass_copy(k, m).wait_send()

        @pl.when(sec < nsec - 1)
        def _():
            pass_copy(k, m).wait_recv()


def make_local_tables(rows):
    length = 2 * rows
    j = np.arange(rows)[None, :]
    b = np.arange(rows)[:, None]
    angle = 2.0 * np.pi * ((j * b) % length) / length
    re, im = np.cos(angle), -np.sin(angle)
    im[0] = np.cos(np.pi * np.arange(rows))
    weight = np.full((rows, 1), 2.0 / length)
    weight[0] = 1.0 / length
    return np.concatenate([re, im]), np.concatenate([re * weight, im * weight]).T


def split(chunks):
    zero, first = chunks * 6 // 32, chunks // 4
    third = (chunks - zero - first) // 2
    counts = (zero, first, chunks - zero - first - third, third)
    bases = tuple(sum(counts[:o]) for o in range(4))
    return counts, bases, chunks // 16, chunks // 8


def quad_kernel(
    nsec, chunk,
    gq_hbm, gk_hbm, vi_hbm, fr_hbm, go_hbm, rate_hbm, skip_hbm, fwd_hbm, inv_hbm, fwdl_hbm, invl_hbm,
    oq_ref, ok_ref, op_ref, of_ref, orate_ref, oskip_ref,
    gq_ref, gk_ref, vi_ref, fr_ref, go_ref, rate_ref, skip_ref, fwd_ref, inv_ref, fwdl_ref, invl_ref,
    in_sem, row_sem,
    sbuf, rbuf, obuf, hbuf, pbuf, lbuf, relin, relout, part, fold, sown, sloc, gown, gloc,
    i_send, i_recv, ri_send, ri_recv, o_send, o_recv, ro_send, ro_recv, p_send, p_recv,
    t_send, t_recv,
):
    n = 4
    rows, channels = gq_ref.shape
    chunks = channels // chunk
    counts, bases, rin, rout = split(chunks)
    most = max(counts)
    seq = rows * n
    me = lax.axis_index("ctx")
    sec = lax.axis_index("section")
    before = lax.rem(sec + nsec - 1, nsec)
    after = lax.rem(sec + 1, nsec)
    is1 = me * (3 - me) * (2 - me) // 2
    is2 = me * (3 - me) * (me - 1) // 2
    is3 = me * (me - 1) * (me - 2) // 6
    is0 = 1 - is1 - is2 - is3
    own = is0 * counts[0] + is1 * counts[1] + is2 * counts[2] + is3 * counts[3]
    base = is1 * bases[1] + is2 * bases[2] + is3 * bases[3]

    def lanes_of(c):
        return pl.ds(pl.multiple_of(c * chunk, chunk), chunk)

    tokens = (
        (gk_hbm, gk_ref), (vi_hbm, vi_ref), (gq_hbm, gq_ref), (go_hbm, go_ref), (fr_hbm, fr_ref)
    )
    whole = (
        (rate_hbm, rate_ref), (skip_hbm, skip_ref), (fwd_hbm, fwd_ref), (inv_hbm, inv_ref),
        (fwdl_hbm, fwdl_ref), (invl_hbm, invl_ref),
    )

    def load(g, o, rest):
        hbm, ref = tokens[g]
        lo = bases[o] + rest
        hi = bases[o] + counts[o] if rest else lo + 1
        cols = slice(lo * chunk, hi * chunk)
        return pltpu.make_async_copy(hbm.at[:, cols], ref.at[:, cols], in_sem.at[g, rest, o])

    def load_whole(g):
        return pltpu.make_async_copy(whole[g][0], whole[g][1], row_sem.at[g])

    load_whole(0).start()
    for rest in range(2):
        for o in reversed(range(n)):
            for g in range(5):
                load(g, o, rest).start()
    for g in range(1, 6):
        load_whole(g).start()

    barrier = pltpu.get_barrier_semaphore()
    for o in range(1, n):
        pl.semaphore_signal(
            barrier, inc=1, device_id={"ctx": lax.rem(me + o, n)}, device_id_type=MESH
        )
    for other in (before, after):
        pl.semaphore_signal(barrier, inc=1, device_id={"section": other}, device_id_type=MESH)
    pl.semaphore_wait(barrier, n + 1)
    load_whole(0).wait()

    def to(d):
        return {"ctx": jnp.int32(d)}

    def remote(src, dst, send, recv, where):
        return pltpu.make_async_remote_copy(
            src_ref=src, dst_ref=dst, send_sem=send, recv_sem=recv,
            device_id=where, device_id_type=MESH,
        )

    def give_pair(o, k):
        c = bases[o] + k
        return remote(
            sbuf.at[c, 0:2], rbuf.at[k, 0, 0:2], i_send.at[c], i_recv.at[k, 0], to(o)
        )

    def give_all(o, k):
        c = bases[o] + k
        return remote(sbuf.at[c], rbuf.at[k, me], i_send.at[c], i_recv.at[k, me], to(o))

    def give_relay(k):
        c = bases[1] + k
        return remote(sbuf.at[c], relin.at[k], i_send.at[c], ri_recv.at[k], to(0))

    def forward_in(i):
        return remote(
            relin.at[i], rbuf.at[i, 2], ri_send.at[i], i_recv.at[i, 2], to(1)
        )

    def got_in(k, s):
        at = rbuf.at[k, 0, 0:2] if s == 0 else rbuf.at[k, s]
        src = sbuf.at[0, 0:2] if s == 0 else sbuf.at[0]
        return remote(src, at, i_send.at[0], i_recv.at[k, s], to(s))

    def back_first(k, m):
        return remote(
            obuf.at[k, m, 2], hbuf.at[base + k, 2], o_send.at[k, m, 0], o_recv.at[base + k, 0],
            to(m),
        )

    def back_corr(k):
        return remote(
            obuf.at[k, 0, 1], hbuf.at[base + k, 1], o_send.at[k, 0, 1], o_recv.at[base + k, 1],
            to(0),
        )

    def back_rest(k, m):
        return remote(
            obuf.at[k, m, 0:2], hbuf.at[base + k, 0:2], o_send.at[k, m, 1],
            o_recv.at[base + k, 1], to(m),
        )

    def back_relay(i):
        k = counts[2] - rout + i
        return remote(obuf.at[k, 1, 0:2], relout.at[i], o_send.at[k, 1, 1], ro_recv.at[i], to(0))

    def forward_out(i):
        c = bases[2] + counts[2] - rout + i
        return remote(relout.at[i], hbuf.at[c, 0:2], ro_send.at[i], o_recv.at[c, 1], to(1))

    def got_first(c):
        return remote(
            obuf.at[0, 0, 2], hbuf.at[c, 2], o_send.at[0, 0, 0], o_recv.at[c, 0], to(1)
        )

    def got_corr(c):
        return remote(
            obuf.at[0, 0, 1], hbuf.at[c, 1], o_send.at[0, 0, 1], o_recv.at[c, 1], to(1)
        )

    def got_rest(c):
        return remote(
            obuf.at[0, 0, 0:2], hbuf.at[c, 0:2], o_send.at[0, 0, 1], o_recv.at[c, 1], to(1)
        )

    def stat_own(o, d):
        cols = slice(bases[o] * chunk, (bases[o] + counts[o]) * chunk)
        return remote(
            sown.at[:, cols], gown.at[:, cols], t_send.at[0, d], t_recv.at[0, o], to(d)
        )

    def stat_local(d):
        return remote(sloc, gloc, t_send.at[1, d], t_recv.at[1, 0], to(d))

    def pass_copy(c):
        return remote(
            pbuf.at[c], op_ref.at[:, lanes_of(c)], p_send.at[c], p_recv.at[c],
            {"section": before},
        )

    when = lax.broadcasted_iota(jnp.int32, (rows, 1), 0) + me * rows
    when = when.astype(F32) * np.float32(1.0 / seq)

    @pl.loop(0, most)
    def _(step):
        for o in reversed(range(n)):
            k = step * counts[o] // most

            @pl.when((step + 1) * counts[o] // most > k)
            def _(o=o, k=k):
                for rest in range(2):
                    @pl.when(k == rest)
                    def _():
                        for g in range(5):
                            load(g, o, rest).wait()

                c = bases[o] + k
                cols = lanes_of(c)
                mixed = (gk_ref[:, cols].astype(F32) * vi_ref[:, cols].astype(F32)).astype(BF16)
                pulled = (gq_ref[:, cols].astype(F32) * go_ref[:, cols].astype(F32)).astype(BF16)
                envelope = jnp.exp(-rate_ref[:, cols] * when)
                filt = (fr_ref[:, cols].astype(F32) * envelope).astype(BF16)
                sbuf[c, 0] = mixed
                sbuf[c, 1] = filt
                sbuf[c, 2] = pulled

                @pl.when(me == o)
                def _():
                    rbuf[k, o, 0] = mixed
                    rbuf[k, o, 1] = filt
                    if o:
                        rbuf[k, o, 2] = pulled

                if o:
                    @pl.when(me == 0)
                    def _():
                        give_pair(o, k).start()

                if o == 1:
                    @pl.when(jnp.logical_and(me == 2, k < rin))
                    def _():
                        give_relay(k).start()

                    @pl.when(jnp.logical_or(me == 3, jnp.logical_and(me == 2, k >= rin)))
                    def _():
                        give_all(o, k).start()
                else:
                    @pl.when(jnp.logical_and(me != 0, me != o))
                    def _():
                        give_all(o, k).start()

    @pl.when(sec == nsec - 1)
    def _():
        op_ref[...] = jnp.zeros_like(op_ref)

    for g in range(1, 6):
        load_whole(g).wait()

    tile = 16
    top = lax.broadcasted_iota(jnp.int32, (rows, 1), 0)

    def product(real_pair, ar, ai, br, bi, sign):
        cross = ai * bi
        re = ar * br + jnp.where(real_pair, 0.0, sign * cross)
        im = jnp.where(real_pair, cross, ar * bi - sign * ai * br)
        return re, im

    def products(spec, real_pair):
        mr, fr, pr = (spec[:rows, g * chunk:(g + 1) * chunk] for g in range(3))
        mi, fi, pi = (spec[rows:, g * chunk:(g + 1) * chunk] for g in range(3))
        return (
            product(real_pair, fr, fi, mr, mi, -1.0),
            product(real_pair, fr, fi, pr, pi, 1.0),
            product(real_pair, mr, mi, pr, pi, 1.0),
        )

    @pl.when(me == 0)
    def _():
        @pl.loop(0, chunks)
        def _(c):
            if rin:
                @pl.when(c < rin)
                def _():
                    give_relay(c).wait_recv()
                    forward_in(c).start()

            for g in range(3):
                part[0, 0:rows, g * chunk:(g + 1) * chunk] = sbuf[c, g]
            spec = jnp.dot(fwdl_ref[...], part[0, 0:rows, :], preferred_element_type=F32)
            outs = products(spec, top == 0)
            for g in range(3):
                lanes = slice(g * chunk, (g + 1) * chunk)
                part[1, 0:rows, lanes] = outs[g][0].astype(BF16)
                part[1, rows:2 * rows, lanes] = outs[g][1].astype(BF16)
            back = jnp.dot(invl_ref[...], part[1], preferred_element_type=F32).astype(BF16)
            corr = back[:, 2 * chunk:3 * chunk]
            hbuf[c, 0] = back[:, 0:chunk]
            lbuf[c, 0] = back[:, chunk:2 * chunk]
            lbuf[c, 1] = corr
            rate = when * corr.astype(F32) * sbuf[c, 1].astype(F32)
            skip = sbuf[c, 0].astype(F32) * sbuf[c, 2].astype(F32)
            cols = lanes_of(c)
            sloc[0:1, cols] = -jnp.sum(rate, axis=0, keepdims=True)
            sloc[1:2, cols] = jnp.sum(skip, axis=0, keepdims=True)

        for d in range(1, n):
            stat_local(d).start()
        gloc[...] = sloc[...]

    @pl.loop(0, own)
    def _(k):
        for s in range(n):
            @pl.when(me != s)
            def _():
                got_in(k, s).wait_recv()

        @pl.loop(0, rows // tile)
        def _(t):
            at = pl.ds(pl.multiple_of(t * tile, tile), tile)
            low = pl.ds(pl.multiple_of(rows + t * tile, tile), tile)
            for g in range(3):
                lanes = slice(g * chunk, (g + 1) * chunk)
                held = range(1, n) if g == 2 else range(n)
                x = {m: rbuf[k, m, g, at, :].astype(F32) for m in held}
                even = [m for m in held if m % 2 == 0]
                odd = [m for m in held if m % 2 == 1]
                zero = jnp.zeros_like(x[1])
                e = combine([(1.0, x[m]) for m in even], zero)
                d = combine([(1.0, x[m]) for m in odd], zero)
                part[0, at, lanes] = (e + d).astype(BF16)
                part[0, low, lanes] = (e - d).astype(BF16)
                for a in range(1, n // 2 + 1):
                    cos = [math.cos(math.pi * m * a / n) for m in range(n)]
                    sin = [math.sin(math.pi * m * a / n) for m in range(n)]
                    ce = combine([(cos[m], x[m]) for m in even], zero)
                    co = combine([(cos[m], x[m]) for m in odd], zero)
                    se = combine([(sin[m], x[m]) for m in even], zero)
                    so = combine([(sin[m], x[m]) for m in odd], zero)
                    part[a, at, lanes] = (ce + co).astype(BF16)
                    part[a, low, lanes] = (-se - so).astype(BF16)
                    if n - a != a:
                        part[n - a, at, lanes] = (ce - co).astype(BF16)
                        part[n - a, low, lanes] = (se - so).astype(BF16)

        @pl.loop(0, n)
        def _(a):
            spec = jnp.dot(fwd_ref[a], part[a], preferred_element_type=F32)
            outs = products(spec, jnp.logical_and(top == 0, a == 0))
            for g in range(3):
                lanes = slice(g * chunk, (g + 1) * chunk)
                part[a, 0:rows, lanes] = outs[g][0].astype(BF16)
                part[a, rows:2 * rows, lanes] = outs[g][1].astype(BF16)
            fold[a] = jnp.dot(inv_ref[a], part[a], preferred_element_type=F32)

        def unfold(t, carry):
            rate_sum, skip_sum = carry
            at = pl.ds(pl.multiple_of(t * tile, tile), tile)
            low = pl.ds(pl.multiple_of(rows + t * tile, tile), tile)
            for g in range(3):
                lanes = slice(g * chunk, (g + 1) * chunk)
                re = [fold[a, at, lanes] for a in range(n)]
                im = [fold[a, low, lanes] for a in range(n)]
                zero = jnp.zeros_like(re[0])
                for m in range(1 if g == 0 else 0, n):
                    terms = [(1.0, re[0]), ((-1.0) ** m, im[0])]
                    for a in range(1, n):
                        terms.append((math.cos(math.pi * m * a / n), re[a]))
                        terms.append((-math.sin(math.pi * m * a / n), im[a]))
                    value = combine(terms, zero).astype(BF16)
                    obuf[k, m, (0, 2, 1)[g], at, :] = value
                    if g == 2:
                        pos = lax.broadcasted_iota(jnp.int32, (tile, 1), 0) + (t * tile + m * rows)
                        pos = pos.astype(F32) * np.float32(1.0 / seq)
                        filt = rbuf[k, m, 1, at, :].astype(F32)
                        rate_sum = rate_sum + pos * value.astype(F32) * filt
                        if m:
                            mixed = rbuf[k, m, 0, at, :].astype(F32)
                            pulled = rbuf[k, m, 2, at, :].astype(F32)
                            skip_sum = skip_sum + mixed * pulled
            return rate_sum, skip_sum

        start = jnp.zeros((tile, chunk), F32)
        rate_sum, skip_sum = lax.fori_loop(0, rows // tile, unfold, (start, start))
        mine = lanes_of(base + k)
        sown[0:1, mine] = -jnp.sum(rate_sum, axis=0, keepdims=True)
        sown[1:2, mine] = jnp.sum(skip_sum, axis=0, keepdims=True)

        for m in reversed(range(n)):
            @pl.when(me != m)
            def _():
                back_first(k, m).start()

        @pl.when(me == 0)
        def _():
            hbuf[base + k, 1:3] = obuf[k, 0, 1:3]

        @pl.when(me != 0)
        def _():
            hbuf[base + k] = obuf[k, me]

    for o in range(n):
        @pl.when(me == o)
        def _():
            cols = slice(bases[o] * chunk, (bases[o] + counts[o]) * chunk)
            for d in range(n):
                if d != o:
                    stat_own(o, d).start()
            gown[:, cols] = sown[:, cols]

    @pl.when(me == 2)
    def _():
        @pl.loop(0, rout)
        def _(i):
            back_relay(i).start()

    @pl.loop(0, own)
    def _(k):
        @pl.when(me != 0)
        def _():
            back_corr(k).start()

        direct = jnp.logical_or(me != 2, k < counts[2] - rout)

        @pl.when(jnp.logical_and(me != 1, direct))
        def _():
            back_rest(k, 1).start()

        for m in range(2, n):
            @pl.when(me != m)
            def _():
                back_rest(k, m).start()

    @pl.loop(0, most)
    def _(k):
        for o in range(n):
            @pl.when(k < counts[o])
            def _():
                if o:
                    @pl.when(me == 0)
                    def _():
                        give_pair(o, k).wait_send()

                @pl.when(jnp.logical_and(me != 0, me != o))
                def _():
                    give_all(o, k).wait_send()

    @pl.loop(0, most)
    def _(step):
        @pl.when(jnp.logical_and(me == 0, step >= most - rout))
        def _():
            back_relay(step - (most - rout)).wait_recv()
            forward_out(step - (most - rout)).start()

        for o in range(n):
            k = step * counts[o] // most

            @pl.when((step + 1) * counts[o] // most > k)
            def _(o=o, k=k):
                c = bases[o] + k

                @pl.when(me != o)
                def _():
                    got_first(c).wait_recv()

                @pl.when(me == 0)
                def _():
                    both = hbuf[c, 2].astype(F32) + lbuf[c, 0].astype(F32)
                    hbuf[c, 2] = both.astype(BF16)

                cols = lanes_of(c)
                pulled = sbuf[c, 2].astype(F32)
                mixed_grad = hbuf[c, 2].astype(F32) + skip_ref[:, cols] * pulled
                pbuf[c] = (mixed_grad * gk_ref[:, cols].astype(F32)).astype(BF16)

                @pl.when(sec > 0)
                def _():
                    pass_copy(c).start()

                ok_ref[:, cols] = (mixed_grad * vi_ref[:, cols].astype(F32)).astype(BF16)

    @pl.when(me != 0)
    def _():
        stat_local(1).wait_recv()

    for o in range(n):
        @pl.when(me != o)
        def _():
            stat_own(o, 0).wait_recv()
    orate_ref[...] = gown[0:1, :] + gloc[0:1, :]
    oskip_ref[...] = gown[1:2, :] + gloc[1:2, :]

    for d in range(1, n):
        @pl.when(me == 0)
        def _():
            stat_local(d).wait_send()
    for o in range(n):
        @pl.when(me == o)
        def _():
            for d in range(n):
                if d != o:
                    stat_own(o, d).wait_send()

    @pl.loop(0, own)
    def _(k):
        for m in range(n):
            @pl.when(me != m)
            def _():
                back_first(k, m).wait_send()

    @pl.loop(0, most)
    def _(step):
        for o in range(n):
            k = step * counts[o] // most

            @pl.when((step + 1) * counts[o] // most > k)
            def _(o=o, k=k):
                c = bases[o] + k

                @pl.when(me == 0)
                def _():
                    if o:
                        got_corr(c).wait_recv()
                    both = hbuf[c, 1].astype(F32) + lbuf[c, 1].astype(F32)
                    hbuf[c, 1] = both.astype(BF16)

                @pl.when(jnp.logical_and(me != 0, me != o))
                def _():
                    got_rest(c).wait_recv()

                cols = lanes_of(c)
                conv = hbuf[c, 0].astype(F32)
                mixed = sbuf[c, 0].astype(F32)
                oq_ref[:, cols] = (
                    go_ref[:, cols].astype(F32) * (conv + skip_ref[:, cols] * mixed)
                ).astype(BF16)
                envelope = jnp.exp(-rate_ref[:, cols] * when)
                of_ref[:, cols] = (hbuf[c, 1].astype(F32) * envelope).astype(BF16)

                @pl.when(sec > 0)
                def _():
                    pass_copy(c).wait_send()

                @pl.when(sec < nsec - 1)
                def _():
                    pass_copy(c).wait_recv()

    @pl.loop(0, own)
    def _(k):
        for m in range(n):
            @pl.when(me != m)
            def _():
                (back_rest(k, m) if m else back_corr(k)).wait_send()

    @pl.when(me == 0)
    def _():
        for i in range(rin):
            forward_in(i).wait_send()

        @pl.loop(0, rout)
        def _(k):
            forward_out(k).wait_send()


def quad_call(nsec, shapes, chunk, args, decay_rate, skip_gain):
    rows, channels = shapes[0].shape
    chunks = channels // chunk
    counts, _, rin, rout = split(chunks)
    most = max(counts)
    tables = (*make_tables(4, rows), *make_local_tables(rows))
    tables = tuple(jnp.asarray(table, BF16) for table in tables)
    dma = pltpu.SemaphoreType.DMA
    block = pltpu.VMEM((rows, channels), BF16)
    row = pltpu.VMEM((1, channels), F32)
    stat = pltpu.VMEM((2, channels), F32)
    return pl.pallas_call(
        functools.partial(quad_kernel, nsec, chunk),
        out_shape=tuple(pltpu.VMEM(shape.shape, shape.dtype) for shape in shapes),
        in_specs=[pl.BlockSpec(memory_space=pl.ANY)] * 11,
        out_specs=(pl.BlockSpec(memory_space=pltpu.VMEM),) * 6,
        scratch_shapes=[
            *([block] * 5), row, row, *(pltpu.VMEM(table.shape, BF16) for table in tables),
            dma((5, 2, 4)), dma((6,)),
            pltpu.VMEM((chunks, 3, rows, chunk), BF16),
            pltpu.VMEM((most, 4, 3, rows, chunk), BF16),
            pltpu.VMEM((most, 4, 3, rows, chunk), BF16),
            pltpu.VMEM((chunks, 3, rows, chunk), BF16),
            pltpu.VMEM((chunks, rows, chunk), BF16),
            pltpu.VMEM((chunks, 2, rows, chunk), BF16),
            pltpu.VMEM((max(rin, 1), 3, rows, chunk), BF16),
            pltpu.VMEM((rout, 2, rows, chunk), BF16),
            pltpu.VMEM((4, 2 * rows, 3 * chunk), BF16),
            pltpu.VMEM((4, 2 * rows, 3 * chunk), F32),
            stat, stat, stat, stat,
            dma((chunks,)), dma((most, 4)), dma((max(rin, 1),)), dma((max(rin, 1),)),
            dma((most, 4, 2)), dma((chunks, 2)), dma((rout,)), dma((rout,)),
            dma((chunks,)), dma((chunks,)), dma((2, 4)), dma((2, 4)),
        ],
        compiler_params=pltpu.CompilerParams(
            collective_id=0, has_side_effects=True, vmem_limit_bytes=58 * 1024 * 1024
        ),
        name="hyena_backward_quad",
    )(*args, decay_rate, skip_gain, *tables)


def finish(*refs):
    count = (len(refs) - 1) // 2
    sem = refs[-1]
    copies = [
        pltpu.make_async_copy(refs[g], refs[count + g], sem.at[g]) for g in range(count)
    ]
    for copy in copies:
        copy.start()
    for copy in copies:
        copy.wait()


def general_call(n, nsec, shapes, chunk, args, decay_rate, skip_gain):
    rows, channels = shapes[0].shape
    width = channels // n
    steps = width // chunk
    fwd, inv = make_tables(n, rows)
    fwd, inv = jnp.asarray(fwd, BF16), jnp.asarray(inv, BF16)
    message = (steps, n, rows, 3 * chunk)
    dma = pltpu.SemaphoreType.DMA
    anywhere = pl.BlockSpec(memory_space=pl.ANY)
    inside = pl.BlockSpec(memory_space=pltpu.VMEM)
    return pl.pallas_call(
        functools.partial(kernel, n, nsec, chunk, steps),
        out_shape=tuple(pltpu.VMEM(shape.shape, shape.dtype) for shape in shapes),
        in_specs=[anywhere] * 9,
        out_specs=(inside,) * 6,
        scratch_shapes=[
            *([pltpu.VMEM((rows, channels), BF16)] * 5),
            *([pltpu.VMEM((1, channels), F32)] * 2),
            *([pltpu.VMEM(fwd.shape, BF16)] * 2),
            dma((5, 2, n)), dma((4,)),
            pltpu.VMEM(message, BF16),
            pltpu.VMEM(message, BF16),
            pltpu.VMEM(message, BF16),
            pltpu.VMEM(message, BF16),
            pltpu.VMEM((steps, n, rows, chunk), BF16),
            pltpu.VMEM((n, 2 * rows, 3 * chunk), BF16),
            pltpu.VMEM((n, 2 * rows, 3 * chunk), F32),
            pltpu.VMEM((2, width), F32),
            pltpu.VMEM((n, 2, width), F32),
            dma((steps, n)), dma((steps, n)), dma((steps, n)), dma((steps, n)),
            dma((steps, n)), dma((steps, n)), dma((n,)), dma((n,)),
        ],
        compiler_params=pltpu.CompilerParams(
            collective_id=0, has_side_effects=True, vmem_limit_bytes=58 * 1024 * 1024
        ),
        name="hyena_backward",
    )(
        *args, decay_rate, skip_gain, fwd, inv,
    )


def shards(n, nsec, gate_q, gate_k, value_in, filter_raw, decay_rate, skip_gain, grad_out):
    rows, channels = gate_q.shape[1:]
    block = jax.ShapeDtypeStruct((rows, channels), BF16)
    row = jax.ShapeDtypeStruct((1, channels), F32)
    dma = pltpu.SemaphoreType.DMA
    anywhere = pl.BlockSpec(memory_space=pl.ANY)
    inside = pl.BlockSpec(memory_space=pltpu.VMEM)
    shapes = (block, block, block, block, row, row)
    args = (gate_q[0], gate_k[0], value_in[0], filter_raw[0], grad_out[0])
    call = quad_call if n == 4 and channels >= 16 * 128 else functools.partial(general_call, n)
    outs = call(nsec, shapes, 128, args, decay_rate, skip_gain)
    oq, ok, op, of, orate, oskip = pl.pallas_call(
        finish,
        out_shape=shapes,
        in_specs=[inside] * 6,
        out_specs=(anywhere,) * 6,
        scratch_shapes=[dma((6,))],
        compiler_params=pltpu.CompilerParams(vmem_limit_bytes=4 * 1024 * 1024),
        name="hand_over",
    )(*(pltpu.with_memory_space_constraint(out, pltpu.VMEM) for out in outs))
    return oq[None], ok[None], op[None], of[None], orate, oskip


def solution(mesh):
    n, nsec = mesh.shape["ctx"], mesh.shape["section"]
    tokens = P("section", "ctx", None)
    return jax.shard_map(
        functools.partial(shards, n, nsec),
        mesh=mesh,
        in_specs=(tokens, tokens, tokens, tokens, P("section", None), P("section", None), tokens),
        out_specs=(tokens, tokens, tokens, tokens, P("section", None), P("section", None)),
        check_vma=False,
    )
```
